128 devices in a mesh: grp: 4 (over x), tile: 32 (over y, z, core).
Axes of the slice: x: 4, y: 4, z: 4, core: 2. Of those that a mesh axis runs over, the one named last changes fastest.
Arguments:
- profiles: float32 [4, 64, 262144], P(None, None, ('grp', 'tile')), may hold values from -6 to 6
- heat_coupling: float32 [64, 262144], P(None, ('grp', 'tile')), may hold values from 0.1 to 10
- momentum_coupling: float32 [64, 262144], P(None, ('grp', 'tile')), may hold values from 0.1 to 10
- layer_mass: float32 [64, 262144], P(None, ('grp', 'tile')), may hold values from 0.3 to 3
- soil_temps: float32 [8, 1572864], P(None, ('grp', 'tile')), may hold values from -6 to 6
- heat_capacity: float32 [8, 1572864], P(None, ('grp', 'tile')), may hold values from 0.5 to 5
- conductance: float32 [8, 1572864], P(None, ('grp', 'tile')), may hold values from 0.2 to 5
- exchange_coeffs: float32 [3, 1572864], P(None, ('grp', 'tile')), may hold values from 0.2 to 5
- wetness: float32 [1572864], P(('grp', 'tile')), may hold values from -1 to 1
- area_table: float32 [256], replicated, may hold values from 0.05 to 1
- entry_column: int32 [1572864], P(('grp', 'tile')), may hold values from 0 to 2047, as said below
- entry_owner: int32 [1572864], P(('grp', 'tile')), may hold values from 0 to 127, as said below
- entry_cell: int32 [1572864], P(('grp', 'tile')), may hold values from 0 to 12287, as said below
- entry_area: int32 [1572864], P(('grp', 'tile')), may hold values from 0 to 255
- surface_type: int32 [1572864], P(('grp', 'tile')), may hold values from 0 to 3
- layer_counts: int32 [4], replicated, may hold values from 1 to 8
Outputs:
- new_profiles: float32 [4, 64, 262144], P(None, None, ('grp', 'tile'))
- new_soil: float32 [8, 1572864], P(None, ('grp', 'tile'))
The draws below stay inside these ranges and needn't reach their ends.
Inputs may be any that keep to these rules, and one draw needn't show every extreme that they name: `entry_column`: every column of a device is named by at least one of that device's entries. `entry_owner`: A device's entries name any one owner at most 192 times, and every device names some owner exactly 192 times; every owner is named by exactly 12288 entries over all devices. `entry_cell`: over all devices, the entries that name one owner carry each cell id of that owner exactly once.
All inputs are finite; a program needn't handle non-finite values.
Results may differ from the reference program's by a relative error of at most 0.00005.
Values sent between devices are 32-bit elements; how exact they have to be, the bound alone decides.
A program may use at most 128 MiB of HBM per device.

```python
import math
import jax
import jax.numpy as jnp
from jax import lax

LEV = 64
COLS_DEV = 2048
LMAX = 8
NTYPES = 4
NAREA = 256
CELLS_DEV = 12288
COLUMNS = 262144
CELLS = 1572864
DEVICES = 128


def intersection_layout(key):
    device_count = DEVICES
    average = CELLS_DEV // device_count
    subkeys = jax.random.split(jax.random.fold_in(key, 11), 5)
    excess = jax.random.randint(subkeys[0], (device_count // 2,), 0, average + 1)
    excess = excess.at[0].set(average)
    weights = jnp.stack([average + excess, average - excess], axis=1).reshape(device_count)
    shifts = jax.random.permutation(subkeys[1], device_count)
    ranking = jax.random.permutation(subkeys[2], device_count)
    inverse = jnp.argsort(ranking)
    bounds = jnp.cumsum(weights)
    entry_pos = jnp.arange(CELLS_DEV, dtype=jnp.int32)
    block_of = jnp.searchsorted(bounds, entry_pos, side='right')
    owners = inverse[(ranking[:, None] + shifts[block_of][None, :]) % device_count]
    cell_perm = jax.vmap(lambda subkey: jax.random.permutation(subkey, CELLS_DEV))(jax.random.split(subkeys[3], device_count))
    cell_ids = cell_perm[owners, jnp.broadcast_to(entry_pos[None, :], owners.shape)]
    shuffle = jax.vmap(lambda subkey: jax.random.permutation(subkey, CELLS_DEV))(jax.random.split(subkeys[4], device_count))
    owners = jnp.take_along_axis(owners, shuffle, axis=1)
    cell_ids = jnp.take_along_axis(cell_ids, shuffle, axis=1)
    return (owners.reshape(-1).astype(jnp.int32), cell_ids.reshape(-1).astype(jnp.int32))


def draw_entry_owner(key, part):
    return intersection_layout(key)[0]


def draw_entry_cell(key, part):
    return intersection_layout(key)[1]


def draw_entry_column(key, part):
    subkeys = jax.random.split(jax.random.fold_in(key, 23), 3)
    firsts = jax.vmap(lambda subkey: jax.random.permutation(subkey, COLS_DEV))(jax.random.split(subkeys[0], DEVICES))
    extras = jax.random.randint(subkeys[1], (DEVICES, CELLS_DEV - COLS_DEV), 0, COLS_DEV)
    joined = jnp.concatenate([firsts, extras], axis=1)
    shuffle = jax.vmap(lambda subkey: jax.random.permutation(subkey, CELLS_DEV))(jax.random.split(subkeys[2], DEVICES))
    return jnp.take_along_axis(joined, shuffle, axis=1).reshape(-1).astype(jnp.int32)


def draw_layer_counts(key, part):
    subkeys = jax.random.split(jax.random.fold_in(key, 37), 2)
    totals = jax.random.randint(subkeys[0], (NTYPES,), 1, LMAX + 1)
    ordering = jax.random.permutation(subkeys[1], NTYPES)
    totals = totals.at[ordering[0]].set(LMAX)
    totals = totals.at[ordering[1]].set(1)
    return totals.astype(jnp.int32)


def set_ends(entries, own_key, low, top_value):
    longest = entries.shape.index(max(entries.shape))
    spots = []
    for shift in (0, 1):
        where = [jax.random.randint(jax.random.fold_in(own_key, axis), (), 0, length) for axis, length in enumerate(entries.shape)]
        where[longest] = (where[longest] + shift) % entries.shape[longest]
        spots.append(tuple(where))
    return entries.at[spots[0]].set(low).at[spots[1]].set(top_value)


def level_of(own_key, dims, cuts, least, largest):
    factor_of = 1.0
    for position, shards_of in cuts:
        steps = jax.random.uniform(jax.random.fold_in(jax.random.fold_in(own_key, 6), position), (shards_of,), jnp.float32, least / len(cuts), largest / len(cuts))
        factor_of = factor_of * jnp.repeat(jnp.exp(steps), dims[position] // shards_of).reshape((-1,) + (1,) * (len(dims) - 1 - position))
    return factor_of


def gaussian(stream_key, extent, width, limit, shards=(), held_as=jnp.bfloat16):
    gain = level_of(stream_key, extent, shards, -0.22, 0.18) if shards else 1.0
    array = jax.random.normal(stream_key, extent, jnp.float32) * width * gain
    return jnp.minimum(jnp.maximum(array, -limit), limit).astype(held_as)


def setup_inputs(seed: int = 0) -> dict:
    key_of = jax.random.split(jax.random.key(seed), 17)
    return {
        "profiles": gaussian(key_of[0], (4, LEV, COLUMNS), 1.0, 6.0, ((2, 128),), jnp.float32),
        "heat_coupling": jnp.clip(jnp.exp(math.log(10.0) - 4.6051702 * jax.random.uniform(key_of[1], (LEV, COLUMNS), jnp.float32) ** level_of(key_of[1], (LEV, COLUMNS), ((1, 128),), -0.2, 0.2)), 0.1, 10.0),
        "momentum_coupling": jnp.clip(jnp.exp(math.log(10.0) - 4.6051702 * jax.random.uniform(key_of[2], (LEV, COLUMNS), jnp.float32) ** level_of(key_of[2], (LEV, COLUMNS), ((1, 128),), -0.2, 0.2)), 0.1, 10.0),
        "layer_mass": jnp.clip(jnp.exp(math.log(3.0) - 2.3025851 * jax.random.uniform(key_of[3], (LEV, COLUMNS), jnp.float32) ** level_of(key_of[3], (LEV, COLUMNS), ((1, 128),), -0.2, 0.2)), 0.3, 3.0),
        "soil_temps": gaussian(key_of[4], (LMAX, CELLS), 1.0, 6.0, ((1, 128),), jnp.float32),
        "heat_capacity": jnp.clip(jnp.exp(math.log(5.0) - 2.3025851 * jax.random.uniform(key_of[5], (LMAX, CELLS), jnp.float32) ** level_of(key_of[5], (LMAX, CELLS), ((1, 128),), -0.2, 0.2)), 0.5, 5.0),
        "conductance": jnp.clip(jnp.exp(math.log(5.0) - 3.218876 * jax.random.uniform(key_of[6], (LMAX, CELLS), jnp.float32) ** level_of(key_of[6], (LMAX, CELLS), ((1, 128),), -0.2, 0.2)), 0.2, 5.0),
        "exchange_coeffs": jnp.clip(jnp.exp(math.log(5.0) - 3.218876 * jax.random.uniform(key_of[7], (3, CELLS), jnp.float32) ** level_of(key_of[7], (3, CELLS), ((1, 128),), -0.2, 0.2)), 0.2, 5.0),
        "wetness": jnp.clip(jax.random.uniform(key_of[8], (CELLS,), jnp.float32, -1.0, 1.0) * level_of(key_of[8], (CELLS,), ((0, 128),), -0.4, 0.0), -1.0, 1.0),
        "area_table": jnp.clip(jnp.exp(jax.random.uniform(key_of[9], (NAREA,), jnp.float32, math.log(0.05), math.log(1.0))), 0.05, 1.0),
        "entry_column": draw_entry_column(jax.random.fold_in(key_of[16], 71), 0),
        "entry_owner": draw_entry_owner(jax.random.fold_in(key_of[16], 71), 0),
        "entry_cell": draw_entry_cell(jax.random.fold_in(key_of[16], 71), 0),
        "entry_area": set_ends(jax.random.randint(key_of[13], (CELLS,), 0, NAREA), jax.random.fold_in(key_of[13], 1), 0, NAREA - 1).astype(jnp.int32),
        "surface_type": set_ends(jax.random.randint(key_of[14], (CELLS,), 0, NTYPES), jax.random.fold_in(key_of[14], 1), 0, NTYPES - 1).astype(jnp.int32),
        "layer_counts": draw_layer_counts(jax.random.fold_in(key_of[16], 71), 0),
    }


def down_sweep(fields, coupling, layer_mass):
    interface = coupling.at[0].set(0.0)
    below_link = jnp.concatenate([interface[1:], jnp.zeros_like(interface[:1])], axis=0)
    diagonal = layer_mass + coupling + below_link
    values = jnp.swapaxes(fields, 0, 1)

    def advance(state_prev, layer_in):
        factor_prev, reduced_prev = state_prev
        next_link, link_here, diag_row, mass_row, value_row = layer_in
        divisor = diag_row + link_here * factor_prev
        factor = -next_link / divisor
        reduced = (mass_row * value_row + link_here * reduced_prev) / divisor
        return (factor, reduced), (factor, reduced, divisor)

    initial = (jnp.zeros_like(coupling[0]), jnp.zeros_like(values[0]))
    _, (factor, reduced, divisor) = lax.scan(advance, initial, (below_link, interface, diagonal, layer_mass, values))
    return factor, reduced, 1.0 / divisor[-1]


def up_sweep(factor, reduced, bottom):
    def retreat(value_next, layer_in):
        factor_row, reduced_row = layer_in
        value_row = reduced_row - factor_row * value_next
        return value_row, value_row

    _, upper_rows = lax.scan(retreat, bottom, (factor[:-1], reduced[:-1]), reverse=True)
    stacked = jnp.concatenate([upper_rows, bottom[None]], axis=0)
    return jnp.swapaxes(stacked, 0, 1)


def surface_heat(heat_rows, exchange_coeffs, wetness, soil_temps, heat_capacity, conductance, layer_total):
    bottom_t = heat_rows[0]
    bottom_q = heat_rows[1]
    heat_scale = heat_rows[2]
    gain_t = exchange_coeffs[0] / (1.0 + exchange_coeffs[0] * heat_scale)
    gain_q = exchange_coeffs[1] / (1.0 + exchange_coeffs[1] * heat_scale)
    layers = soil_temps.shape[0]
    factors = []
    reduceds = []
    link_prev = jnp.zeros_like(gain_t)
    factor_prev = jnp.zeros_like(gain_t)
    reduced_prev = jnp.zeros_like(gain_t)
    for stratum in range(layers):
        link_here = jnp.where(layer_total > stratum + 1, conductance[stratum], 0.0)
        deep_link = jnp.where(layer_total == stratum + 1, conductance[stratum], 0.0)
        diag_row = heat_capacity[stratum] + link_here + link_prev + deep_link
        rhs_row = heat_capacity[stratum] * soil_temps[stratum]
        if stratum == 0:
            diag_row = diag_row + gain_t
            rhs_row = rhs_row + gain_t * bottom_t
        divisor = diag_row + link_prev * factor_prev
        factor_prev = -link_here / divisor
        reduced_prev = (rhs_row + link_prev * reduced_prev) / divisor
        factors.append(factor_prev)
        reduceds.append(reduced_prev)
        link_prev = link_here
    value_next = reduceds[layers - 1]
    new_rows = [value_next]
    for stratum in range(layers - 2, -1, -1):
        value_next = reduceds[stratum] - factors[stratum] * value_next
        new_rows.insert(0, value_next)
    new_soil = jnp.stack(new_rows, axis=0)
    surface = new_soil[0]
    flux = jnp.stack([gain_t * (surface - bottom_t), gain_q * (wetness + 0.5 * surface - bottom_q)], axis=0)
    return new_soil, flux


def surface_wind(wind_rows, drag_coeff):
    denominator = 1.0 + drag_coeff * wind_rows[2]
    return jnp.stack([-drag_coeff * wind_rows[0] / denominator, -drag_coeff * wind_rows[1] / denominator], axis=0)


def reference(profiles, heat_coupling, momentum_coupling, layer_mass, soil_temps, heat_capacity, conductance, exchange_coeffs, wetness, area_table, entry_column, entry_owner, entry_cell, entry_area, surface_type, layer_counts):
    heat_factor, heat_reduced, heat_scale = down_sweep(profiles[0:2], heat_coupling, layer_mass)
    wind_factor, wind_reduced, wind_scale = down_sweep(profiles[2:4], momentum_coupling, layer_mass)
    heat_rows = jnp.concatenate([heat_reduced[-1], heat_scale[None]], axis=0)
    wind_rows = jnp.concatenate([wind_reduced[-1], wind_scale[None]], axis=0)
    source = (jnp.arange(CELLS, dtype=jnp.int32) // CELLS_DEV).astype(jnp.int32)
    column_of = (source * COLS_DEV + entry_column).astype(jnp.int32)
    cell_of = (entry_owner * CELLS_DEV + entry_cell).astype(jnp.int32)
    heat_cells = jnp.zeros((3, CELLS), jnp.float32).at[:, cell_of].set(heat_rows[:, column_of])
    wind_cells = jnp.zeros((3, CELLS), jnp.float32).at[:, cell_of].set(wind_rows[:, column_of])
    layer_total = layer_counts[surface_type]
    new_soil, heat_flux = surface_heat(heat_cells, exchange_coeffs, wetness, soil_temps, heat_capacity, conductance, layer_total)
    wind_flux = surface_wind(wind_cells, exchange_coeffs[2])
    flux_cells = jnp.concatenate([heat_flux, wind_flux], axis=0)
    flux_entry = flux_cells[:, cell_of]
    weights = area_table[entry_area]
    column_sums = jnp.zeros((5, COLUMNS), jnp.float32).at[:, column_of].add(
        jnp.concatenate([flux_entry * weights[None], weights[None]], axis=0))
    column_flux = column_sums[0:4] / column_sums[4]
    heat_new = up_sweep(heat_factor, heat_reduced, heat_reduced[-1] + heat_scale[None] * column_flux[0:2])
    wind_new = up_sweep(wind_factor, wind_reduced, wind_reduced[-1] + wind_scale[None] * column_flux[2:4])
    return jnp.concatenate([heat_new, wind_new], axis=0), new_soil
```

```python
import jax
import jax.numpy as jnp
from jax import lax
from jax.experimental import pallas as pl
from jax.experimental.pallas import tpu as pltpu
from jax.sharding import PartitionSpec as P

PEERS = 128
LANES = 128
SLOT_ROWS = 192
MSG_ROWS = 8
BF16 = jnp.bfloat16
F32 = jnp.float32
I32 = jnp.int32
VMEM_LIMIT = 56 * 1024 * 1024


def iota(shape, dim):
    return lax.broadcasted_iota(I32, shape, dim)


def split3(x):
    high = x.astype(BF16).astype(F32)
    rest = x - high
    mid = rest.astype(BF16).astype(F32)
    return high, mid, rest - mid


def lane_gather(table, index):
    return jnp.take_along_axis(table, index, axis=1, mode="promise_in_bounds")


def dot_nt(a, b):
    return lax.dot_general(a, b, (((1,), (1,)), ((), ())), preferred_element_type=F32)


def low_half(shape):
    return iota(shape, 1) < 64


def pack_message(fields, message_ref):
    count = len(fields)
    for f, field_ref in enumerate(fields):
        for g in range(16):
            message_ref[pl.ds(64 * g + f, 8, stride=8), :] = field_ref[8 * g : 8 * g + 8, :]
    for pair in range((count + 1) // 2):
        row = count + pair
        for g in range(8):
            rows = slice(128 + 8 * g, 136 + 8 * g)
            first = fields[2 * pair][rows, :]
            if 2 * pair + 1 < count:
                second = fields[2 * pair + 1][rows, :]
            else:
                second = jnp.zeros_like(first)
            low = low_half(first.shape)
            near = jnp.where(low, first, pltpu.roll(second, 64, 1))
            far = jnp.where(low, pltpu.roll(first, 64, 1), second)
            message_ref[pl.ds(64 * g + row, 8, stride=8), :] = near
            message_ref[pl.ds(64 * (g + 8) + row, 8, stride=8), :] = far


def unpack_message(message_ref, fields):
    count = len(fields)
    for f, field_ref in enumerate(fields):
        for g in range(16):
            field_ref[8 * g : 8 * g + 8, :] = message_ref[pl.ds(64 * g + f, 8, stride=8), :]
    for pair in range((count + 1) // 2):
        row = count + pair
        for g in range(8):
            rows = slice(128 + 8 * g, 136 + 8 * g)
            near = message_ref[pl.ds(64 * g + row, 8, stride=8), :]
            far = message_ref[pl.ds(64 * (g + 8) + row, 8, stride=8), :]
            low = low_half(near.shape)
            fields[2 * pair][rows, :] = jnp.where(low, near, pltpu.roll(far, 64, 1))
            if 2 * pair + 1 < count:
                fields[2 * pair + 1][rows, :] = jnp.where(low, pltpu.roll(near, 64, 1), far)


def assign_slots(owner_ref, pieces_refs, onehot_scr, rank_scr, left_scr, right_scr, acc_scr):
    entry_rows = owner_ref.shape[0]
    upper = (iota((LANES, 2 * LANES), 0) < iota((LANES, 2 * LANES), 1)).astype(F32).astype(BF16)
    owners = iota((PEERS, LANES), 0)

    def rank_body(step, base):
        for q in range(8):
            r = step * 8 + q
            hit = owners == owner_ref[pl.ds(r, 1), :]
            onehot = hit.astype(F32).astype(BF16)
            onehot_scr[:, pl.ds(pl.multiple_of(r * LANES, LANES), LANES)] = onehot
            before = jnp.dot(onehot, upper, preferred_element_type=F32)
            rank_scr[pl.ds(r, 1), :] = jnp.sum(
                jnp.where(hit, before[:, :LANES] + base, 0.0), axis=0, keepdims=True
            )
            base = base + before[:, LANES:]
        return base

    lax.fori_loop(0, entry_rows // 8, rank_body, jnp.zeros((PEERS, LANES), F32))
    acc_scr[...] = jnp.zeros_like(acc_scr)
    ranks = iota((2 * LANES, LANES), 0).astype(F32)

    def scatter_body(step, carry):
        for q in range(8):
            r = step * 8 + q
            onehot = onehot_scr[:, pl.ds(pl.multiple_of(r * LANES, LANES), LANES)]
            for p, piece_ref in enumerate(pieces_refs):
                piece = jnp.broadcast_to(piece_ref[pl.ds(r, 1), :], (PEERS, LANES)).astype(BF16)
                left_scr[p * PEERS : (p + 1) * PEERS, q * LANES : (q + 1) * LANES] = onehot * piece
            right_scr[:, q * LANES : (q + 1) * LANES] = (
                (ranks == rank_scr[pl.ds(r, 1), :]).astype(F32).astype(BF16)
            )
        acc_scr[...] += dot_nt(left_scr[...], right_scr[...])
        return carry

    lax.fori_loop(0, entry_rows // 8, scatter_body, 0)


def slots_of(acc, piece):
    base = piece * PEERS
    for g in range(16):
        yield acc[base + 8 * g : base + 8 * g + 8, 0:LANES]
    for g in range(8):
        near = acc[base + 8 * g : base + 8 * g + 8, LANES : 2 * LANES]
        far = acc[base + 64 + 8 * g : base + 64 + 8 * g + 8, LANES : 2 * LANES]
        yield jnp.where(low_half(near.shape), near, pltpu.roll(far, 64, 1))


def down_sweep(profiles_ref, heat_ref, momentum_ref, mass_ref, factor_ref, reduced_ref, bottom_scr):
    couplings = (heat_ref, momentum_ref)
    zero = jnp.zeros((8, LANES), F32)

    def rows_of(g, i, half):
        return pl.ds(g * 128 + half * 64 + i, 8, stride=8)

    def body(g, carry):
        link, factor, reduced, inverse = carry
        link, factor, reduced, inverse = list(link), list(factor), list(reduced), list(inverse)
        following = jnp.minimum(g + 1, 7)
        keep = (g < 7).astype(F32)
        for i in range(8):
            for half in range(2):
                mass = mass_ref[rows_of(g, i, half), :]
                out_rows = pl.ds(pl.multiple_of(g * 128 + i * 16 + half * 8, 8), 8)
                for pair in range(2):
                    k = 2 * pair + half
                    if i < 7:
                        below = couplings[pair][rows_of(g, i + 1, half), :]
                    else:
                        below = couplings[pair][rows_of(following, 0, half), :] * keep
                    here = link[k]
                    divisor = mass + here + below + here * factor[k]
                    inverse[k] = 1.0 / divisor
                    factor[k] = -below * inverse[k]
                    factor_ref[pair, out_rows, :] = factor[k]
                    for member in range(2):
                        field = 2 * pair + member
                        m = 2 * field + half
                        value = profiles_ref[field, rows_of(g, i, half), :]
                        reduced[m] = (mass * value + here * reduced[m]) * inverse[k]
                        reduced_ref[field, out_rows, :] = reduced[m]
                    link[k] = below
        return tuple(link), tuple(factor), tuple(reduced), tuple(inverse)

    first = tuple(couplings[k // 2][rows_of(0, 0, k % 2), :] for k in range(4))
    _, _, reduced, inverse = lax.fori_loop(
        0, 8, body, (first, (zero,) * 4, (zero,) * 8, (zero,) * 4)
    )
    for half in range(2):
        rows = slice(8 * half, 8 * half + 8)
        for field in range(4):
            bottom_scr[field, rows, :] = reduced[2 * field + half]
        bottom_scr[4, rows, :] = inverse[half]
        bottom_scr[5, rows, :] = inverse[2 + half]


def source_kernel(
    owner_ref, cell_ref, column_ref, area_ref, table_ref, profiles_ref, heat_ref, momentum_ref, mass_ref,
    message_ref, column_slot_ref, weight_slot_ref, wind_slot_ref, factor_ref, reduced_ref, bottom_ref,
    piece_scr, onehot_scr, rank_scr, left_scr, right_scr, acc_scr, field_scr,
):
    down_sweep(profiles_ref, heat_ref, momentum_ref, mass_ref, factor_ref, reduced_ref, bottom_ref)
    cell = cell_ref[...]
    column = column_ref[...]
    piece_scr[0] = ((cell >> 8) + 1).astype(F32)
    piece_scr[1] = (cell & 255).astype(F32)
    piece_scr[2] = (column >> 7).astype(F32)
    piece_scr[3] = (column & 127).astype(F32)
    piece_scr[4] = area_ref[...].astype(F32)
    assign_slots(
        owner_ref, [piece_scr.at[p] for p in range(5)],
        onehot_scr, rank_scr, left_scr, right_scr, acc_scr,
    )
    for g, (cell_high, cell_low, row, lane, area) in enumerate(
        zip(*[slots_of(acc_scr, p) for p in range(5)])
    ):
        rows = slice(8 * g, 8 * g + 8)
        field_scr[0, rows, :] = cell_high * 256.0 + cell_low
        row, lane, area = row.astype(I32), lane.astype(I32), area.astype(I32)
        column_slot_ref[rows, :] = row * LANES + lane
        near = lane_gather(jnp.broadcast_to(table_ref[0:1, :], (8, LANES)), area & 127)
        far = lane_gather(jnp.broadcast_to(table_ref[1:2, :], (8, LANES)), area & 127)
        weight = jnp.where(area < LANES, near, far)
        weight_slot_ref[rows, :] = jnp.where(cell_high > 0.0, weight, 0.0)

    def expand(step, carry):
        index = [column_slot_ref[pl.ds(pl.multiple_of(step * 32 + 8 * j, 8), 8), :] for j in range(4)]
        high = [x >> 7 for x in index]
        low = [x & 127 for x in index]
        totals = [[jnp.zeros((8, LANES), F32) for _ in range(4)] for _ in range(4)]
        for h in range(16):
            tables = [
                jnp.broadcast_to(bottom_ref[f, h : h + 1, :], (8, LANES)) for f in (0, 1, 4, 5)
            ]
            for j in range(4):
                hit = high[j] == h
                for f in range(4):
                    totals[j][f] = jnp.where(hit, lane_gather(tables[f], low[j]), totals[j][f])
        for j in range(4):
            rows = pl.ds(pl.multiple_of(step * 32 + 8 * j, 8), 8)
            for f in range(3):
                field_scr[f + 1, rows, :] = totals[j][f]
            wind_slot_ref[rows, :] = totals[j][3]
        return carry

    lax.fori_loop(0, 6, expand, 0)
    pack_message([field_scr.at[f] for f in range(4)], message_ref)


def soil_block(a, b, soil_ref, capacity_ref, conductance_ref, exchange_ref, wetness_ref, type_ref, counts_ref,
               cells_scr, soil_out_ref, table_scr):
    tiles = pl.ds(16 * a + b, 8, stride=2)
    here = (pl.ds(pl.multiple_of(8 * a, 8), 8), slice(LANES * b, LANES * b + LANES))
    bottom_t = cells_scr[0][here]
    bottom_q = cells_scr[1][here]
    heat_scale = cells_scr[2][here]
    kind = type_ref[tiles, :]
    total = jnp.zeros((8, LANES), I32)
    for t in range(4):
        total = jnp.where(kind == t, counts_ref[t], total)
    heat, moist, drag = (exchange_ref[i, tiles, :] for i in range(3))
    gain_t = heat / (1.0 + heat * heat_scale)
    gain_q = moist / (1.0 + moist * heat_scale)
    link_prev = factor = reduced = None
    factors, reduceds = [], []
    for layer in range(8):
        rows = pl.ds((16 * a + b) * 8 + layer, 8, stride=16)
        conductance = conductance_ref[rows, :]
        capacity = capacity_ref[rows, :]
        link = jnp.where(total > layer + 1, conductance, 0.0)
        deep = jnp.where(total == layer + 1, conductance, 0.0)
        diagonal = capacity + link + deep
        rhs = capacity * soil_ref[rows, :]
        if layer == 0:
            divisor = diagonal + gain_t
            rhs = rhs + gain_t * bottom_t
        else:
            divisor = diagonal + link_prev + link_prev * factor
            rhs = rhs + link_prev * reduced
        inverse = 1.0 / divisor
        factor = -link * inverse
        reduced = rhs * inverse
        factors.append(factor)
        reduceds.append(reduced)
        link_prev = link
    value = None
    for layer in range(7, -1, -1):
        rows = pl.ds((16 * a + b) * 8 + layer, 8, stride=16)
        value = reduceds[layer] if layer == 7 else reduceds[layer] - factors[layer] * value
        kept = value if layer == 0 else jnp.where(total > layer, value, soil_ref[rows, :])
        soil_out_ref[rows, :] = kept
    table_scr[0, tiles, :] = gain_t * (value - bottom_t)
    table_scr[1, tiles, :] = gain_q * (wetness_ref[tiles, :] + 0.5 * value - bottom_q)
    table_scr[2, tiles, :] = drag


def owner_kernel(
    counts_ref, message_ref, soil_ref, capacity_ref, conductance_ref, exchange_ref, wetness_ref, type_ref,
    reply_ref, soil_out_ref,
    field_scr, piece_scr, left_scr, right_scr, acc_scr, cells_scr, table_scr, index_scr,
):
    unpack_message(message_ref, [field_scr.at[f] for f in range(4)])
    index_scr[...] = field_scr[0].astype(I32) - 256
    for f in range(3):
        for p, piece in enumerate(split3(field_scr[f + 1])):
            piece_scr[3 * f + p] = piece
    acc_scr[...] = jnp.zeros_like(acc_scr)
    highs = iota((48, LANES), 0)
    lows = iota((256, LANES), 0)

    def scatter_body(step, carry):
        for q in range(8):
            r = step * 8 + q
            cell = index_scr[pl.ds(r, 1), :]
            lanes = slice(q * LANES, (q + 1) * LANES)
            right_scr[:, lanes] = (lows == (cell & 255)).astype(F32).astype(BF16)
            onehot = (highs == (cell >> 8)).astype(F32).astype(BF16)
            for p in range(9):
                piece = jnp.broadcast_to(piece_scr[p, pl.ds(r, 1), :], (48, LANES)).astype(BF16)
                left_scr[48 * p : 48 * p + 48, lanes] = onehot * piece
        acc_scr[...] += dot_nt(left_scr[...], right_scr[...])
        return carry

    lax.fori_loop(0, SLOT_ROWS // 8, scatter_body, 0)
    for f in range(3):
        base = 144 * f
        cells_scr[f] = (
            acc_scr[base : base + 48] + acc_scr[base + 48 : base + 96] + acc_scr[base + 96 : base + 144]
        )

    def soil_body(a, carry):
        for b in range(2):
            soil_block(
                a, b, soil_ref, capacity_ref, conductance_ref, exchange_ref, wetness_ref, type_ref,
                counts_ref, [cells_scr.at[f] for f in range(3)], soil_out_ref, table_scr,
            )
        return carry

    lax.fori_loop(0, 6, soil_body, 0)

    def gather_step(step, carry):
        index = [index_scr[pl.ds(pl.multiple_of(step * 48 + 8 * j, 8), 8), :] for j in range(6)]
        high = [x >> 7 for x in index]
        low = [x & 127 for x in index]

        def row_body(four, totals):
            totals = [list(x) for x in totals]
            for u in range(4):
                h = four * 4 + u
                tables = [
                    jnp.broadcast_to(table_scr[f, pl.ds(h, 1), :], (8, LANES)) for f in range(3)
                ]
                for j in range(6):
                    hit = high[j] == h
                    for f in range(3):
                        totals[j][f] = jnp.where(hit, lane_gather(tables[f], low[j]), totals[j][f])
            return tuple(tuple(x) for x in totals)

        zero = jnp.zeros((8, LANES), F32)
        totals = lax.fori_loop(0, 24, row_body, ((zero,) * 3,) * 6)
        for j in range(6):
            rows = pl.ds(pl.multiple_of(step * 48 + 8 * j, 8), 8)
            for f in range(3):
                field_scr[f, rows, :] = totals[j][f]
        return carry

    lax.fori_loop(0, 4, gather_step, 0)
    pack_message([field_scr.at[f] for f in range(3)], reply_ref)


def column_kernel(
    reply_ref, column_slot_ref, weight_slot_ref, wind_slot_ref, factor_ref, reduced_ref, bottom_ref,
    out_ref,
    field_scr, piece_scr, left_scr, right_scr, acc_scr,
):
    unpack_message(reply_ref, [field_scr.at[f] for f in range(3)])
    weight = weight_slot_ref[...]
    drag = field_scr[2]
    values = (
        weight * field_scr[0],
        weight * field_scr[1],
        weight * (drag / (1.0 + drag * wind_slot_ref[...])),
        weight,
    )
    for f in range(4):
        for p, piece in enumerate(split3(values[f])):
            piece_scr[3 * f + p] = piece
    acc_scr[...] = jnp.zeros_like(acc_scr)
    highs = iota((16, LANES), 0)
    lows = iota((LANES, LANES), 0)

    def scatter_body(step, carry):
        for q in range(8):
            r = step * 8 + q
            column = column_slot_ref[pl.ds(r, 1), :]
            lanes = slice(q * LANES, (q + 1) * LANES)
            right_scr[:, lanes] = (lows == (column & 127)).astype(F32).astype(BF16)
            onehot = (highs == (column >> 7)).astype(F32).astype(BF16)
            for p in range(12):
                piece = jnp.broadcast_to(piece_scr[p, pl.ds(r, 1), :], (16, LANES)).astype(BF16)
                left_scr[16 * p : 16 * p + 16, lanes] = onehot * piece
        acc_scr[...] += dot_nt(left_scr[...], right_scr[...])
        return carry

    lax.fori_loop(0, SLOT_ROWS // 8, scatter_body, 0)
    sums = []
    for f in range(4):
        base = 48 * f
        sums.append(acc_scr[base : base + 16] + acc_scr[base + 16 : base + 32] + acc_scr[base + 32 : base + 48])
    flux = (
        sums[0] / sums[3],
        sums[1] / sums[3],
        -bottom_ref[2] * (sums[2] / sums[3]),
        -bottom_ref[3] * (sums[2] / sums[3]),
    )
    values = []
    for field in range(4):
        lowest = bottom_ref[field] + bottom_ref[4 + field // 2] * flux[field]
        for half in range(2):
            value = lowest[8 * half : 8 * half + 8]
            out_ref[field, pl.ds(7 * 128 + half * 64 + 7, 8, stride=8), :] = value
            values.append(value)

    def retreat(values, g, i):
        values = list(values)
        for half in range(2):
            rows = pl.ds(pl.multiple_of(g * 128 + i * 16 + half * 8, 8), 8)
            for field in range(4):
                k = 2 * field + half
                values[k] = reduced_ref[field, rows, :] - factor_ref[field // 2, rows, :] * values[k]
                out_ref[field, pl.ds(g * 128 + half * 64 + i, 8, stride=8), :] = values[k]
        return tuple(values)

    values = tuple(values)
    for i in range(6, -1, -1):
        values = retreat(values, 7, i)

    def body(step, values):
        for i in range(7, -1, -1):
            values = retreat(values, 6 - step, i)
        return values

    lax.fori_loop(0, 7, body, values)


def call(kernel, out_shapes, scratch, in_specs, **params):
    return pl.pallas_call(
        kernel,
        out_shape=out_shapes,
        in_specs=in_specs,
        out_specs=[pl.BlockSpec(memory_space=pltpu.VMEM)] * len(out_shapes),
        scratch_shapes=scratch,
        compiler_params=pltpu.CompilerParams(vmem_limit_bytes=VMEM_LIMIT, **params),
    )


def tiles_of(x):
    *lead, rows, lanes = x.shape
    x = x.reshape(*lead, rows // 8, 8, lanes // LANES, LANES)
    return jnp.swapaxes(x, -3, -2).reshape(*lead, rows * lanes // LANES, LANES)


def untile(x, rows, lanes):
    *lead, _, _ = x.shape
    x = x.reshape(*lead, rows // 8, lanes // LANES, 8, LANES)
    return jnp.swapaxes(x, -3, -2).reshape(*lead, rows, lanes)


def exchange(message):
    blocks = message.reshape(PEERS, MSG_ROWS, LANES)
    return lax.all_to_all(blocks, ("grp", "tile"), split_axis=0, concat_axis=0, tiled=True).reshape(
        message.shape
    )


def local(
    profiles, heat_coupling, momentum_coupling, layer_mass, soil_temps, heat_capacity, conductance,
    exchange_coeffs, wetness, area_table, entry_column, entry_owner, entry_cell, entry_area,
    surface_type, layer_counts,
):
    shape = jax.ShapeDtypeStruct
    vmem = pl.BlockSpec(memory_space=pltpu.VMEM)
    smem = pl.BlockSpec(memory_space=pltpu.SMEM)
    flat = lambda x: x.reshape(-1, LANES)
    message, column_slot, weight_slot, wind_slot, factor, reduced, bottom = call(
        source_kernel,
        [
            shape((PEERS * MSG_ROWS, LANES), F32),
            shape((SLOT_ROWS, LANES), I32),
            shape((SLOT_ROWS, LANES), F32),
            shape((SLOT_ROWS, LANES), F32),
            shape((2, 1024, LANES), F32),
            shape((4, 1024, LANES), F32),
            shape((6, 16, LANES), F32),
        ],
        [
            pltpu.VMEM((5, 96, LANES), F32),
            pltpu.VMEM((PEERS, 96 * LANES), BF16),
            pltpu.VMEM((96, LANES), F32),
            pltpu.VMEM((5 * PEERS, 1024), BF16),
            pltpu.VMEM((256, 1024), BF16),
            pltpu.VMEM((5 * PEERS, 256), F32),
            pltpu.VMEM((4, SLOT_ROWS, LANES), F32),
        ],
        [vmem] * 9,
    )(
        flat(entry_owner), flat(entry_cell), flat(entry_column), flat(entry_area), flat(area_table),
        tiles_of(profiles), tiles_of(heat_coupling), tiles_of(momentum_coupling), tiles_of(layer_mass),
    )
    received = exchange(message)
    reply, new_soil = call(
        owner_kernel,
        [shape((PEERS * MSG_ROWS, LANES), F32), shape((768, LANES), F32)],
        [
            pltpu.VMEM((4, SLOT_ROWS, LANES), F32),
            pltpu.VMEM((9, SLOT_ROWS, LANES), F32),
            pltpu.VMEM((432, 1024), BF16),
            pltpu.VMEM((256, 1024), BF16),
            pltpu.VMEM((432, 256), F32),
            pltpu.VMEM((3, 48, 256), F32),
            pltpu.VMEM((3, 96, LANES), F32),
            pltpu.VMEM((SLOT_ROWS, LANES), I32),
        ],
        [smem] + [vmem] * 7,
    )(
        layer_counts, received, tiles_of(soil_temps), tiles_of(heat_capacity), tiles_of(conductance),
        exchange_coeffs.reshape(3, 96, LANES), flat(wetness), flat(surface_type),
    )
    returned = exchange(reply)
    (new_profiles,) = call(
        column_kernel,
        [shape((4, 1024, LANES), F32)],
        [
            pltpu.VMEM((3, SLOT_ROWS, LANES), F32),
            pltpu.VMEM((12, SLOT_ROWS, LANES), F32),
            pltpu.VMEM((192, 1024), BF16),
            pltpu.VMEM((LANES, 1024), BF16),
            pltpu.VMEM((192, LANES), F32),
        ],
        [vmem] * 7,
    )(returned, column_slot, weight_slot, wind_slot, factor, reduced, bottom)
    return untile(new_profiles, 64, 2048), untile(new_soil, 8, 12288)


def solution(mesh):
    split = ("grp", "tile")
    return jax.shard_map(
        local,
        mesh=mesh,
        in_specs=(
            P(None, None, split), P(None, split), P(None, split), P(None, split), P(None, split),
            P(None, split), P(None, split), P(None, split), P(split), P(), P(split), P(split),
            P(split), P(split), P(split), P(),
        ),
        out_specs=(P(None, None, split), P(None, split)),
        check_vma=False,
    )
```

```python
import jax
import jax.numpy as jnp
from jax import lax
from jax.experimental import pallas as pl
from jax.experimental.pallas import tpu as pltpu
from jax.sharding import PartitionSpec as P

PEERS = 128
LANES = 128
SLOT_ROWS = 192
MSG_ROWS = 8
SEND_ROWS = 6
REPLY_ROWS = 5
BF16 = jnp.bfloat16
F32 = jnp.float32
I32 = jnp.int32
VMEM_LIMIT = 56 * 1024 * 1024


def iota(shape, dim):
    return lax.broadcasted_iota(I32, shape, dim)


def split3(x):
    high = x.astype(BF16).astype(F32)
    rest = x - high
    mid = rest.astype(BF16).astype(F32)
    return high, mid, rest - mid


def lane_gather(table, index):
    return jnp.take_along_axis(table, index, axis=1, mode="promise_in_bounds")


def dot_nt(a, b):
    return lax.dot_general(a, b, (((1,), (1,)), ((), ())), preferred_element_type=F32)


def low_half(shape):
    return iota(shape, 1) < 64


def pack_message(fields, message_ref):
    count = len(fields)
    for f, field_ref in enumerate(fields):
        for g in range(16):
            message_ref[pl.ds(64 * g + f, 8, stride=8), :] = field_ref[8 * g : 8 * g + 8, :]
    for pair in range((count + 1) // 2):
        row = count + pair
        for g in range(8):
            rows = slice(128 + 8 * g, 136 + 8 * g)
            first = fields[2 * pair][rows, :]
            if 2 * pair + 1 < count:
                second = fields[2 * pair + 1][rows, :]
            else:
                second = jnp.zeros_like(first)
            low = low_half(first.shape)
            near = jnp.where(low, first, pltpu.roll(second, 64, 1))
            far = jnp.where(low, pltpu.roll(first, 64, 1), second)
            message_ref[pl.ds(64 * g + row, 8, stride=8), :] = near
            message_ref[pl.ds(64 * (g + 8) + row, 8, stride=8), :] = far


def unpack_message(message_ref, fields):
    count = len(fields)
    for f, field_ref in enumerate(fields):
        for g in range(16):
            field_ref[8 * g : 8 * g + 8, :] = message_ref[pl.ds(64 * g + f, 8, stride=8), :]
    for pair in range((count + 1) // 2):
        row = count + pair
        for g in range(8):
            rows = slice(128 + 8 * g, 136 + 8 * g)
            near = message_ref[pl.ds(64 * g + row, 8, stride=8), :]
            far = message_ref[pl.ds(64 * (g + 8) + row, 8, stride=8), :]
            low = low_half(near.shape)
            fields[2 * pair][rows, :] = jnp.where(low, near, pltpu.roll(far, 64, 1))
            if 2 * pair + 1 < count:
                fields[2 * pair + 1][rows, :] = jnp.where(low, pltpu.roll(near, 64, 1), far)


def assign_slots(owner_ref, pieces_refs, onehot_scr, rank_scr, left_scr, right_scr, acc_scr):
    entry_rows = owner_ref.shape[0]
    upper = (iota((LANES, 2 * LANES), 0) < iota((LANES, 2 * LANES), 1)).astype(F32).astype(BF16)
    owners = iota((PEERS, LANES), 0)

    def rank_body(step, base):
        for q in range(8):
            r = step * 8 + q
            hit = owners == owner_ref[pl.ds(r, 1), :]
            onehot = hit.astype(F32).astype(BF16)
            onehot_scr[:, pl.ds(pl.multiple_of(r * LANES, LANES), LANES)] = onehot
            before = jnp.dot(onehot, upper, preferred_element_type=F32)
            rank_scr[pl.ds(r, 1), :] = jnp.sum(
                jnp.where(hit, before[:, :LANES] + base, 0.0), axis=0, keepdims=True
            )
            base = base + before[:, LANES:]
        return base

    lax.fori_loop(0, entry_rows // 8, rank_body, jnp.zeros((PEERS, LANES), F32))
    acc_scr[...] = jnp.zeros_like(acc_scr)
    ranks = iota((2 * LANES, LANES), 0).astype(F32)

    def scatter_body(step, carry):
        for q in range(8):
            r = step * 8 + q
            onehot = onehot_scr[:, pl.ds(pl.multiple_of(r * LANES, LANES), LANES)]
            for p, piece_ref in enumerate(pieces_refs):
                piece = jnp.broadcast_to(piece_ref[pl.ds(r, 1), :], (PEERS, LANES)).astype(BF16)
                left_scr[p * PEERS : (p + 1) * PEERS, q * LANES : (q + 1) * LANES] = onehot * piece
            right_scr[:, q * LANES : (q + 1) * LANES] = (
                (ranks == rank_scr[pl.ds(r, 1), :]).astype(F32).astype(BF16)
            )
        acc_scr[...] += dot_nt(left_scr[...], right_scr[...])
        return carry

    lax.fori_loop(0, entry_rows // 8, scatter_body, 0)


def slots_of(acc, piece):
    base = piece * PEERS
    for g in range(16):
        yield acc[base + 8 * g : base + 8 * g + 8, 0:LANES]
    for g in range(8):
        near = acc[base + 8 * g : base + 8 * g + 8, LANES : 2 * LANES]
        far = acc[base + 64 + 8 * g : base + 64 + 8 * g + 8, LANES : 2 * LANES]
        yield jnp.where(low_half(near.shape), near, pltpu.roll(far, 64, 1))


def down_sweep(profiles_ref, heat_ref, momentum_ref, mass_ref, factor_ref, reduced_ref, bottom_scr):
    couplings = (heat_ref, momentum_ref)
    zero = jnp.zeros((8, LANES), F32)

    def rows_of(g, i, half):
        return pl.ds(g * 128 + half * 64 + i, 8, stride=8)

    def body(g, carry):
        link, factor, reduced, inverse = carry
        link, factor, reduced, inverse = list(link), list(factor), list(reduced), list(inverse)
        following = jnp.minimum(g + 1, 7)
        keep = (g < 7).astype(F32)
        for i in range(8):
            for half in range(2):
                mass = mass_ref[rows_of(g, i, half), :]
                out_rows = pl.ds(pl.multiple_of(g * 128 + i * 16 + half * 8, 8), 8)
                for pair in range(2):
                    k = 2 * pair + half
                    if i < 7:
                        below = couplings[pair][rows_of(g, i + 1, half), :]
                    else:
                        below = couplings[pair][rows_of(following, 0, half), :] * keep
                    here = link[k]
                    divisor = mass + here + below + here * factor[k]
                    inverse[k] = 1.0 / divisor
                    factor[k] = -below * inverse[k]
                    factor_ref[pair, out_rows, :] = factor[k]
                    for member in range(2):
                        field = 2 * pair + member
                        m = 2 * field + half
                        value = profiles_ref[field, rows_of(g, i, half), :]
                        reduced[m] = (mass * value + here * reduced[m]) * inverse[k]
                        reduced_ref[field, out_rows, :] = reduced[m]
                    link[k] = below
        return tuple(link), tuple(factor), tuple(reduced), tuple(inverse)

    first = tuple(couplings[k // 2][rows_of(0, 0, k % 2), :] for k in range(4))
    _, _, reduced, inverse = lax.fori_loop(
        0, 8, body, (first, (zero,) * 4, (zero,) * 8, (zero,) * 4)
    )
    for half in range(2):
        rows = slice(8 * half, 8 * half + 8)
        for field in range(4):
            bottom_scr[field, rows, :] = reduced[2 * field + half]
        bottom_scr[4, rows, :] = inverse[half]
        bottom_scr[5, rows, :] = inverse[2 + half]


def prepare_pieces(cell_ref, column_ref, area_ref, piece_scr):
    cell = cell_ref[...]
    column = column_ref[...]
    piece_scr[0] = ((cell >> 8) + 1).astype(F32)
    piece_scr[1] = (cell & 255).astype(F32)
    piece_scr[2] = (column >> 7).astype(F32)
    piece_scr[3] = (column & 127).astype(F32)
    piece_scr[4] = area_ref[...].astype(F32)


def read_slots(acc_scr, table_ref, id_ref, column_slot_ref, weight_slot_ref):
    for g, (cell_high, cell_low, row, lane, area) in enumerate(
        zip(*[slots_of(acc_scr, p) for p in range(5)])
    ):
        rows = slice(8 * g, 8 * g + 8)
        id_ref[rows, :] = cell_high * 256.0 + cell_low
        row, lane, area = row.astype(I32), lane.astype(I32), area.astype(I32)
        column_slot_ref[rows, :] = row * LANES + lane
        near = lane_gather(jnp.broadcast_to(table_ref[0:1, :], (8, LANES)), area & 127)
        far = lane_gather(jnp.broadcast_to(table_ref[1:2, :], (8, LANES)), area & 127)
        weight = jnp.where(area < LANES, near, far)
        weight_slot_ref[rows, :] = jnp.where(cell_high > 0.0, weight, 0.0)


def expand_columns(bottom_ref, column_slot_ref, field_scr, wind_slot_ref):
    def expand(step, carry):
        index = [column_slot_ref[pl.ds(pl.multiple_of(step * 32 + 8 * j, 8), 8), :] for j in range(4)]
        high = [x >> 7 for x in index]
        low = [x & 127 for x in index]
        totals = [[jnp.zeros((8, LANES), F32) for _ in range(4)] for _ in range(4)]
        for h in range(16):
            tables = [
                jnp.broadcast_to(bottom_ref[f, h : h + 1, :], (8, LANES)) for f in (0, 1, 4, 5)
            ]
            for j in range(4):
                hit = high[j] == h
                for f in range(4):
                    totals[j][f] = jnp.where(hit, lane_gather(tables[f], low[j]), totals[j][f])
        for j in range(4):
            rows = pl.ds(pl.multiple_of(step * 32 + 8 * j, 8), 8)
            for f in range(3):
                field_scr[f + 1, rows, :] = totals[j][f]
            wind_slot_ref[rows, :] = totals[j][3]
        return carry

    lax.fori_loop(0, 6, expand, 0)


def soil_block(a, b, soil_ref, capacity_ref, conductance_ref, exchange_ref, wetness_ref, type_ref, counts_ref,
               cells_scr, soil_out_ref, table_scr):
    tiles = pl.ds(16 * a + b, 8, stride=2)
    here = (pl.ds(pl.multiple_of(8 * a, 8), 8), slice(LANES * b, LANES * b + LANES))
    bottom_t = cells_scr[0][here]
    bottom_q = cells_scr[1][here]
    heat_scale = cells_scr[2][here]
    kind = type_ref[tiles, :]
    total = jnp.zeros((8, LANES), I32)
    for t in range(4):
        total = jnp.where(kind == t, counts_ref[t], total)
    heat, moist, drag = (exchange_ref[i, tiles, :] for i in range(3))
    gain_t = heat / (1.0 + heat * heat_scale)
    gain_q = moist / (1.0 + moist * heat_scale)
    link_prev = factor = reduced = None
    factors, reduceds = [], []
    for layer in range(8):
        rows = pl.ds((16 * a + b) * 8 + layer, 8, stride=16)
        conductance = conductance_ref[rows, :]
        capacity = capacity_ref[rows, :]
        link = jnp.where(total > layer + 1, conductance, 0.0)
        deep = jnp.where(total == layer + 1, conductance, 0.0)
        diagonal = capacity + link + deep
        rhs = capacity * soil_ref[rows, :]
        if layer == 0:
            divisor = diagonal + gain_t
            rhs = rhs + gain_t * bottom_t
        else:
            divisor = diagonal + link_prev + link_prev * factor
            rhs = rhs + link_prev * reduced
        inverse = 1.0 / divisor
        factor = -link * inverse
        reduced = rhs * inverse
        factors.append(factor)
        reduceds.append(reduced)
        link_prev = link
    value = None
    for layer in range(7, -1, -1):
        rows = pl.ds((16 * a + b) * 8 + layer, 8, stride=16)
        value = reduceds[layer] if layer == 7 else reduceds[layer] - factors[layer] * value
        kept = value if layer == 0 else jnp.where(total > layer, value, soil_ref[rows, :])
        soil_out_ref[rows, :] = kept
    table_scr[0, tiles, :] = gain_t * (value - bottom_t)
    table_scr[1, tiles, :] = gain_q * (wetness_ref[tiles, :] + 0.5 * value - bottom_q)
    table_scr[2, tiles, :] = drag


def cells_of_slots(index_scr, field_scr, piece_scr, left_scr, right_scr, acc_scr, cells_scr):
    index_scr[...] = field_scr[0].astype(I32) - 256
    for f in range(3):
        for p, piece in enumerate(split3(field_scr[f + 1])):
            piece_scr[3 * f + p] = piece
    acc_scr[...] = jnp.zeros_like(acc_scr)
    highs = iota((48, LANES), 0)
    lows = iota((256, LANES), 0)

    def scatter_body(step, carry):
        for q in range(8):
            r = step * 8 + q
            cell = index_scr[pl.ds(r, 1), :]
            lanes = slice(q * LANES, (q + 1) * LANES)
            right_scr[:, lanes] = (lows == (cell & 255)).astype(F32).astype(BF16)
            onehot = (highs == (cell >> 8)).astype(F32).astype(BF16)
            for p in range(9):
                piece = jnp.broadcast_to(piece_scr[p, pl.ds(r, 1), :], (48, LANES)).astype(BF16)
                left_scr[48 * p : 48 * p + 48, lanes] = onehot * piece
        acc_scr[...] += dot_nt(left_scr[...], right_scr[...])
        return carry

    lax.fori_loop(0, SLOT_ROWS // 8, scatter_body, 0)
    for f in range(3):
        base = 144 * f
        cells_scr[f] = (
            acc_scr[base : base + 48] + acc_scr[base + 48 : base + 96] + acc_scr[base + 96 : base + 144]
        )


def solve_soil(*refs):
    def soil_body(a, carry):
        for b in range(2):
            soil_block(a, b, *refs)
        return carry

    lax.fori_loop(0, 6, soil_body, 0)


def slots_of_cells(index_scr, table_scr, field_scr):
    def gather_step(step, carry):
        index = [index_scr[pl.ds(pl.multiple_of(step * 48 + 8 * j, 8), 8), :] for j in range(6)]
        high = [x >> 7 for x in index]
        low = [x & 127 for x in index]

        def row_body(four, totals):
            totals = [list(x) for x in totals]
            for u in range(4):
                h = four * 4 + u
                tables = [
                    jnp.broadcast_to(table_scr[f, pl.ds(h, 1), :], (8, LANES)) for f in range(3)
                ]
                for j in range(6):
                    hit = high[j] == h
                    for f in range(3):
                        totals[j][f] = jnp.where(hit, lane_gather(tables[f], low[j]), totals[j][f])
            return tuple(tuple(x) for x in totals)

        zero = jnp.zeros((8, LANES), F32)
        totals = lax.fori_loop(0, 24, row_body, ((zero,) * 3,) * 6)
        for j in range(6):
            rows = pl.ds(pl.multiple_of(step * 48 + 8 * j, 8), 8)
            for f in range(3):
                field_scr[f, rows, :] = totals[j][f]
        return carry

    lax.fori_loop(0, 4, gather_step, 0)


def column_sums(
    column_slot_ref, weight_slot_ref, wind_slot_ref, field_scr, piece_scr, left_scr, right_scr, acc_scr
):
    weight = weight_slot_ref[...]
    drag = field_scr[2]
    values = (
        weight * field_scr[0],
        weight * field_scr[1],
        weight * (drag / (1.0 + drag * wind_slot_ref[...])),
        weight,
    )
    for f in range(4):
        for p, piece in enumerate(split3(values[f])):
            piece_scr[3 * f + p] = piece
    acc_scr[...] = jnp.zeros_like(acc_scr)
    highs = iota((16, LANES), 0)
    lows = iota((LANES, LANES), 0)

    def scatter_body(step, carry):
        for q in range(8):
            r = step * 8 + q
            column = column_slot_ref[pl.ds(r, 1), :]
            lanes = slice(q * LANES, (q + 1) * LANES)
            right_scr[:, lanes] = (lows == (column & 127)).astype(F32).astype(BF16)
            onehot = (highs == (column >> 7)).astype(F32).astype(BF16)
            for p in range(12):
                piece = jnp.broadcast_to(piece_scr[p, pl.ds(r, 1), :], (16, LANES)).astype(BF16)
                left_scr[16 * p : 16 * p + 16, lanes] = onehot * piece
        acc_scr[...] += dot_nt(left_scr[...], right_scr[...])
        return carry

    lax.fori_loop(0, SLOT_ROWS // 8, scatter_body, 0)
    sums = []
    for f in range(4):
        base = 48 * f
        sums.append(acc_scr[base : base + 16] + acc_scr[base + 16 : base + 32] + acc_scr[base + 32 : base + 48])
    return sums


def up_sweep(sums, factor_ref, reduced_ref, bottom_ref, out_ref):
    flux = (
        sums[0] / sums[3],
        sums[1] / sums[3],
        -bottom_ref[2] * (sums[2] / sums[3]),
        -bottom_ref[3] * (sums[2] / sums[3]),
    )
    values = []
    for field in range(4):
        lowest = bottom_ref[field] + bottom_ref[4 + field // 2] * flux[field]
        for half in range(2):
            value = lowest[8 * half : 8 * half + 8]
            out_ref[field, pl.ds(7 * 128 + half * 64 + 7, 8, stride=8), :] = value
            values.append(value)

    def retreat(values, g, i):
        values = list(values)
        for half in range(2):
            rows = pl.ds(pl.multiple_of(g * 128 + i * 16 + half * 8, 8), 8)
            for field in range(4):
                k = 2 * field + half
                values[k] = reduced_ref[field, rows, :] - factor_ref[field // 2, rows, :] * values[k]
                out_ref[field, pl.ds(g * 128 + half * 64 + i, 8, stride=8), :] = values[k]
        return tuple(values)

    values = tuple(values)
    for i in range(6, -1, -1):
        values = retreat(values, 7, i)

    def body(step, values):
        for i in range(7, -1, -1):
            values = retreat(values, 6 - step, i)
        return values

    lax.fori_loop(0, 7, body, values)


def device_of(peer):
    return (peer // 32, lax.rem(peer, 32))


def greet(me):
    barrier = pltpu.get_barrier_semaphore()

    def signal(d, carry):
        pl.semaphore_signal(
            barrier, inc=1, device_id=device_of(lax.rem(me + d, PEERS)),
            device_id_type=pl.DeviceIdType.MESH,
        )
        return carry

    lax.fori_loop(1, PEERS, signal, 0)


def send_all(me, send_ref, recv_ref, rows, send_sem, recv_sem):
    def start(d, carry):
        peer = lax.rem(me + d, PEERS)
        pltpu.make_async_remote_copy(
            src_ref=send_ref.at[pl.ds(pl.multiple_of(peer * MSG_ROWS, MSG_ROWS), rows)],
            dst_ref=recv_ref.at[pl.ds(pl.multiple_of(me * MSG_ROWS, MSG_ROWS), rows)],
            send_sem=send_sem, recv_sem=recv_sem, device_id=device_of(peer),
            device_id_type=pl.DeviceIdType.MESH,
        ).start()
        return carry

    lax.fori_loop(1, PEERS, start, 0)
    own = pl.ds(pl.multiple_of(me * MSG_ROWS, MSG_ROWS), MSG_ROWS)
    recv_ref[own, :] = send_ref[own, :]


def all_of(me, send_ref, recv_ref, rows, send_sem, recv_sem):
    whole = pl.ds(0, (PEERS - 1) * rows)
    return pltpu.make_async_remote_copy(
        src_ref=send_ref.at[whole], dst_ref=recv_ref.at[whole], send_sem=send_sem, recv_sem=recv_sem,
        device_id=device_of(me), device_id_type=pl.DeviceIdType.MESH,
    )


def step_kernel(
    owner_ref, cell_ref, column_ref, area_ref, table_ref, profiles_ref, heat_ref, momentum_ref, mass_ref,
    counts_ref, soil_ref, capacity_ref, conductance_ref, exchange_ref, wetness_ref, type_ref,
    out_ref, soil_out_ref,
    column_slot_scr, weight_slot_scr, wind_slot_scr, factor_scr, reduced_scr, bottom_scr,
    piece_scr, onehot_scr, rank_scr, left_scr, right_scr, slot_acc_scr, field_scr,
    slot_piece_scr, cell_acc_scr, cells_scr, table_scr, index_scr, column_acc_scr,
    send_scr, recv_scr, reply_scr, return_scr, sems,
):
    me = lax.axis_index("grp") * 32 + lax.axis_index("tile")
    greet(me)
    prepare_pieces(cell_ref, column_ref, area_ref, piece_scr)
    assign_slots(
        owner_ref, [piece_scr.at[p] for p in range(5)],
        onehot_scr, rank_scr, left_scr, right_scr, slot_acc_scr,
    )
    read_slots(slot_acc_scr, table_ref, field_scr.at[0], column_slot_scr, weight_slot_scr)
    down_sweep(profiles_ref, heat_ref, momentum_ref, mass_ref, factor_scr, reduced_scr, bottom_scr)
    expand_columns(bottom_scr, column_slot_scr, field_scr, wind_slot_scr)
    fields = [field_scr.at[f] for f in range(4)]
    pack_message(fields, send_scr)
    pl.semaphore_wait(pltpu.get_barrier_semaphore(), PEERS - 1)
    send_all(me, send_scr, recv_scr, SEND_ROWS, sems.at[0], sems.at[1])
    there = all_of(me, send_scr, recv_scr, SEND_ROWS, sems.at[0], sems.at[1])
    there.wait_recv()
    unpack_message(recv_scr, fields)
    cells_of_slots(
        index_scr, field_scr, slot_piece_scr, left_scr.at[0:432], right_scr, cell_acc_scr, cells_scr
    )
    solve_soil(
        soil_ref, capacity_ref, conductance_ref, exchange_ref, wetness_ref, type_ref, counts_ref,
        [cells_scr.at[f] for f in range(3)], soil_out_ref, table_scr,
    )
    slots_of_cells(index_scr, table_scr, field_scr)
    pack_message(fields[:3], reply_scr)
    send_all(me, reply_scr, return_scr, REPLY_ROWS, sems.at[2], sems.at[3])
    back = all_of(me, reply_scr, return_scr, REPLY_ROWS, sems.at[2], sems.at[3])
    back.wait_recv()
    unpack_message(return_scr, fields[:3])
    sums = column_sums(
        column_slot_scr, weight_slot_scr, wind_slot_scr, field_scr, slot_piece_scr,
        left_scr.at[0:192], right_scr.at[0:LANES], column_acc_scr,
    )
    up_sweep(sums, factor_scr, reduced_scr, bottom_scr, out_ref)
    there.wait_send()
    back.wait_send()


def call(kernel, out_shapes, scratch, in_specs, **params):
    return pl.pallas_call(
        kernel,
        out_shape=out_shapes,
        in_specs=in_specs,
        out_specs=[pl.BlockSpec(memory_space=pltpu.VMEM)] * len(out_shapes),
        scratch_shapes=scratch,
        compiler_params=pltpu.CompilerParams(vmem_limit_bytes=VMEM_LIMIT, **params),
    )


def tiles_of(x):
    *lead, rows, lanes = x.shape
    x = x.reshape(*lead, rows // 8, 8, lanes // LANES, LANES)
    return jnp.swapaxes(x, -3, -2).reshape(*lead, rows * lanes // LANES, LANES)


def untile(x, rows, lanes):
    *lead, _, _ = x.shape
    x = x.reshape(*lead, rows // 8, lanes // LANES, 8, LANES)
    return jnp.swapaxes(x, -3, -2).reshape(*lead, rows, lanes)


def local(
    profiles, heat_coupling, momentum_coupling, layer_mass, soil_temps, heat_capacity, conductance,
    exchange_coeffs, wetness, area_table, entry_column, entry_owner, entry_cell, entry_area,
    surface_type, layer_counts,
):
    shape = jax.ShapeDtypeStruct
    vmem = pl.BlockSpec(memory_space=pltpu.VMEM)
    smem = pl.BlockSpec(memory_space=pltpu.SMEM)
    flat = lambda x: x.reshape(-1, LANES)
    slots = (SLOT_ROWS, LANES)
    messages = pltpu.VMEM((PEERS * MSG_ROWS, LANES), F32)
    new_profiles, new_soil = call(
        step_kernel,
        [shape((4, 1024, LANES), F32), shape((768, LANES), F32)],
        [
            pltpu.VMEM(slots, I32),
            pltpu.VMEM(slots, F32),
            pltpu.VMEM(slots, F32),
            pltpu.VMEM((2, 1024, LANES), F32),
            pltpu.VMEM((4, 1024, LANES), F32),
            pltpu.VMEM((6, 16, LANES), F32),
            pltpu.VMEM((5, 96, LANES), F32),
            pltpu.VMEM((PEERS, 96 * LANES), BF16),
            pltpu.VMEM((96, LANES), F32),
            pltpu.VMEM((5 * PEERS, 1024), BF16),
            pltpu.VMEM((256, 1024), BF16),
            pltpu.VMEM((5 * PEERS, 256), F32),
            pltpu.VMEM((4,) + slots, F32),
            pltpu.VMEM((12,) + slots, F32),
            pltpu.VMEM((432, 256), F32),
            pltpu.VMEM((3, 48, 256), F32),
            pltpu.VMEM((3, 96, LANES), F32),
            pltpu.VMEM(slots, I32),
            pltpu.VMEM((192, LANES), F32),
            messages, messages, messages, messages,
            pltpu.SemaphoreType.DMA((4,)),
        ],
        [vmem] * 9 + [smem] + [vmem] * 6,
        collective_id=0, has_side_effects=True,
    )(
        flat(entry_owner), flat(entry_cell), flat(entry_column), flat(entry_area), flat(area_table),
        tiles_of(profiles), tiles_of(heat_coupling), tiles_of(momentum_coupling), tiles_of(layer_mass),
        layer_counts, tiles_of(soil_temps), tiles_of(heat_capacity), tiles_of(conductance),
        exchange_coeffs.reshape(3, 96, LANES), flat(wetness), flat(surface_type),
    )
    return untile(new_profiles, 64, 2048), untile(new_soil, 8, 12288)


def solution(mesh):
    split = ("grp", "tile")
    return jax.shard_map(
        local,
        mesh=mesh,
        in_specs=(
            P(None, None, split), P(None, split), P(None, split), P(None, split), P(None, split),
            P(None, split), P(None, split), P(None, split), P(split), P(), P(split), P(split),
            P(split), P(split), P(split), P(),
        ),
        out_specs=(P(None, None, split), P(None, split)),
        check_vma=False,
    )
```

```python
import jax
import jax.numpy as jnp
from jax import lax
from jax.experimental import pallas as pl
from jax.experimental.pallas import tpu as pltpu
from jax.sharding import PartitionSpec as P

PEERS = 128
LANES = 128
SLOT_ROWS = 192
MSG_ROWS = 8
SEND_ROWS = 6
REPLY_ROWS = 5
CHUNKS = 4
CHUNK_PEERS = PEERS // CHUNKS
LAG = 1
BF16 = jnp.bfloat16
F32 = jnp.float32
I32 = jnp.int32
VMEM_LIMIT = 56 * 1024 * 1024


def iota(shape, dim):
    return lax.broadcasted_iota(I32, shape, dim)


def split3(x):
    high = x.astype(BF16).astype(F32)
    rest = x - high
    mid = rest.astype(BF16).astype(F32)
    return high, mid, rest - mid


def lane_gather(table, index):
    return jnp.take_along_axis(table, index, axis=1, mode="promise_in_bounds")


def dot_nt(a, b):
    return lax.dot_general(a, b, (((1,), (1,)), ((), ())), preferred_element_type=F32)


def low_half(shape):
    return iota(shape, 1) < 64


def aligned(x, step):
    return pl.multiple_of(x * step, step)


def pack_group(j, fields, base, message_ref):
    count = len(fields)
    near_rows = lambda f: pl.ds(aligned(j, 64) + f, 8, stride=8)
    far_rows = lambda f: pl.ds(aligned(j, 64) + 512 + f, 8, stride=8)
    part = lambda f, k: fields[f][pl.ds(base + 8 * k, 8), :]
    for f in range(count):
        message_ref[near_rows(f), :] = part(f, 0)
        message_ref[far_rows(f), :] = part(f, 1)
    for pair in range((count + 1) // 2):
        first = part(2 * pair, 2)
        second = part(2 * pair + 1, 2) if 2 * pair + 1 < count else jnp.zeros_like(first)
        low = low_half(first.shape)
        message_ref[near_rows(count + pair), :] = jnp.where(low, first, pltpu.roll(second, 64, 1))
        message_ref[far_rows(count + pair), :] = jnp.where(low, pltpu.roll(first, 64, 1), second)


def unpack_group(j, message_ref, count):
    near_rows = lambda f: pl.ds(aligned(j, 64) + f, 8, stride=8)
    far_rows = lambda f: pl.ds(aligned(j, 64) + 512 + f, 8, stride=8)
    fields = [[message_ref[near_rows(f), :], message_ref[far_rows(f), :]] for f in range(count)]
    for pair in range((count + 1) // 2):
        near = message_ref[near_rows(count + pair), :]
        far = message_ref[far_rows(count + pair), :]
        low = low_half(near.shape)
        fields[2 * pair].append(jnp.where(low, near, pltpu.roll(far, 64, 1)))
        if 2 * pair + 1 < count:
            fields[2 * pair + 1].append(jnp.where(low, pltpu.roll(near, 64, 1), far))
    return fields


def onehot_rows(ids, count):
    return (iota((count, LANES), 0) == ids).astype(F32).astype(BF16)


def rank_entries(owner_ref, rank_scr):
    upper = (iota((LANES, 2 * LANES), 0) < iota((LANES, 2 * LANES), 1)).astype(F32).astype(BF16)
    owners = iota((PEERS, LANES), 0)
    block = 32

    def body(step, base):
        hits = [owners == owner_ref[pl.ds(step * block + q, 1), :] for q in range(block)]
        onehots = jnp.concatenate([hit.astype(F32).astype(BF16) for hit in hits], axis=0)
        before = jnp.dot(onehots, upper, preferred_element_type=F32)
        for q, hit in enumerate(hits):
            here = before[PEERS * q : PEERS * q + PEERS]
            rank_scr[pl.ds(step * block + q, 1), :] = jnp.sum(
                jnp.where(hit, here[:, :LANES] + base, 0.0), axis=0, keepdims=True
            )
            base = base + here[:, LANES:]
        return base

    lax.fori_loop(0, owner_ref.shape[0] // block, body, jnp.zeros((PEERS, LANES), F32))


def assign_slots(owner_ref, rank_scr, piece_scr, acc_scr):
    acc_scr[...] = jnp.zeros_like(acc_scr)
    ranks = iota((2 * LANES, LANES), 0).astype(F32)
    block = 48

    def body(step, carry):
        lefts, rights = [], []
        for q in range(block):
            r = step * block + q
            onehot = onehot_rows(owner_ref[pl.ds(r, 1), :], PEERS)
            lefts.append(jnp.concatenate([
                onehot * jnp.broadcast_to(piece_scr[p, pl.ds(r, 1), :], (PEERS, LANES)).astype(BF16)
                for p in range(5)
            ], axis=0))
            rights.append((ranks == rank_scr[pl.ds(r, 1), :]).astype(F32).astype(BF16))
        acc_scr[...] += dot_nt(jnp.concatenate(lefts, axis=1), jnp.concatenate(rights, axis=1))
        return carry

    lax.fori_loop(0, owner_ref.shape[0] // block, body, 0)


def down_sweep(profiles_ref, heat_ref, momentum_ref, mass_ref, factor_ref, reduced_ref, bottom_scr):
    couplings = (heat_ref, momentum_ref)
    zero = jnp.zeros((8, LANES), F32)

    def rows_of(g, i, half):
        return pl.ds(g * 128 + half * 64 + i, 8, stride=8)

    def body(g, carry):
        link, factor, reduced, inverse = carry
        link, factor, reduced, inverse = list(link), list(factor), list(reduced), list(inverse)
        following = jnp.minimum(g + 1, 7)
        keep = (g < 7).astype(F32)
        for i in range(8):
            for half in range(2):
                mass = mass_ref[rows_of(g, i, half), :]
                out_rows = pl.ds(pl.multiple_of(g * 128 + i * 16 + half * 8, 8), 8)
                for pair in range(2):
                    k = 2 * pair + half
                    if i < 7:
                        below = couplings[pair][rows_of(g, i + 1, half), :]
                    else:
                        below = couplings[pair][rows_of(following, 0, half), :] * keep
                    here = link[k]
                    divisor = mass + here + below + here * factor[k]
                    inverse[k] = 1.0 / divisor
                    factor[k] = -below * inverse[k]
                    factor_ref[pair, out_rows, :] = factor[k]
                    for member in range(2):
                        field = 2 * pair + member
                        m = 2 * field + half
                        value = profiles_ref[field, rows_of(g, i, half), :]
                        reduced[m] = (mass * value + here * reduced[m]) * inverse[k]
                        reduced_ref[field, out_rows, :] = reduced[m]
                    link[k] = below
        return tuple(link), tuple(factor), tuple(reduced), tuple(inverse)

    first = tuple(couplings[k // 2][rows_of(0, 0, k % 2), :] for k in range(4))
    _, _, reduced, inverse = lax.fori_loop(
        0, 8, body, (first, (zero,) * 4, (zero,) * 8, (zero,) * 4)
    )
    for half in range(2):
        rows = slice(8 * half, 8 * half + 8)
        for field in range(4):
            bottom_scr[field, rows, :] = reduced[2 * field + half]
        bottom_scr[4, rows, :] = inverse[half]
        bottom_scr[5, rows, :] = inverse[2 + half]


def prepare_pieces(cell_ref, column_ref, area_ref, piece_scr):
    cell = cell_ref[...]
    column = column_ref[...]
    piece_scr[0] = ((cell >> 8) + 1).astype(F32)
    piece_scr[1] = (cell & 255).astype(F32)
    piece_scr[2] = (column >> 7).astype(F32)
    piece_scr[3] = (column & 127).astype(F32)
    piece_scr[4] = area_ref[...].astype(F32)


def prepare_group(
    j, acc_scr, table_ref, bottom_ref, field_scr, column_slot_ref, weight_slot_ref, wind_slot_ref, send_scr
):
    near_table = jnp.broadcast_to(table_ref[0:1, :], (8, LANES))
    far_table = jnp.broadcast_to(table_ref[1:2, :], (8, LANES))
    base = aligned(j, 24)

    def pieces(p):
        near = pl.ds(PEERS * p + aligned(j, 8), 8)
        far = pl.ds(PEERS * p + 64 + aligned(j, 8), 8)
        last_near, last_far = acc_scr[near, LANES : 2 * LANES], acc_scr[far, LANES : 2 * LANES]
        last = jnp.where(low_half(last_near.shape), last_near, pltpu.roll(last_far, 64, 1))
        return acc_scr[near, 0:LANES], acc_scr[far, 0:LANES], last

    highs, lows = [], []
    for k, (cell_high, cell_low, row, lane, area) in enumerate(zip(*[pieces(p) for p in range(5)])):
        rows = pl.ds(base + 8 * k, 8)
        field_scr[0, rows, :] = cell_high * 256.0 + cell_low
        row, lane, area = row.astype(I32), lane.astype(I32), area.astype(I32)
        column_slot_ref[rows, :] = row * LANES + lane
        weight = jnp.where(
            area < LANES, lane_gather(near_table, area & 127), lane_gather(far_table, area & 127)
        )
        weight_slot_ref[rows, :] = jnp.where(cell_high > 0.0, weight, 0.0)
        highs.append(row)
        lows.append(lane)
    totals = [[jnp.zeros((8, LANES), F32) for _ in range(4)] for _ in range(3)]
    for h in range(16):
        tables = [jnp.broadcast_to(bottom_ref[f, h : h + 1, :], (8, LANES)) for f in (0, 1, 4, 5)]
        for k in range(3):
            hit = highs[k] == h
            for f in range(4):
                totals[k][f] = jnp.where(hit, lane_gather(tables[f], lows[k]), totals[k][f])
    for k in range(3):
        rows = pl.ds(base + 8 * k, 8)
        for f in range(3):
            field_scr[f + 1, rows, :] = totals[k][f]
        wind_slot_ref[rows, :] = totals[k][3]
    pack_group(j, [field_scr.at[f] for f in range(4)], base, send_scr)


def soil_block(a, b, soil_ref, capacity_ref, conductance_ref, exchange_ref, wetness_ref, type_ref, counts_ref,
               cells_scr, soil_out_ref, table_scr):
    tiles = pl.ds(16 * a + b, 8, stride=2)
    here = (pl.ds(pl.multiple_of(8 * a, 8), 8), slice(LANES * b, LANES * b + LANES))
    bottom_t = cells_scr[0][here]
    bottom_q = cells_scr[1][here]
    heat_scale = cells_scr[2][here]
    kind = type_ref[tiles, :]
    total = jnp.zeros((8, LANES), I32)
    for t in range(4):
        total = jnp.where(kind == t, counts_ref[t], total)
    heat, moist, drag = (exchange_ref[i, tiles, :] for i in range(3))
    gain_t = heat / (1.0 + heat * heat_scale)
    gain_q = moist / (1.0 + moist * heat_scale)
    link_prev = factor = reduced = None
    factors, reduceds = [], []
    for layer in range(8):
        rows = pl.ds((16 * a + b) * 8 + layer, 8, stride=16)
        conductance = conductance_ref[rows, :]
        capacity = capacity_ref[rows, :]
        link = jnp.where(total > layer + 1, conductance, 0.0)
        deep = jnp.where(total == layer + 1, conductance, 0.0)
        diagonal = capacity + link + deep
        rhs = capacity * soil_ref[rows, :]
        if layer == 0:
            divisor = diagonal + gain_t
            rhs = rhs + gain_t * bottom_t
        else:
            divisor = diagonal + link_prev + link_prev * factor
            rhs = rhs + link_prev * reduced
        inverse = 1.0 / divisor
        factor = -link * inverse
        reduced = rhs * inverse
        factors.append(factor)
        reduceds.append(reduced)
        link_prev = link
    value = None
    for layer in range(7, -1, -1):
        rows = pl.ds((16 * a + b) * 8 + layer, 8, stride=16)
        value = reduceds[layer] if layer == 7 else reduceds[layer] - factors[layer] * value
        kept = value if layer == 0 else jnp.where(total > layer, value, soil_ref[rows, :])
        soil_out_ref[rows, :] = kept
    fluxes = (
        gain_t * (value - bottom_t),
        gain_q * (wetness_ref[tiles, :] + 0.5 * value - bottom_q),
        drag,
    )
    for f, flux in enumerate(fluxes):
        table_scr[f, here[0], here[1]] = flux


def clear_cells(acc_scr):
    acc_scr[...] = jnp.zeros_like(acc_scr)


def scatter_group(groups, recv_scr, index_scr, piece_scr, acc_scr):
    lefts, rights = [], []
    for j in groups:
        base = aligned(j, 24)
        ids, *values = unpack_group(j, recv_scr, 4)
        for k in range(3):
            rows = pl.ds(base + 8 * k, 8)
            index_scr[rows, :] = ids[k].astype(I32) - 256
            for f in range(3):
                for p, piece in enumerate(split3(values[f][k])):
                    piece_scr[3 * f + p, rows, :] = piece
        for q in range(24):
            row = pl.ds(base + q, 1)
            cell = index_scr[row, :]
            onehot = onehot_rows(cell >> 8, 48)
            lefts.append(jnp.concatenate([
                onehot * jnp.broadcast_to(piece_scr[p, row, :], (48, LANES)).astype(BF16)
                for p in range(9)
            ], axis=0))
            rights.append(onehot_rows(cell & 255, 256))
    acc_scr[...] += dot_nt(jnp.concatenate(lefts, axis=1), jnp.concatenate(rights, axis=1))


def cells_of_slots(acc_scr, cells_scr):
    for f in range(3):
        base = 144 * f
        cells_scr[f] = (
            acc_scr[base : base + 48] + acc_scr[base + 48 : base + 96] + acc_scr[base + 96 : base + 144]
        )


def solve_soil(*refs):
    def soil_body(a, carry):
        for b in range(2):
            soil_block(a, b, *refs)
        return carry

    lax.fori_loop(0, 6, soil_body, 0)


def cut_table(table_scr, pieces_scr):
    for f in range(3):
        for p, piece in enumerate(split3(table_scr[f])):
            pieces_scr[48 * f : 48 * f + 48, 256 * p : 256 * p + 256] = piece.astype(BF16)


def gather_group(groups, index_scr, pieces_scr, field_scr, reply_scr):
    width = 8 * LANES
    highs, lows = iota((48, width), 0), iota((256, width), 0)
    for j in groups:
        base = aligned(j, 24)
        for k in range(3):
            cell = jnp.concatenate(
                [index_scr[pl.ds(base + 8 * k + q, 1), :] for q in range(8)], axis=1
            )
            onehot = (lows == (cell & 255)).astype(F32).astype(BF16)
            found = sum(
                jnp.dot(pieces_scr[:, 256 * p : 256 * p + 256], onehot, preferred_element_type=F32)
                for p in range(3)
            )
            hit = highs == (cell >> 8)
            for f in range(3):
                value = jnp.sum(
                    jnp.where(hit, found[48 * f : 48 * f + 48], 0.0), axis=0, keepdims=True
                )
                for q in range(8):
                    field_scr[f, pl.ds(base + 8 * k + q, 1), :] = value[:, LANES * q : LANES * q + LANES]
        pack_group(j, [field_scr.at[f] for f in range(3)], base, reply_scr)


def sum_group(groups, return_scr, column_slot_ref, weight_slot_ref, wind_slot_ref, piece_scr, acc_scr):
    lefts, rights = [], []
    for j in groups:
        base = aligned(j, 24)
        heat, moist, drags = unpack_group(j, return_scr, 3)
        for k in range(3):
            rows = pl.ds(base + 8 * k, 8)
            weight = weight_slot_ref[rows, :]
            drag = drags[k]
            values = (
                weight * heat[k],
                weight * moist[k],
                weight * (drag / (1.0 + drag * wind_slot_ref[rows, :])),
                weight,
            )
            for f in range(4):
                for p, piece in enumerate(split3(values[f])):
                    piece_scr[3 * f + p, rows, :] = piece
        for q in range(24):
            row = pl.ds(base + q, 1)
            column = column_slot_ref[row, :]
            onehot = onehot_rows(column >> 7, 16)
            lefts.append(jnp.concatenate([
                onehot * jnp.broadcast_to(piece_scr[p, row, :], (16, LANES)).astype(BF16)
                for p in range(12)
            ], axis=0))
            rights.append(onehot_rows(column & 127, LANES))
    acc_scr[...] += dot_nt(jnp.concatenate(lefts, axis=1), jnp.concatenate(rights, axis=1))


def column_sums(acc_scr):
    sums = []
    for f in range(4):
        base = 48 * f
        sums.append(acc_scr[base : base + 16] + acc_scr[base + 16 : base + 32] + acc_scr[base + 32 : base + 48])
    return sums


def up_sweep(sums, factor_ref, reduced_ref, bottom_ref, out_ref):
    flux = (
        sums[0] / sums[3],
        sums[1] / sums[3],
        -bottom_ref[2] * (sums[2] / sums[3]),
        -bottom_ref[3] * (sums[2] / sums[3]),
    )
    values = []
    for field in range(4):
        lowest = bottom_ref[field] + bottom_ref[4 + field // 2] * flux[field]
        for half in range(2):
            value = lowest[8 * half : 8 * half + 8]
            out_ref[field, pl.ds(7 * 128 + half * 64 + 7, 8, stride=8), :] = value
            values.append(value)

    def retreat(values, g, i):
        values = list(values)
        for half in range(2):
            rows = pl.ds(pl.multiple_of(g * 128 + i * 16 + half * 8, 8), 8)
            for field in range(4):
                k = 2 * field + half
                values[k] = reduced_ref[field, rows, :] - factor_ref[field // 2, rows, :] * values[k]
                out_ref[field, pl.ds(g * 128 + half * 64 + i, 8, stride=8), :] = values[k]
        return tuple(values)

    values = tuple(values)
    for i in range(6, -1, -1):
        values = retreat(values, 7, i)

    def body(step, values):
        for i in range(7, -1, -1):
            values = retreat(values, 6 - step, i)
        return values

    lax.fori_loop(0, 7, body, values)


def device_of(peer):
    return (peer // 32, lax.rem(peer, 32))


def greet(me):
    barrier = pltpu.get_barrier_semaphore()

    def signal(d, carry):
        pl.semaphore_signal(
            barrier, inc=1, device_id=device_of(lax.rem(me + d, PEERS)),
            device_id_type=pl.DeviceIdType.MESH,
        )
        return carry

    lax.fori_loop(1, PEERS, signal, 0)


def send_chunk(me, chunk, own, send_ref, recv_ref, rows, send_sem, recv_sem):
    near = CHUNK_PEERS // 2
    mine = lax.rem(me, near) + near * (me // 64)
    here = pl.ds(aligned(me, MSG_ROWS), rows)
    for k in range(1 if own else 0, CHUNK_PEERS):
        place = lax.rem(mine + k, CHUNK_PEERS) if own else k
        peer = near * chunk + place % near + 64 * (place // near)
        pltpu.make_async_remote_copy(
            src_ref=send_ref.at[pl.ds(aligned(peer, MSG_ROWS), rows)], dst_ref=recv_ref.at[here],
            send_sem=send_sem, recv_sem=recv_sem, device_id=device_of(peer),
            device_id_type=pl.DeviceIdType.MESH,
        ).start()
    if own:
        pltpu.make_async_copy(send_ref.at[here], recv_ref.at[here], recv_sem).start()


def messages_of(me, count, send_ref, recv_ref, rows, send_sem, recv_sem):
    whole = pl.ds(0, count * rows)
    return pltpu.make_async_remote_copy(
        src_ref=send_ref.at[whole], dst_ref=recv_ref.at[whole], send_sem=send_sem, recv_sem=recv_sem,
        device_id=device_of(me), device_id_type=pl.DeviceIdType.MESH,
    )


def step_kernel(
    owner_ref, cell_ref, column_ref, area_ref, table_ref, profiles_ref, heat_ref, momentum_ref, mass_ref,
    counts_ref, soil_ref, capacity_ref, conductance_ref, exchange_ref, wetness_ref, type_ref,
    out_ref, soil_out_ref,
    column_slot_scr, weight_slot_scr, wind_slot_scr, factor_scr, reduced_scr, bottom_scr,
    piece_scr, rank_scr, slot_acc_scr, field_scr, slot_piece_scr, cell_acc_scr, cells_scr, table_scr,
    table_piece_scr, index_scr, column_acc_scr, send_scr, recv_scr, reply_scr, return_scr,
    sent_sem, there_sems, back_sems,
):
    me = lax.axis_index("grp") * 32 + lax.axis_index("tile")
    mine = lax.rem(me, 64) // (CHUNK_PEERS // 2)
    greet(me)
    prepare_pieces(cell_ref, column_ref, area_ref, piece_scr)
    rank_entries(owner_ref, rank_scr)
    assign_slots(owner_ref, rank_scr, piece_scr, slot_acc_scr)
    down_sweep(profiles_ref, heat_ref, momentum_ref, mass_ref, factor_scr, reduced_scr, bottom_scr)
    cell_acc_scr[...] = jnp.zeros_like(cell_acc_scr)
    column_acc_scr[...] = jnp.zeros_like(column_acc_scr)

    def groups_of(chunk):
        return [chunk * (8 // CHUNKS) + k for k in range(8 // CHUNKS)]

    def ahead(i):
        return lax.rem(mine + i, CHUNKS)

    def behind(i):
        return lax.rem(mine + CHUNKS - i, CHUNKS)

    def prepare(i):
        for j in groups_of(ahead(i)):
            prepare_group(
                j, slot_acc_scr, table_ref, bottom_scr, field_scr, column_slot_scr, weight_slot_scr,
                wind_slot_scr, send_scr,
            )

    def send(i, own):
        send_chunk(me, ahead(i), own, send_scr, recv_scr, SEND_ROWS, sent_sem.at[0], there_sems.at[mine])

    def scatter(i):
        chunk = behind(i)
        messages_of(
            me, CHUNK_PEERS, send_scr, recv_scr, SEND_ROWS, sent_sem.at[0], there_sems.at[chunk]
        ).wait_recv()
        scatter_group(groups_of(chunk), recv_scr, index_scr, slot_piece_scr, cell_acc_scr)

    prepare(0)
    pl.semaphore_wait(pltpu.get_barrier_semaphore(), PEERS - 1)
    send(0, True)

    def there(i, carry):
        prepare(i)
        send(i, False)
        scatter(i - 1)
        return carry

    lax.fori_loop(1, CHUNKS, there, 0)
    scatter(CHUNKS - 1)
    cells_of_slots(cell_acc_scr, cells_scr)
    solve_soil(
        soil_ref, capacity_ref, conductance_ref, exchange_ref, wetness_ref, type_ref, counts_ref,
        [cells_scr.at[f] for f in range(3)], soil_out_ref, table_scr,
    )
    cut_table(table_scr, table_piece_scr)

    def gather(i, own):
        chunk = ahead(i)
        gather_group(groups_of(chunk), index_scr, table_piece_scr, field_scr, reply_scr)
        send_chunk(me, chunk, own, reply_scr, return_scr, REPLY_ROWS, sent_sem.at[1], back_sems.at[mine])

    def collect(i):
        chunk = behind(i)
        messages_of(
            me, CHUNK_PEERS, reply_scr, return_scr, REPLY_ROWS, sent_sem.at[1], back_sems.at[chunk]
        ).wait_recv()
        sum_group(
            groups_of(chunk), return_scr, column_slot_scr, weight_slot_scr, wind_slot_scr,
            slot_piece_scr, column_acc_scr,
        )

    gather(0, True)
    for i in range(1, LAG):
        gather(i, False)

    def back(i, carry):
        gather(i, False)
        collect(i - LAG)
        return carry

    lax.fori_loop(LAG, CHUNKS, back, 0)

    def last(i, carry):
        collect(i)
        return carry

    lax.fori_loop(CHUNKS - LAG, CHUNKS, last, 0)
    up_sweep(column_sums(column_acc_scr), factor_scr, reduced_scr, bottom_scr, out_ref)
    messages_of(
        me, PEERS - 1, send_scr, recv_scr, SEND_ROWS, sent_sem.at[0], there_sems.at[0]
    ).wait_send()
    messages_of(
        me, PEERS - 1, reply_scr, return_scr, REPLY_ROWS, sent_sem.at[1], back_sems.at[0]
    ).wait_send()


def call(kernel, out_shapes, scratch, in_specs, **params):
    return pl.pallas_call(
        kernel,
        out_shape=out_shapes,
        in_specs=in_specs,
        out_specs=[pl.BlockSpec(memory_space=pltpu.VMEM)] * len(out_shapes),
        scratch_shapes=scratch,
        compiler_params=pltpu.CompilerParams(vmem_limit_bytes=VMEM_LIMIT, **params),
    )


def tiles_of(x):
    *lead, rows, lanes = x.shape
    x = x.reshape(*lead, rows // 8, 8, lanes // LANES, LANES)
    return jnp.swapaxes(x, -3, -2).reshape(*lead, rows * lanes // LANES, LANES)


def untile(x, rows, lanes):
    *lead, _, _ = x.shape
    x = x.reshape(*lead, rows // 8, lanes // LANES, 8, LANES)
    return jnp.swapaxes(x, -3, -2).reshape(*lead, rows, lanes)


def local(
    profiles, heat_coupling, momentum_coupling, layer_mass, soil_temps, heat_capacity, conductance,
    exchange_coeffs, wetness, area_table, entry_column, entry_owner, entry_cell, entry_area,
    surface_type, layer_counts,
):
    shape = jax.ShapeDtypeStruct
    vmem = pl.BlockSpec(memory_space=pltpu.VMEM)
    smem = pl.BlockSpec(memory_space=pltpu.SMEM)
    flat = lambda x: x.reshape(-1, LANES)
    slots = (SLOT_ROWS, LANES)
    messages = pltpu.VMEM((PEERS * MSG_ROWS, LANES), F32)
    new_profiles, new_soil = call(
        step_kernel,
        [shape((4, 1024, LANES), F32), shape((768, LANES), F32)],
        [
            pltpu.VMEM(slots, I32),
            pltpu.VMEM(slots, F32),
            pltpu.VMEM(slots, F32),
            pltpu.VMEM((2, 1024, LANES), F32),
            pltpu.VMEM((4, 1024, LANES), F32),
            pltpu.VMEM((6, 16, LANES), F32),
            pltpu.VMEM((5, 96, LANES), F32),
            pltpu.VMEM((96, LANES), F32),
            pltpu.VMEM((5 * PEERS, 256), F32),
            pltpu.VMEM((4,) + slots, F32),
            pltpu.VMEM((12,) + slots, F32),
            pltpu.VMEM((432, 256), F32),
            pltpu.VMEM((3, 48, 256), F32),
            pltpu.VMEM((3, 48, 256), F32),
            pltpu.VMEM((144, 768), BF16),
            pltpu.VMEM(slots, I32),
            pltpu.VMEM((192, LANES), F32),
            messages, messages, messages, messages,
            pltpu.SemaphoreType.DMA((2,)),
            pltpu.SemaphoreType.DMA((CHUNKS,)),
            pltpu.SemaphoreType.DMA((CHUNKS,)),
        ],
        [vmem] * 9 + [smem] + [vmem] * 6,
        collective_id=0, has_side_effects=True,
    )(
        flat(entry_owner), flat(entry_cell), flat(entry_column), flat(entry_area), flat(area_table),
        tiles_of(profiles), tiles_of(heat_coupling), tiles_of(momentum_coupling), tiles_of(layer_mass),
        layer_counts, tiles_of(soil_temps), tiles_of(heat_capacity), tiles_of(conductance),
        exchange_coeffs.reshape(3, 96, LANES), flat(wetness), flat(surface_type),
    )
    return untile(new_profiles, 64, 2048), untile(new_soil, 8, 12288)


def solution(mesh):
    split = ("grp", "tile")
    return jax.shard_map(
        local,
        mesh=mesh,
        in_specs=(
            P(None, None, split), P(None, split), P(None, split), P(None, split), P(None, split),
            P(None, split), P(None, split), P(None, split), P(split), P(), P(split), P(split),
            P(split), P(split), P(split), P(),
        ),
        out_specs=(P(None, None, split), P(None, split)),
        check_vma=False,
    )
```

```python
import jax
import jax.numpy as jnp
from jax import lax
from jax.experimental import pallas as pl
from jax.experimental.pallas import tpu as pltpu
from jax.sharding import PartitionSpec as P

PEERS = 128
LANES = 128
SLOT_ROWS = 192
MSG_ROWS = 8
SEND_ROWS = 6
REPLY_ROWS = 5
CHUNKS = 4
CHUNK_PEERS = PEERS // CHUNKS
LAG = 3
PIECES = 2
BF16 = jnp.bfloat16
F32 = jnp.float32
I32 = jnp.int32
VMEM_LIMIT = 56 * 1024 * 1024


def iota(shape, dim):
    return lax.broadcasted_iota(I32, shape, dim)


def split(x):
    pieces = []
    for _ in range(PIECES):
        pieces.append(x.astype(BF16).astype(F32))
        x = x - pieces[-1]
    return pieces


def lane_gather(table, index):
    return jnp.take_along_axis(table, index, axis=1, mode="promise_in_bounds")


def dot_nt(a, b):
    return lax.dot_general(a, b, (((1,), (1,)), ((), ())), preferred_element_type=F32)


def low_half(shape):
    return iota(shape, 1) < 64


def aligned(x, step):
    return pl.multiple_of(x * step, step)


def pack_group(j, fields, base, message_ref):
    count = len(fields)
    near_rows = lambda f: pl.ds(aligned(j, 64) + f, 8, stride=8)
    far_rows = lambda f: pl.ds(aligned(j, 64) + 512 + f, 8, stride=8)
    part = lambda f, k: fields[f][pl.ds(base + 8 * k, 8), :]
    for f in range(count):
        message_ref[near_rows(f), :] = part(f, 0)
        message_ref[far_rows(f), :] = part(f, 1)
    for pair in range((count + 1) // 2):
        first = part(2 * pair, 2)
        second = part(2 * pair + 1, 2) if 2 * pair + 1 < count else jnp.zeros_like(first)
        low = low_half(first.shape)
        message_ref[near_rows(count + pair), :] = jnp.where(low, first, pltpu.roll(second, 64, 1))
        message_ref[far_rows(count + pair), :] = jnp.where(low, pltpu.roll(first, 64, 1), second)


def unpack_group(j, message_ref, count):
    near_rows = lambda f: pl.ds(aligned(j, 64) + f, 8, stride=8)
    far_rows = lambda f: pl.ds(aligned(j, 64) + 512 + f, 8, stride=8)
    fields = [[message_ref[near_rows(f), :], message_ref[far_rows(f), :]] for f in range(count)]
    for pair in range((count + 1) // 2):
        near = message_ref[near_rows(count + pair), :]
        far = message_ref[far_rows(count + pair), :]
        low = low_half(near.shape)
        fields[2 * pair].append(jnp.where(low, near, pltpu.roll(far, 64, 1)))
        if 2 * pair + 1 < count:
            fields[2 * pair + 1].append(jnp.where(low, pltpu.roll(near, 64, 1), far))
    return fields


def onehot_rows(ids, count):
    return (iota((count, LANES), 0) == ids).astype(F32).astype(BF16)


def rank_entries(owner_ref, rank_scr, greet):
    upper = (iota((LANES, 2 * LANES), 0) < iota((LANES, 2 * LANES), 1)).astype(F32).astype(BF16)
    owners = iota((PEERS, LANES), 0)
    block = 32

    def body(step, base):
        greet(step)
        hits = [owners == owner_ref[pl.ds(step * block + q, 1), :] for q in range(block)]
        onehots = jnp.concatenate([hit.astype(F32).astype(BF16) for hit in hits], axis=0)
        before = jnp.dot(onehots, upper, preferred_element_type=F32)
        for q, hit in enumerate(hits):
            here = before[PEERS * q : PEERS * q + PEERS]
            rank_scr[pl.ds(step * block + q, 1), :] = jnp.sum(
                jnp.where(hit, here[:, :LANES] + base, 0.0), axis=0, keepdims=True
            )
            base = base + here[:, LANES:]
        return base

    lax.fori_loop(0, owner_ref.shape[0] // block, body, jnp.zeros((PEERS, LANES), F32))


def assign_slots(owner_ref, rank_scr, piece_scr, acc_scr):
    acc_scr[...] = jnp.zeros_like(acc_scr)
    ranks = iota((2 * LANES, LANES), 0).astype(F32)
    block = 48

    def body(step, carry):
        lefts, rights = [], []
        for q in range(block):
            r = step * block + q
            onehot = onehot_rows(owner_ref[pl.ds(r, 1), :], PEERS)
            lefts.append(jnp.concatenate([
                onehot * jnp.broadcast_to(piece_scr[p, pl.ds(r, 1), :], (PEERS, LANES)).astype(BF16)
                for p in range(5)
            ], axis=0))
            rights.append((ranks == rank_scr[pl.ds(r, 1), :]).astype(F32).astype(BF16))
        acc_scr[...] += dot_nt(jnp.concatenate(lefts, axis=1), jnp.concatenate(rights, axis=1))
        return carry

    lax.fori_loop(0, owner_ref.shape[0] // block, body, 0)


def down_sweep(profiles_ref, heat_ref, momentum_ref, mass_ref, factor_ref, reduced_ref, bottom_scr):
    couplings = (heat_ref, momentum_ref)
    zero = jnp.zeros((8, LANES), F32)

    def rows_of(g, i, half):
        return pl.ds(g * 128 + half * 64 + i, 8, stride=8)

    def body(g, carry):
        link, factor, reduced, inverse = carry
        link, factor, reduced, inverse = list(link), list(factor), list(reduced), list(inverse)
        following = jnp.minimum(g + 1, 7)
        keep = (g < 7).astype(F32)
        for i in range(8):
            for half in range(2):
                mass = mass_ref[rows_of(g, i, half), :]
                out_rows = pl.ds(pl.multiple_of(g * 128 + i * 16 + half * 8, 8), 8)
                for pair in range(2):
                    k = 2 * pair + half
                    if i < 7:
                        below = couplings[pair][rows_of(g, i + 1, half), :]
                    else:
                        below = couplings[pair][rows_of(following, 0, half), :] * keep
                    here = link[k]
                    divisor = mass + here + below + here * factor[k]
                    inverse[k] = 1.0 / divisor
                    factor[k] = -below * inverse[k]
                    factor_ref[pair, out_rows, :] = factor[k]
                    for member in range(2):
                        field = 2 * pair + member
                        m = 2 * field + half
                        value = profiles_ref[field, rows_of(g, i, half), :]
                        reduced[m] = (mass * value + here * reduced[m]) * inverse[k]
                        reduced_ref[field, out_rows, :] = reduced[m]
                    link[k] = below
        return tuple(link), tuple(factor), tuple(reduced), tuple(inverse)

    first = tuple(couplings[k // 2][rows_of(0, 0, k % 2), :] for k in range(4))
    _, _, reduced, inverse = lax.fori_loop(
        0, 8, body, (first, (zero,) * 4, (zero,) * 8, (zero,) * 4)
    )
    for half in range(2):
        rows = slice(8 * half, 8 * half + 8)
        for field in range(4):
            bottom_scr[field, rows, :] = reduced[2 * field + half]
        bottom_scr[4, rows, :] = inverse[half]
        bottom_scr[5, rows, :] = inverse[2 + half]


def prepare_pieces(cell_ref, column_ref, area_ref, piece_scr):
    cell = cell_ref[...]
    column = column_ref[...]
    piece_scr[0] = ((cell >> 8) + 1).astype(F32)
    piece_scr[1] = (cell & 255).astype(F32)
    piece_scr[2] = (column >> 7).astype(F32)
    piece_scr[3] = (column & 127).astype(F32)
    piece_scr[4] = area_ref[...].astype(F32)


def prepare_group(
    j, acc_scr, table_ref, bottom_ref, field_scr, column_slot_ref, weight_slot_ref, wind_slot_ref, send_scr
):
    near_table = jnp.broadcast_to(table_ref[0:1, :], (8, LANES))
    far_table = jnp.broadcast_to(table_ref[1:2, :], (8, LANES))
    base = aligned(j, 24)

    def pieces(p):
        near = pl.ds(PEERS * p + aligned(j, 8), 8)
        far = pl.ds(PEERS * p + 64 + aligned(j, 8), 8)
        last_near, last_far = acc_scr[near, LANES : 2 * LANES], acc_scr[far, LANES : 2 * LANES]
        last = jnp.where(low_half(last_near.shape), last_near, pltpu.roll(last_far, 64, 1))
        return acc_scr[near, 0:LANES], acc_scr[far, 0:LANES], last

    highs, lows = [], []
    for k, (cell_high, cell_low, row, lane, area) in enumerate(zip(*[pieces(p) for p in range(5)])):
        rows = pl.ds(base + 8 * k, 8)
        field_scr[0, rows, :] = cell_high * 256.0 + cell_low
        row, lane, area = row.astype(I32), lane.astype(I32), area.astype(I32)
        column_slot_ref[rows, :] = row * LANES + lane
        weight = jnp.where(
            area < LANES, lane_gather(near_table, area & 127), lane_gather(far_table, area & 127)
        )
        weight_slot_ref[rows, :] = jnp.where(cell_high > 0.0, weight, 0.0)
        highs.append(row)
        lows.append(lane)
    totals = [[jnp.zeros((8, LANES), F32) for _ in range(4)] for _ in range(3)]
    for h in range(16):
        tables = [jnp.broadcast_to(bottom_ref[f, h : h + 1, :], (8, LANES)) for f in (0, 1, 4, 5)]
        for k in range(3):
            hit = highs[k] == h
            for f in range(4):
                totals[k][f] = jnp.where(hit, lane_gather(tables[f], lows[k]), totals[k][f])
    for k in range(3):
        rows = pl.ds(base + 8 * k, 8)
        for f in range(3):
            field_scr[f + 1, rows, :] = totals[k][f]
        wind_slot_ref[rows, :] = totals[k][3]
    pack_group(j, [field_scr.at[f] for f in range(4)], base, send_scr)


def soil_block(a, b, soil_ref, capacity_ref, conductance_ref, exchange_ref, wetness_ref, type_ref, counts_ref,
               cells_scr, soil_out_ref, table_scr):
    tiles = pl.ds(16 * a + b, 8, stride=2)
    here = (pl.ds(pl.multiple_of(8 * a, 8), 8), slice(LANES * b, LANES * b + LANES))
    bottom_t = cells_scr[0][here]
    bottom_q = cells_scr[1][here]
    heat_scale = cells_scr[2][here]
    kind = type_ref[tiles, :]
    total = jnp.zeros((8, LANES), I32)
    for t in range(4):
        total = jnp.where(kind == t, counts_ref[t], total)
    heat, moist, drag = (exchange_ref[i, tiles, :] for i in range(3))
    gain_t = heat / (1.0 + heat * heat_scale)
    gain_q = moist / (1.0 + moist * heat_scale)
    link_prev = factor = reduced = None
    factors, reduceds = [], []
    for layer in range(8):
        rows = pl.ds((16 * a + b) * 8 + layer, 8, stride=16)
        conductance = conductance_ref[rows, :]
        capacity = capacity_ref[rows, :]
        link = jnp.where(total > layer + 1, conductance, 0.0)
        deep = jnp.where(total == layer + 1, conductance, 0.0)
        diagonal = capacity + link + deep
        rhs = capacity * soil_ref[rows, :]
        if layer == 0:
            divisor = diagonal + gain_t
            rhs = rhs + gain_t * bottom_t
        else:
            divisor = diagonal + link_prev + link_prev * factor
            rhs = rhs + link_prev * reduced
        inverse = 1.0 / divisor
        factor = -link * inverse
        reduced = rhs * inverse
        factors.append(factor)
        reduceds.append(reduced)
        link_prev = link
    value = None
    for layer in range(7, -1, -1):
        rows = pl.ds((16 * a + b) * 8 + layer, 8, stride=16)
        value = reduceds[layer] if layer == 7 else reduceds[layer] - factors[layer] * value
        kept = value if layer == 0 else jnp.where(total > layer, value, soil_ref[rows, :])
        soil_out_ref[rows, :] = kept
    fluxes = (
        gain_t * (value - bottom_t),
        gain_q * (wetness_ref[tiles, :] + 0.5 * value - bottom_q),
        drag,
    )
    for f, flux in enumerate(fluxes):
        table_scr[f, here[0], here[1]] = flux


def clear_cells(acc_scr):
    acc_scr[...] = jnp.zeros_like(acc_scr)


def scatter_group(groups, recv_scr, index_scr, piece_scr, acc_scr):
    lefts, rights = [], []
    for j in groups:
        base = aligned(j, 24)
        ids, *values = unpack_group(j, recv_scr, 4)
        for k in range(3):
            rows = pl.ds(base + 8 * k, 8)
            index_scr[rows, :] = ids[k].astype(I32) - 256
            for f in range(3):
                for p, piece in enumerate(split(values[f][k])):
                    piece_scr[PIECES * f + p, rows, :] = piece
        for q in range(24):
            row = pl.ds(base + q, 1)
            cell = index_scr[row, :]
            onehot = onehot_rows(cell >> 8, 48)
            lefts.append(jnp.concatenate([
                onehot * jnp.broadcast_to(piece_scr[p, row, :], (48, LANES)).astype(BF16)
                for p in range(3 * PIECES)
            ], axis=0))
            rights.append(onehot_rows(cell & 255, 256))
    acc_scr[...] += dot_nt(jnp.concatenate(lefts, axis=1), jnp.concatenate(rights, axis=1))


def cells_of_slots(acc_scr, cells_scr):
    for f in range(3):
        base = 48 * PIECES * f
        cells_scr[f] = sum(acc_scr[base + 48 * p : base + 48 * p + 48] for p in range(PIECES))


def solve_soil(*refs):
    def soil_body(a, carry):
        for b in range(2):
            soil_block(a, b, *refs)
        return carry

    lax.fori_loop(0, 6, soil_body, 0)


def cut_table(table_scr, pieces_scr):
    for f in range(3):
        for p, piece in enumerate(split(table_scr[f])):
            pieces_scr[48 * f : 48 * f + 48, 256 * p : 256 * p + 256] = piece.astype(BF16)


def gather_group(groups, index_scr, pieces_scr, field_scr, reply_scr):
    width = 8 * LANES
    highs, lows = iota((48, width), 0), iota((256, width), 0)
    for j in groups:
        base = aligned(j, 24)
        for k in range(3):
            cell = jnp.concatenate(
                [index_scr[pl.ds(base + 8 * k + q, 1), :] for q in range(8)], axis=1
            )
            onehot = (lows == (cell & 255)).astype(F32).astype(BF16)
            found = sum(
                jnp.dot(pieces_scr[:, 256 * p : 256 * p + 256], onehot, preferred_element_type=F32)
                for p in range(PIECES)
            )
            hit = highs == (cell >> 8)
            for f in range(3):
                value = jnp.sum(
                    jnp.where(hit, found[48 * f : 48 * f + 48], 0.0), axis=0, keepdims=True
                )
                for q in range(8):
                    field_scr[f, pl.ds(base + 8 * k + q, 1), :] = value[:, LANES * q : LANES * q + LANES]
        pack_group(j, [field_scr.at[f] for f in range(3)], base, reply_scr)


def sum_group(groups, return_scr, column_slot_ref, weight_slot_ref, wind_slot_ref, piece_scr, acc_scr):
    lefts, rights = [], []
    for j in groups:
        base = aligned(j, 24)
        heat, moist, drags = unpack_group(j, return_scr, 3)
        for k in range(3):
            rows = pl.ds(base + 8 * k, 8)
            weight = weight_slot_ref[rows, :]
            drag = drags[k]
            values = (
                weight * heat[k],
                weight * moist[k],
                weight * (drag / (1.0 + drag * wind_slot_ref[rows, :])),
                weight,
            )
            for f in range(4):
                for p, piece in enumerate(split(values[f])):
                    piece_scr[PIECES * f + p, rows, :] = piece
        for q in range(24):
            row = pl.ds(base + q, 1)
            column = column_slot_ref[row, :]
            onehot = onehot_rows(column >> 7, 16)
            lefts.append(jnp.concatenate([
                onehot * jnp.broadcast_to(piece_scr[p, row, :], (16, LANES)).astype(BF16)
                for p in range(4 * PIECES)
            ], axis=0))
            rights.append(onehot_rows(column & 127, LANES))
    acc_scr[...] += dot_nt(jnp.concatenate(lefts, axis=1), jnp.concatenate(rights, axis=1))


def column_sums(acc_scr):
    sums = []
    for f in range(4):
        base = 16 * PIECES * f
        sums.append(sum(acc_scr[base + 16 * p : base + 16 * p + 16] for p in range(PIECES)))
    return sums


def lowest_values(sums, bottom_ref, lowest_ref):
    flux = (
        sums[0] / sums[3],
        sums[1] / sums[3],
        -bottom_ref[2] * (sums[2] / sums[3]),
        -bottom_ref[3] * (sums[2] / sums[3]),
    )
    for field in range(4):
        lowest_ref[field] = bottom_ref[field] + bottom_ref[4 + field // 2] * flux[field]


def up_kernel(
    lowest_ref, factor_ref, reduced_ref, soil_ref, out_ref, soil_out_ref,
    factor_scr, reduced_scr, out_scr, soil_scr, soil_sems, factor_sems, reduced_sems, out_sems,
):
    soil_load = pltpu.make_async_copy(soil_ref, soil_scr, soil_sems.at[0])
    soil_store = pltpu.make_async_copy(soil_scr, soil_out_ref, soil_sems.at[1])

    def part(source, target, sems, g):
        rows = pl.ds(128 * g, 128)
        return pltpu.make_async_copy(source.at[:, rows], target.at[:, rows], sems.at[g])

    loads = [
        (part(factor_ref, factor_scr, factor_sems, g), part(reduced_ref, reduced_scr, reduced_sems, g))
        for g in range(8)
    ]
    stores = [part(out_scr, out_ref, out_sems, g) for g in range(8)]
    for g in range(7, -1, -1):
        for load in loads[g]:
            load.start()
    soil_load.start()
    values = [lowest_ref[field, 8 * half : 8 * half + 8] for field in range(4) for half in range(2)]
    for g in range(7, -1, -1):
        for load in loads[g]:
            load.wait()
        for i in range(7, -1, -1):
            for half in range(2):
                rows = pl.ds(g * 128 + i * 16 + half * 8, 8)
                for field in range(4):
                    k = 2 * field + half
                    if g < 7 or i < 7:
                        factor = factor_scr[field // 2, rows, :]
                        values[k] = reduced_scr[field, rows, :] - factor * values[k]
                    out_scr[field, pl.ds(g * 128 + half * 64 + i, 8, stride=8), :] = values[k]
        stores[g].start()
        if g == 4:
            soil_load.wait()
            soil_store.start()
    for store in stores:
        store.wait()
    soil_store.wait()


def device_of(peer):
    return (peer // 32, lax.rem(peer, 32))


def greet(me, first, count):
    barrier = pltpu.get_barrier_semaphore()
    for k in range(count):
        pl.semaphore_signal(
            barrier, inc=1, device_id=device_of(lax.rem(me + first + k, PEERS)),
            device_id_type=pl.DeviceIdType.MESH,
        )


def send_chunk(me, chunk, own, send_ref, recv_ref, rows, send_sem, recv_sem):
    near = CHUNK_PEERS // 2
    mine = lax.rem(me, near) + near * (me // 64)
    here = pl.ds(aligned(me, MSG_ROWS), rows)
    for k in range(1 if own else 0, CHUNK_PEERS):
        place = lax.rem(mine + k, CHUNK_PEERS)
        peer = near * chunk + place % near + 64 * (place // near)
        pltpu.make_async_remote_copy(
            src_ref=send_ref.at[pl.ds(aligned(peer, MSG_ROWS), rows)], dst_ref=recv_ref.at[here],
            send_sem=send_sem, recv_sem=recv_sem, device_id=device_of(peer),
            device_id_type=pl.DeviceIdType.MESH,
        ).start()
    if own:
        pltpu.make_async_copy(send_ref.at[here], recv_ref.at[here], recv_sem).start()


def messages_of(me, count, send_ref, recv_ref, rows, send_sem, recv_sem):
    whole = pl.ds(0, count * rows)
    return pltpu.make_async_remote_copy(
        src_ref=send_ref.at[whole], dst_ref=recv_ref.at[whole], send_sem=send_sem, recv_sem=recv_sem,
        device_id=device_of(me), device_id_type=pl.DeviceIdType.MESH,
    )


def step_kernel(
    owner_ref, cell_ref, column_ref, area_ref, table_ref, profiles_any, heat_any, momentum_any, mass_any,
    counts_ref, soil_any, capacity_any, conductance_any, exchange_ref, wetness_ref, type_ref,
    lowest_ref, soil_out_ref, factor_any, reduced_any,
    profiles_ref, heat_ref, momentum_ref, mass_ref, soil_ref, capacity_ref, conductance_ref, load_sems,
    column_slot_scr, weight_slot_scr, wind_slot_scr, factor_scr, reduced_scr, bottom_scr,
    piece_scr, rank_scr, slot_acc_scr, field_scr, slot_piece_scr, cell_acc_scr, cells_scr, table_scr,
    table_piece_scr, index_scr, column_acc_scr, send_scr, recv_scr, reply_scr, return_scr,
    sent_sem, there_sems, back_sems,
):
    me = lax.axis_index("grp") * 32 + lax.axis_index("tile")
    mine = lax.rem(me, 64) // (CHUNK_PEERS // 2)
    column_loads = [
        pltpu.make_async_copy(source, target, load_sems.at[k])
        for k, (source, target) in enumerate((
            (heat_any, heat_ref), (momentum_any, momentum_ref), (mass_any, mass_ref),
            (profiles_any, profiles_ref),
        ))
    ]
    soil_loads = [
        pltpu.make_async_copy(source, target, load_sems.at[4 + k])
        for k, (source, target) in enumerate((
            (soil_any, soil_ref), (capacity_any, capacity_ref), (conductance_any, conductance_ref),
        ))
    ]
    sweep_stores = [
        pltpu.make_async_copy(factor_scr, factor_any, load_sems.at[7]),
        pltpu.make_async_copy(reduced_scr, reduced_any, load_sems.at[8]),
    ]
    for load in column_loads + soil_loads:
        load.start()
    greet(me, 1, 1)
    prepare_pieces(cell_ref, column_ref, area_ref, piece_scr)
    rank_entries(owner_ref, rank_scr, lambda step: greet(me, 2 + 42 * step, 42))
    assign_slots(owner_ref, rank_scr, piece_scr, slot_acc_scr)
    for load in column_loads:
        load.wait()
    down_sweep(profiles_ref, heat_ref, momentum_ref, mass_ref, factor_scr, reduced_scr, bottom_scr)
    for store in sweep_stores:
        store.start()
    cell_acc_scr[...] = jnp.zeros_like(cell_acc_scr)
    column_acc_scr[...] = jnp.zeros_like(column_acc_scr)

    def groups_of(chunk):
        return [chunk * (8 // CHUNKS) + k for k in range(8 // CHUNKS)]

    def ahead(i):
        return lax.rem(mine + i, CHUNKS)

    def behind(i):
        return lax.rem(mine + CHUNKS - i, CHUNKS)

    def prepare(i):
        for j in groups_of(ahead(i)):
            prepare_group(
                j, slot_acc_scr, table_ref, bottom_scr, field_scr, column_slot_scr, weight_slot_scr,
                wind_slot_scr, send_scr,
            )

    def send(i, own):
        send_chunk(me, ahead(i), own, send_scr, recv_scr, SEND_ROWS, sent_sem.at[0], there_sems.at[mine])

    def scatter(i):
        chunk = behind(i)
        messages_of(
            me, CHUNK_PEERS, send_scr, recv_scr, SEND_ROWS, sent_sem.at[0], there_sems.at[chunk]
        ).wait_recv()
        scatter_group(groups_of(chunk), recv_scr, index_scr, slot_piece_scr, cell_acc_scr)

    prepare(0)
    pl.semaphore_wait(pltpu.get_barrier_semaphore(), PEERS - 1)
    send(0, True)

    def there(i, carry):
        prepare(i)
        send(i, False)
        return carry

    lax.fori_loop(1, CHUNKS, there, 0)

    def arrive(i, carry):
        scatter(i)
        return carry

    lax.fori_loop(0, CHUNKS, arrive, 0)
    for load in soil_loads:
        load.wait()
    cells_of_slots(cell_acc_scr, cells_scr)
    solve_soil(
        soil_ref, capacity_ref, conductance_ref, exchange_ref, wetness_ref, type_ref, counts_ref,
        [cells_scr.at[f] for f in range(3)], soil_out_ref, table_scr,
    )
    cut_table(table_scr, table_piece_scr)

    def gather(i, own):
        chunk = ahead(i)
        gather_group(groups_of(chunk), index_scr, table_piece_scr, field_scr, reply_scr)
        send_chunk(me, chunk, own, reply_scr, return_scr, REPLY_ROWS, sent_sem.at[1], back_sems.at[mine])

    def collect(i):
        chunk = behind(i)
        messages_of(
            me, CHUNK_PEERS, reply_scr, return_scr, REPLY_ROWS, sent_sem.at[1], back_sems.at[chunk]
        ).wait_recv()
        sum_group(
            groups_of(chunk), return_scr, column_slot_scr, weight_slot_scr, wind_slot_scr,
            slot_piece_scr, column_acc_scr,
        )

    gather(0, True)

    def ask(i, carry):
        gather(i, False)
        return carry

    lax.fori_loop(1, LAG, ask, 0)

    def back(i, carry):
        gather(i, False)
        collect(i - LAG)
        return carry

    if LAG < CHUNKS:
        lax.fori_loop(LAG, CHUNKS, back, 0)

    def last(i, carry):
        collect(i)
        return carry

    lax.fori_loop(CHUNKS - LAG, CHUNKS, last, 0)
    lowest_values(column_sums(column_acc_scr), bottom_scr, lowest_ref)
    for store in sweep_stores:
        store.wait()
    messages_of(
        me, PEERS - 1, send_scr, recv_scr, SEND_ROWS, sent_sem.at[0], there_sems.at[0]
    ).wait_send()
    messages_of(
        me, PEERS - 1, reply_scr, return_scr, REPLY_ROWS, sent_sem.at[1], back_sems.at[0]
    ).wait_send()


def call(kernel, out_shapes, scratch, in_specs, out_specs, **params):
    return pl.pallas_call(
        kernel,
        out_shape=out_shapes,
        in_specs=in_specs,
        out_specs=out_specs,
        scratch_shapes=scratch,
        compiler_params=pltpu.CompilerParams(vmem_limit_bytes=VMEM_LIMIT, **params),
    )


def tiles_of(x):
    *lead, rows, lanes = x.shape
    x = x.reshape(*lead, rows // 8, 8, lanes // LANES, LANES)
    return jnp.swapaxes(x, -3, -2).reshape(*lead, rows * lanes // LANES, LANES)


def untile(x, rows, lanes):
    *lead, _, _ = x.shape
    x = x.reshape(*lead, rows // 8, lanes // LANES, 8, LANES)
    return jnp.swapaxes(x, -3, -2).reshape(*lead, rows, lanes)


def local(
    profiles, heat_coupling, momentum_coupling, layer_mass, soil_temps, heat_capacity, conductance,
    exchange_coeffs, wetness, area_table, entry_column, entry_owner, entry_cell, entry_area,
    surface_type, layer_counts,
):
    shape = jax.ShapeDtypeStruct
    vmem = pl.BlockSpec(memory_space=pltpu.VMEM)
    smem = pl.BlockSpec(memory_space=pltpu.SMEM)
    flat = lambda x: x.reshape(-1, LANES)
    slots = (SLOT_ROWS, LANES)
    messages = pltpu.VMEM((PEERS * MSG_ROWS, LANES), F32)
    anywhere = pl.BlockSpec(memory_space=pl.ANY)
    columns, cells = pltpu.VMEM((1024, LANES), F32), pltpu.VMEM((768, LANES), F32)
    lowest, soil, factor, reduced = call(
        step_kernel,
        [
            shape((4, 16, LANES), F32), shape((768, LANES), F32),
            shape((2, 1024, LANES), F32), shape((4, 1024, LANES), F32),
        ],
        [
            pltpu.VMEM((4, 1024, LANES), F32),
            columns, columns, columns, cells, cells, cells,
            pltpu.SemaphoreType.DMA((9,)),
            pltpu.VMEM(slots, I32),
            pltpu.VMEM(slots, F32),
            pltpu.VMEM(slots, F32),
            pltpu.VMEM((2, 1024, LANES), F32),
            pltpu.VMEM((4, 1024, LANES), F32),
            pltpu.VMEM((6, 16, LANES), F32),
            pltpu.VMEM((5, 96, LANES), F32),
            pltpu.VMEM((96, LANES), F32),
            pltpu.VMEM((5 * PEERS, 256), F32),
            pltpu.VMEM((4,) + slots, F32),
            pltpu.VMEM((4 * PIECES,) + slots, F32),
            pltpu.VMEM((144 * PIECES, 256), F32),
            pltpu.VMEM((3, 48, 256), F32),
            pltpu.VMEM((3, 48, 256), F32),
            pltpu.VMEM((144, 256 * PIECES), BF16),
            pltpu.VMEM(slots, I32),
            pltpu.VMEM((64 * PIECES, LANES), F32),
            messages, messages, messages, messages,
            pltpu.SemaphoreType.DMA((2,)),
            pltpu.SemaphoreType.DMA((CHUNKS,)),
            pltpu.SemaphoreType.DMA((CHUNKS,)),
        ],
        [vmem] * 5 + [anywhere] * 4 + [smem] + [anywhere] * 3 + [vmem] * 3,
        [vmem] * 2 + [anywhere] * 2,
        collective_id=0, has_side_effects=True,
    )(
        flat(entry_owner), flat(entry_cell), flat(entry_column), flat(entry_area), flat(area_table),
        tiles_of(profiles), tiles_of(heat_coupling), tiles_of(momentum_coupling), tiles_of(layer_mass),
        layer_counts, tiles_of(soil_temps), tiles_of(heat_capacity), tiles_of(conductance),
        exchange_coeffs.reshape(3, 96, LANES), flat(wetness), flat(surface_type),
    )
    new_profiles, new_soil = call(
        up_kernel,
        [shape((4, 1024, LANES), F32), shape((768, LANES), F32)],
        [
            pltpu.VMEM((2, 1024, LANES), F32),
            pltpu.VMEM((4, 1024, LANES), F32),
            pltpu.VMEM((4, 1024, LANES), F32),
            cells,
            pltpu.SemaphoreType.DMA((2,)),
            pltpu.SemaphoreType.DMA((8,)),
            pltpu.SemaphoreType.DMA((8,)),
            pltpu.SemaphoreType.DMA((8,)),
        ],
        [vmem] + [anywhere] * 3,
        [anywhere] * 2,
    )(lowest, factor, reduced, soil)
    return untile(new_profiles, 64, 2048), untile(new_soil, 8, 12288)


def solution(mesh):
    split = ("grp", "tile")
    return jax.shard_map(
        local,
        mesh=mesh,
        in_specs=(
            P(None, None, split), P(None, split), P(None, split), P(None, split), P(None, split),
            P(None, split), P(None, split), P(None, split), P(split), P(), P(split), P(split),
            P(split), P(split), P(split), P(),
        ),
        out_specs=(P(None, None, split), P(None, split)),
        check_vma=False,
    )
```

```python
import jax
import jax.numpy as jnp
from jax import lax
from jax.experimental import pallas as pl
from jax.experimental.pallas import tpu as pltpu
from jax.sharding import PartitionSpec as P

PEERS = 128
LANES = 128
SLOT_ROWS = 192
MSG_ROWS = 8
SEND_ROWS = 6
REPLY_ROWS = 5
CHUNKS = 4
CHUNK_PEERS = PEERS // CHUNKS
LAG = 3
PIECES = 2
BF16 = jnp.bfloat16
F32 = jnp.float32
I32 = jnp.int32
VMEM_LIMIT = 28 * 1024 * 1024


def iota(shape, dim):
    return lax.broadcasted_iota(I32, shape, dim)


def split(x):
    pieces = []
    for _ in range(PIECES):
        pieces.append(x.astype(BF16).astype(F32))
        x = x - pieces[-1]
    return pieces


def lane_gather(table, index):
    return jnp.take_along_axis(table, index, axis=1, mode="promise_in_bounds")


def dot_nt(a, b):
    return lax.dot_general(a, b, (((1,), (1,)), ((), ())), preferred_element_type=F32)


def low_half(shape):
    return iota(shape, 1) < 64


def aligned(x, step):
    return pl.multiple_of(x * step, step)


def pack_group(j, fields, base, message_ref):
    count = len(fields)
    near_rows = lambda f: pl.ds(aligned(j, 64) + f, 8, stride=8)
    far_rows = lambda f: pl.ds(aligned(j, 64) + 512 + f, 8, stride=8)
    part = lambda f, k: fields[f][pl.ds(base + 8 * k, 8), :]
    for f in range(count):
        message_ref[near_rows(f), :] = part(f, 0)
        message_ref[far_rows(f), :] = part(f, 1)
    for pair in range((count + 1) // 2):
        first = part(2 * pair, 2)
        second = part(2 * pair + 1, 2) if 2 * pair + 1 < count else jnp.zeros_like(first)
        low = low_half(first.shape)
        message_ref[near_rows(count + pair), :] = jnp.where(low, first, pltpu.roll(second, 64, 1))
        message_ref[far_rows(count + pair), :] = jnp.where(low, pltpu.roll(first, 64, 1), second)


def unpack_group(j, message_ref, count):
    near_rows = lambda f: pl.ds(aligned(j, 64) + f, 8, stride=8)
    far_rows = lambda f: pl.ds(aligned(j, 64) + 512 + f, 8, stride=8)
    fields = [[message_ref[near_rows(f), :], message_ref[far_rows(f), :]] for f in range(count)]
    for pair in range((count + 1) // 2):
        near = message_ref[near_rows(count + pair), :]
        far = message_ref[far_rows(count + pair), :]
        low = low_half(near.shape)
        fields[2 * pair].append(jnp.where(low, near, pltpu.roll(far, 64, 1)))
        if 2 * pair + 1 < count:
            fields[2 * pair + 1].append(jnp.where(low, pltpu.roll(near, 64, 1), far))
    return fields


def onehot_rows(ids, count):
    return (iota((count, LANES), 0) == ids).astype(F32).astype(BF16)


def rank_entries(owner_ref, rank_scr, greet):
    upper = (iota((LANES, 2 * LANES), 0) < iota((LANES, 2 * LANES), 1)).astype(F32).astype(BF16)
    owners = iota((PEERS, LANES), 0)
    block = 32

    def body(step, base):
        greet(step)
        hits = [owners == owner_ref[pl.ds(step * block + q, 1), :] for q in range(block)]
        onehots = jnp.concatenate([hit.astype(F32).astype(BF16) for hit in hits], axis=0)
        before = jnp.dot(onehots, upper, preferred_element_type=F32)
        for q, hit in enumerate(hits):
            here = before[PEERS * q : PEERS * q + PEERS]
            rank_scr[pl.ds(step * block + q, 1), :] = jnp.sum(
                jnp.where(hit, here[:, :LANES] + base, 0.0), axis=0, keepdims=True
            )
            base = base + here[:, LANES:]
        return base

    lax.fori_loop(0, owner_ref.shape[0] // block, body, jnp.zeros((PEERS, LANES), F32))


def assign_slots(owner_ref, rank_scr, piece_scr, acc_scr):
    acc_scr[...] = jnp.zeros_like(acc_scr)
    ranks = iota((2 * LANES, LANES), 0).astype(F32)
    block = 48

    def body(step, carry):
        lefts, rights = [], []
        for q in range(block):
            r = step * block + q
            onehot = onehot_rows(owner_ref[pl.ds(r, 1), :], PEERS)
            lefts.append(jnp.concatenate([
                onehot * jnp.broadcast_to(piece_scr[p, pl.ds(r, 1), :], (PEERS, LANES)).astype(BF16)
                for p in range(5)
            ], axis=0))
            rights.append((ranks == rank_scr[pl.ds(r, 1), :]).astype(F32).astype(BF16))
        acc_scr[...] += dot_nt(jnp.concatenate(lefts, axis=1), jnp.concatenate(rights, axis=1))
        return carry

    lax.fori_loop(0, owner_ref.shape[0] // block, body, 0)


def down_sweep(profiles_ref, heat_ref, momentum_ref, mass_ref, factor_ref, reduced_ref, bottom_scr):
    couplings = (heat_ref, momentum_ref)
    zero = jnp.zeros((8, LANES), F32)

    def rows_of(g, i, half):
        return pl.ds(g * 128 + half * 64 + i, 8, stride=8)

    def body(g, carry):
        link, factor, reduced, inverse = carry
        link, factor, reduced, inverse = list(link), list(factor), list(reduced), list(inverse)
        following = jnp.minimum(g + 1, 7)
        keep = (g < 7).astype(F32)
        for i in range(8):
            for half in range(2):
                mass = mass_ref[rows_of(g, i, half), :]
                out_rows = pl.ds(pl.multiple_of(g * 128 + i * 16 + half * 8, 8), 8)
                for pair in range(2):
                    k = 2 * pair + half
                    if i < 7:
                        below = couplings[pair][rows_of(g, i + 1, half), :]
                    else:
                        below = couplings[pair][rows_of(following, 0, half), :] * keep
                    here = link[k]
                    divisor = mass + here + below + here * factor[k]
                    inverse[k] = 1.0 / divisor
                    factor[k] = -below * inverse[k]
                    factor_ref[pair, out_rows, :] = factor[k]
                    for member in range(2):
                        field = 2 * pair + member
                        m = 2 * field + half
                        value = profiles_ref[field, rows_of(g, i, half), :]
                        reduced[m] = (mass * value + here * reduced[m]) * inverse[k]
                        reduced_ref[field, out_rows, :] = reduced[m]
                    link[k] = below
        return tuple(link), tuple(factor), tuple(reduced), tuple(inverse)

    first = tuple(couplings[k // 2][rows_of(0, 0, k % 2), :] for k in range(4))
    _, _, reduced, inverse = lax.fori_loop(
        0, 8, body, (first, (zero,) * 4, (zero,) * 8, (zero,) * 4)
    )
    for half in range(2):
        rows = slice(8 * half, 8 * half + 8)
        for field in range(4):
            bottom_scr[field, rows, :] = reduced[2 * field + half]
        bottom_scr[4, rows, :] = inverse[half]
        bottom_scr[5, rows, :] = inverse[2 + half]


def prepare_pieces(cell_ref, column_ref, area_ref, piece_scr):
    cell = cell_ref[...]
    column = column_ref[...]
    piece_scr[0] = ((cell >> 8) + 1).astype(F32)
    piece_scr[1] = (cell & 255).astype(F32)
    piece_scr[2] = (column >> 7).astype(F32)
    piece_scr[3] = (column & 127).astype(F32)
    piece_scr[4] = area_ref[...].astype(F32)


def prepare_group(
    j, acc_scr, table_ref, bottom_ref, field_scr, column_slot_ref, weight_slot_ref, wind_slot_ref, send_scr
):
    near_table = jnp.broadcast_to(table_ref[0:1, :], (8, LANES))
    far_table = jnp.broadcast_to(table_ref[1:2, :], (8, LANES))
    base = aligned(j, 24)

    def pieces(p):
        near = pl.ds(PEERS * p + aligned(j, 8), 8)
        far = pl.ds(PEERS * p + 64 + aligned(j, 8), 8)
        last_near, last_far = acc_scr[near, LANES : 2 * LANES], acc_scr[far, LANES : 2 * LANES]
        last = jnp.where(low_half(last_near.shape), last_near, pltpu.roll(last_far, 64, 1))
        return acc_scr[near, 0:LANES], acc_scr[far, 0:LANES], last

    highs, lows = [], []
    for k, (cell_high, cell_low, row, lane, area) in enumerate(zip(*[pieces(p) for p in range(5)])):
        rows = pl.ds(base + 8 * k, 8)
        field_scr[0, rows, :] = cell_high * 256.0 + cell_low
        row, lane, area = row.astype(I32), lane.astype(I32), area.astype(I32)
        column_slot_ref[rows, :] = row * LANES + lane
        weight = jnp.where(
            area < LANES, lane_gather(near_table, area & 127), lane_gather(far_table, area & 127)
        )
        weight_slot_ref[rows, :] = jnp.where(cell_high > 0.0, weight, 0.0)
        highs.append(row)
        lows.append(lane)
    totals = [[jnp.zeros((8, LANES), F32) for _ in range(4)] for _ in range(3)]
    for h in range(16):
        tables = [jnp.broadcast_to(bottom_ref[f, h : h + 1, :], (8, LANES)) for f in (0, 1, 4, 5)]
        for k in range(3):
            hit = highs[k] == h
            for f in range(4):
                totals[k][f] = jnp.where(hit, lane_gather(tables[f], lows[k]), totals[k][f])
    for k in range(3):
        rows = pl.ds(base + 8 * k, 8)
        for f in range(3):
            field_scr[f + 1, rows, :] = totals[k][f]
        wind_slot_ref[rows, :] = totals[k][3]
    pack_group(j, [field_scr.at[f] for f in range(4)], base, send_scr)


def soil_block(a, b, soil_ref, capacity_ref, conductance_ref, exchange_ref, wetness_ref, type_ref, counts_ref,
               cells_scr, soil_out_ref, table_scr):
    tiles = pl.ds(16 * a + b, 8, stride=2)
    here = (pl.ds(pl.multiple_of(8 * a, 8), 8), slice(LANES * b, LANES * b + LANES))
    bottom_t = cells_scr[0][here]
    bottom_q = cells_scr[1][here]
    heat_scale = cells_scr[2][here]
    kind = type_ref[tiles, :]
    total = jnp.zeros((8, LANES), I32)
    for t in range(4):
        total = jnp.where(kind == t, counts_ref[t], total)
    heat, moist, drag = (exchange_ref[i, tiles, :] for i in range(3))
    gain_t = heat / (1.0 + heat * heat_scale)
    gain_q = moist / (1.0 + moist * heat_scale)
    link_prev = factor = reduced = None
    factors, reduceds = [], []
    for layer in range(8):
        rows = pl.ds((16 * a + b) * 8 + layer, 8, stride=16)
        conductance = conductance_ref[rows, :]
        capacity = capacity_ref[rows, :]
        link = jnp.where(total > layer + 1, conductance, 0.0)
        deep = jnp.where(total == layer + 1, conductance, 0.0)
        diagonal = capacity + link + deep
        rhs = capacity * soil_ref[rows, :]
        if layer == 0:
            divisor = diagonal + gain_t
            rhs = rhs + gain_t * bottom_t
        else:
            divisor = diagonal + link_prev + link_prev * factor
            rhs = rhs + link_prev * reduced
        inverse = 1.0 / divisor
        factor = -link * inverse
        reduced = rhs * inverse
        factors.append(factor)
        reduceds.append(reduced)
        link_prev = link
    value = None
    for layer in range(7, -1, -1):
        rows = pl.ds((16 * a + b) * 8 + layer, 8, stride=16)
        value = reduceds[layer] if layer == 7 else reduceds[layer] - factors[layer] * value
        kept = value if layer == 0 else jnp.where(total > layer, value, soil_ref[rows, :])
        soil_out_ref[rows, :] = kept
    fluxes = (
        gain_t * (value - bottom_t),
        gain_q * (wetness_ref[tiles, :] + 0.5 * value - bottom_q),
        drag,
    )
    for f, flux in enumerate(fluxes):
        table_scr[f, here[0], here[1]] = flux


def clear_cells(acc_scr):
    acc_scr[...] = jnp.zeros_like(acc_scr)


def scatter_group(groups, recv_scr, index_scr, piece_scr, acc_scr):
    lefts, rights = [], []
    for j in groups:
        base = aligned(j, 24)
        ids, *values = unpack_group(j, recv_scr, 4)
        for k in range(3):
            rows = pl.ds(base + 8 * k, 8)
            index_scr[rows, :] = ids[k].astype(I32) - 256
            for f in range(3):
                for p, piece in enumerate(split(values[f][k])):
                    piece_scr[PIECES * f + p, rows, :] = piece
        for q in range(24):
            row = pl.ds(base + q, 1)
            cell = index_scr[row, :]
            onehot = onehot_rows(cell >> 8, 48)
            lefts.append(jnp.concatenate([
                onehot * jnp.broadcast_to(piece_scr[p, row, :], (48, LANES)).astype(BF16)
                for p in range(3 * PIECES)
            ], axis=0))
            rights.append(onehot_rows(cell & 255, 256))
    acc_scr[...] += dot_nt(jnp.concatenate(lefts, axis=1), jnp.concatenate(rights, axis=1))


def cells_of_slots(acc_scr, cells_scr):
    for f in range(3):
        base = 48 * PIECES * f
        cells_scr[f] = sum(acc_scr[base + 48 * p : base + 48 * p + 48] for p in range(PIECES))


def solve_soil(*refs):
    def soil_body(a, carry):
        for b in range(2):
            soil_block(a, b, *refs)
        return carry

    lax.fori_loop(0, 6, soil_body, 0)


def cut_table(table_scr, pieces_scr):
    for f in range(3):
        for p, piece in enumerate(split(table_scr[f])):
            pieces_scr[48 * f : 48 * f + 48, 256 * p : 256 * p + 256] = piece.astype(BF16)


def gather_group(groups, index_scr, pieces_scr, field_scr, reply_scr):
    width = 8 * LANES
    highs, lows = iota((48, width), 0), iota((256, width), 0)
    for j in groups:
        base = aligned(j, 24)
        for k in range(3):
            cell = jnp.concatenate(
                [index_scr[pl.ds(base + 8 * k + q, 1), :] for q in range(8)], axis=1
            )
            onehot = (lows == (cell & 255)).astype(F32).astype(BF16)
            found = sum(
                jnp.dot(pieces_scr[:, 256 * p : 256 * p + 256], onehot, preferred_element_type=F32)
                for p in range(PIECES)
            )
            hit = highs == (cell >> 8)
            for f in range(3):
                value = jnp.sum(
                    jnp.where(hit, found[48 * f : 48 * f + 48], 0.0), axis=0, keepdims=True
                )
                for q in range(8):
                    field_scr[f, pl.ds(base + 8 * k + q, 1), :] = value[:, LANES * q : LANES * q + LANES]
        pack_group(j, [field_scr.at[f] for f in range(3)], base, reply_scr)


def sum_group(groups, return_scr, column_slot_ref, weight_slot_ref, wind_slot_ref, piece_scr, acc_scr):
    lefts, rights = [], []
    for j in groups:
        base = aligned(j, 24)
        heat, moist, drags = unpack_group(j, return_scr, 3)
        for k in range(3):
            rows = pl.ds(base + 8 * k, 8)
            weight = weight_slot_ref[rows, :]
            drag = drags[k]
            values = (
                weight * heat[k],
                weight * moist[k],
                weight * (drag / (1.0 + drag * wind_slot_ref[rows, :])),
                weight,
            )
            for f in range(4):
                for p, piece in enumerate(split(values[f])):
                    piece_scr[PIECES * f + p, rows, :] = piece
        for q in range(24):
            row = pl.ds(base + q, 1)
            column = column_slot_ref[row, :]
            onehot = onehot_rows(column >> 7, 16)
            lefts.append(jnp.concatenate([
                onehot * jnp.broadcast_to(piece_scr[p, row, :], (16, LANES)).astype(BF16)
                for p in range(4 * PIECES)
            ], axis=0))
            rights.append(onehot_rows(column & 127, LANES))
    acc_scr[...] += dot_nt(jnp.concatenate(lefts, axis=1), jnp.concatenate(rights, axis=1))


def column_sums(acc_scr):
    sums = []
    for f in range(4):
        base = 16 * PIECES * f
        sums.append(sum(acc_scr[base + 16 * p : base + 16 * p + 16] for p in range(PIECES)))
    return sums


def lowest_values(sums, bottom_ref, lowest_ref):
    flux = (
        sums[0] / sums[3],
        sums[1] / sums[3],
        -bottom_ref[2] * (sums[2] / sums[3]),
        -bottom_ref[3] * (sums[2] / sums[3]),
    )
    for field in range(4):
        lowest_ref[field] = bottom_ref[field] + bottom_ref[4 + field // 2] * flux[field]


def up_kernel(lowest_ref, factor_ref, reduced_ref, soil_ref, out_ref, soil_out_ref, out_scr, soil_sem, out_sems):
    soil = pltpu.make_async_copy(soil_ref, soil_out_ref, soil_sem)
    soil.start()
    stores = [
        pltpu.make_async_copy(
            out_scr.at[:, pl.ds(128 * g, 128)], out_ref.at[:, pl.ds(128 * g, 128)], out_sems.at[g]
        )
        for g in range(8)
    ]
    values = [lowest_ref[field, 8 * half : 8 * half + 8] for field in range(4) for half in range(2)]
    for g in range(7, -1, -1):
        for i in range(7, -1, -1):
            for half in range(2):
                rows = pl.ds(g * 128 + i * 16 + half * 8, 8)
                for field in range(4):
                    k = 2 * field + half
                    if g < 7 or i < 7:
                        factor = factor_ref[field // 2, rows, :]
                        values[k] = reduced_ref[field, rows, :] - factor * values[k]
                    out_scr[field, pl.ds(g * 128 + half * 64 + i, 8, stride=8), :] = values[k]
        stores[g].start()
    for store in stores:
        store.wait()
    soil.wait()


def device_of(peer):
    return (peer // 32, lax.rem(peer, 32))


def greet(me, first, count):
    barrier = pltpu.get_barrier_semaphore()
    for k in range(count):
        pl.semaphore_signal(
            barrier, inc=1, device_id=device_of(lax.rem(me + first + k, PEERS)),
            device_id_type=pl.DeviceIdType.MESH,
        )


def send_chunk(me, chunk, own, send_ref, recv_ref, rows, send_sem, recv_sem):
    near = CHUNK_PEERS // 2
    mine = lax.rem(me, near) + near * (me // 64)
    here = pl.ds(aligned(me, MSG_ROWS), rows)
    for k in range(1 if own else 0, CHUNK_PEERS):
        place = lax.rem(mine + k, CHUNK_PEERS)
        peer = near * chunk + place % near + 64 * (place // near)
        pltpu.make_async_remote_copy(
            src_ref=send_ref.at[pl.ds(aligned(peer, MSG_ROWS), rows)], dst_ref=recv_ref.at[here],
            send_sem=send_sem, recv_sem=recv_sem, device_id=device_of(peer),
            device_id_type=pl.DeviceIdType.MESH,
        ).start()
    if own:
        pltpu.make_async_copy(send_ref.at[here], recv_ref.at[here], recv_sem).start()


def messages_of(me, count, send_ref, recv_ref, rows, send_sem, recv_sem):
    whole = pl.ds(0, count * rows)
    return pltpu.make_async_remote_copy(
        src_ref=send_ref.at[whole], dst_ref=recv_ref.at[whole], send_sem=send_sem, recv_sem=recv_sem,
        device_id=device_of(me), device_id_type=pl.DeviceIdType.MESH,
    )


def step_kernel(
    owner_any, cell_any, column_any, area_any, table_any, profiles_any, heat_any, momentum_any, mass_any,
    counts_ref, soil_any, capacity_any, conductance_any, exchange_any, wetness_any, type_any,
    lowest_ref, soil_out_ref, factor_scr, reduced_scr,
    owner_ref, cell_ref, column_ref, area_ref, table_ref, exchange_ref, wetness_ref, type_ref,
    profiles_ref, heat_ref, momentum_ref, mass_ref, soil_ref, capacity_ref, conductance_ref, load_sems,
    exchange_scr,
    column_slot_scr, weight_slot_scr, wind_slot_scr, bottom_scr,
    piece_scr, rank_scr, slot_acc_scr, field_scr, slot_piece_scr, cell_acc_scr, cells_scr, table_scr,
    table_piece_scr, index_scr, column_acc_scr, send_scr, recv_scr, reply_scr, return_scr,
    sent_sem, there_sems, back_sems,
):
    me = lax.axis_index("grp") * 32 + lax.axis_index("tile")
    mine = lax.rem(me, 64) // (CHUNK_PEERS // 2)
    loads = [
        pltpu.make_async_copy(source, target, load_sems.at[k])
        for k, (source, target) in enumerate((
            (owner_any, owner_ref), (cell_any, cell_ref), (column_any, column_ref), (area_any, area_ref),
            (table_any, table_ref), (heat_any, heat_ref), (momentum_any, momentum_ref),
            (mass_any, mass_ref), (profiles_any, profiles_ref), (exchange_any, exchange_ref),
            (soil_any, soil_ref), (capacity_any, capacity_ref), (conductance_any, conductance_ref),
            (wetness_any, wetness_ref), (type_any, type_ref),
        ))
    ]
    entry_loads, column_loads, soil_loads = loads[:4], loads[4:10], loads[10:]
    for load in loads:
        load.start()
    greet(me, 1, 1)
    for load in entry_loads:
        load.wait()
    prepare_pieces(cell_ref, column_ref, area_ref, piece_scr)
    rank_entries(owner_ref, rank_scr, lambda step: greet(me, 2 + 42 * step, 42))
    assign_slots(owner_ref, rank_scr, piece_scr, slot_acc_scr)
    for load in column_loads:
        load.wait()
    for row in range(3):
        exchange_scr[row] = exchange_ref[row : row + 1, :].reshape(96, LANES)
    down_sweep(profiles_ref, heat_ref, momentum_ref, mass_ref, factor_scr, reduced_scr, bottom_scr)
    cell_acc_scr[...] = jnp.zeros_like(cell_acc_scr)
    column_acc_scr[...] = jnp.zeros_like(column_acc_scr)

    def groups_of(chunk):
        return [chunk * (8 // CHUNKS) + k for k in range(8 // CHUNKS)]

    def ahead(i):
        return lax.rem(mine + i, CHUNKS)

    def behind(i):
        return lax.rem(mine + CHUNKS - i, CHUNKS)

    def prepare(i):
        for j in groups_of(ahead(i)):
            prepare_group(
                j, slot_acc_scr, table_ref, bottom_scr, field_scr, column_slot_scr, weight_slot_scr,
                wind_slot_scr, send_scr,
            )

    def send(i, own):
        send_chunk(me, ahead(i), own, send_scr, recv_scr, SEND_ROWS, sent_sem.at[0], there_sems.at[mine])

    def scatter(i):
        chunk = behind(i)
        messages_of(
            me, CHUNK_PEERS, send_scr, recv_scr, SEND_ROWS, sent_sem.at[0], there_sems.at[chunk]
        ).wait_recv()
        scatter_group(groups_of(chunk), recv_scr, index_scr, slot_piece_scr, cell_acc_scr)

    prepare(0)
    pl.semaphore_wait(pltpu.get_barrier_semaphore(), PEERS - 1)
    send(0, True)

    def there(i, carry):
        prepare(i)
        send(i, False)
        return carry

    lax.fori_loop(1, CHUNKS, there, 0)

    def arrive(i, carry):
        scatter(i)
        return carry

    lax.fori_loop(0, CHUNKS, arrive, 0)
    for load in soil_loads:
        load.wait()
    cells_of_slots(cell_acc_scr, cells_scr)
    solve_soil(
        soil_ref, capacity_ref, conductance_ref, exchange_scr, wetness_ref, type_ref, counts_ref,
        [cells_scr.at[f] for f in range(3)], soil_out_ref, table_scr,
    )
    cut_table(table_scr, table_piece_scr)

    def gather(i, own):
        chunk = ahead(i)
        gather_group(groups_of(chunk), index_scr, table_piece_scr, field_scr, reply_scr)
        send_chunk(me, chunk, own, reply_scr, return_scr, REPLY_ROWS, sent_sem.at[1], back_sems.at[mine])

    def collect(i):
        chunk = behind(i)
        messages_of(
            me, CHUNK_PEERS, reply_scr, return_scr, REPLY_ROWS, sent_sem.at[1], back_sems.at[chunk]
        ).wait_recv()
        sum_group(
            groups_of(chunk), return_scr, column_slot_scr, weight_slot_scr, wind_slot_scr,
            slot_piece_scr, column_acc_scr,
        )

    gather(0, True)

    def ask(i, carry):
        gather(i, False)
        return carry

    lax.fori_loop(1, LAG, ask, 0)

    def back(i, carry):
        gather(i, False)
        collect(i - LAG)
        return carry

    if LAG < CHUNKS:
        lax.fori_loop(LAG, CHUNKS, back, 0)

    def last(i, carry):
        collect(i)
        return carry

    lax.fori_loop(CHUNKS - LAG, CHUNKS, last, 0)
    lowest_values(column_sums(column_acc_scr), bottom_scr, lowest_ref)
    messages_of(
        me, PEERS - 1, send_scr, recv_scr, SEND_ROWS, sent_sem.at[0], there_sems.at[0]
    ).wait_send()
    messages_of(
        me, PEERS - 1, reply_scr, return_scr, REPLY_ROWS, sent_sem.at[1], back_sems.at[0]
    ).wait_send()


def call(kernel, out_shapes, scratch, in_specs, out_specs, **params):
    return pl.pallas_call(
        kernel,
        out_shape=out_shapes,
        in_specs=in_specs,
        out_specs=out_specs,
        scratch_shapes=scratch,
        compiler_params=pltpu.CompilerParams(vmem_limit_bytes=VMEM_LIMIT, **params),
    )


def tiles_of(x):
    *lead, rows, lanes = x.shape
    x = x.reshape(*lead, rows // 8, 8, lanes // LANES, LANES)
    return jnp.swapaxes(x, -3, -2).reshape(*lead, rows * lanes // LANES, LANES)


def untile(x, rows, lanes):
    *lead, _, _ = x.shape
    x = x.reshape(*lead, rows // 8, lanes // LANES, 8, LANES)
    return jnp.swapaxes(x, -3, -2).reshape(*lead, rows, lanes)


def local(
    profiles, heat_coupling, momentum_coupling, layer_mass, soil_temps, heat_capacity, conductance,
    exchange_coeffs, wetness, area_table, entry_column, entry_owner, entry_cell, entry_area,
    surface_type, layer_counts,
):
    shape = jax.ShapeDtypeStruct
    vmem = pl.BlockSpec(memory_space=pltpu.VMEM)
    smem = pl.BlockSpec(memory_space=pltpu.SMEM)
    flat = lambda x: stay(x.reshape(-1, LANES))
    slots = (SLOT_ROWS, LANES)
    messages = pltpu.VMEM((PEERS * MSG_ROWS, LANES), F32)
    hbm = pl.BlockSpec(memory_space=pltpu.HBM)
    entries = pltpu.VMEM((96, LANES), I32)
    stay = lambda x: pltpu.with_memory_space_constraint(x, pltpu.HBM)
    far = lambda x: stay(tiles_of(x))
    columns, cells = pltpu.VMEM((1024, LANES), F32), pltpu.VMEM((768, LANES), F32)
    lowest, soil, factor, reduced = call(
        step_kernel,
        [
            shape((4, 16, LANES), F32), shape((768, LANES), F32),
            shape((2, 1024, LANES), F32), shape((4, 1024, LANES), F32),
        ],
        [
            entries, entries, entries, entries,
            pltpu.VMEM((2, LANES), F32),
            pltpu.VMEM((3, 96 * LANES), F32),
            pltpu.VMEM((96, LANES), F32),
            entries,
            pltpu.VMEM((4, 1024, LANES), F32),
            columns, columns, columns, cells, cells, cells,
            pltpu.SemaphoreType.DMA((15,)),
            pltpu.VMEM((3, 96, LANES), F32),
            pltpu.VMEM(slots, I32),
            pltpu.VMEM(slots, F32),
            pltpu.VMEM(slots, F32),
            pltpu.VMEM((6, 16, LANES), F32),
            pltpu.VMEM((5, 96, LANES), F32),
            pltpu.VMEM((96, LANES), F32),
            pltpu.VMEM((5 * PEERS, 256), F32),
            pltpu.VMEM((4,) + slots, F32),
            pltpu.VMEM((4 * PIECES,) + slots, F32),
            pltpu.VMEM((144 * PIECES, 256), F32),
            pltpu.VMEM((3, 48, 256), F32),
            pltpu.VMEM((3, 48, 256), F32),
            pltpu.VMEM((144, 256 * PIECES), BF16),
            pltpu.VMEM(slots, I32),
            pltpu.VMEM((64 * PIECES, LANES), F32),
            messages, messages, messages, messages,
            pltpu.SemaphoreType.DMA((2,)),
            pltpu.SemaphoreType.DMA((CHUNKS,)),
            pltpu.SemaphoreType.DMA((CHUNKS,)),
        ],
        [hbm] * 9 + [smem] + [hbm] * 6,
        [vmem] * 4,
        collective_id=0, has_side_effects=True,
    )(
        flat(entry_owner), flat(entry_cell), flat(entry_column), flat(entry_area), flat(area_table),
        far(profiles), far(heat_coupling), far(momentum_coupling), far(layer_mass),
        stay(layer_counts), far(soil_temps), far(heat_capacity), far(conductance),
        stay(exchange_coeffs), flat(wetness), flat(surface_type),
    )
    new_profiles, new_soil = call(
        up_kernel,
        [shape((4, 1024, LANES), F32), shape((768, LANES), F32)],
        [
            pltpu.VMEM((4, 1024, LANES), F32),
            pltpu.SemaphoreType.DMA,
            pltpu.SemaphoreType.DMA((8,)),
        ],
        [vmem] * 4,
        [hbm] * 2,
    )(lowest, factor, reduced, soil)
    return untile(new_profiles, 64, 2048), untile(new_soil, 8, 12288)


def solution(mesh):
    split = ("grp", "tile")
    return jax.shard_map(
        local,
        mesh=mesh,
        in_specs=(
            P(None, None, split), P(None, split), P(None, split), P(None, split), P(None, split),
            P(None, split), P(None, split), P(None, split), P(split), P(), P(split), P(split),
            P(split), P(split), P(split), P(),
        ),
        out_specs=(P(None, None, split), P(None, split)),
        check_vma=False,
    )
```

```python
import jax
import jax.numpy as jnp
from jax import lax
from jax.experimental import pallas as pl
from jax.experimental.pallas import tpu as pltpu
from jax.sharding import PartitionSpec as P

PEERS = 128
LANES = 128
SLOT_ROWS = 192
MSG_ROWS = 8
SEND_ROWS = 6
REPLY_ROWS = 5
CHUNKS = 4
CHUNK_PEERS = PEERS // CHUNKS
LAG = 4
PIECES = 2
BF16 = jnp.bfloat16
F32 = jnp.float32
I32 = jnp.int32
VMEM_LIMIT = 28 * 1024 * 1024


def iota(shape, dim):
    return lax.broadcasted_iota(I32, shape, dim)


def split(x):
    pieces = []
    for _ in range(PIECES):
        pieces.append(x.astype(BF16).astype(F32))
        x = x - pieces[-1]
    return pieces


def lane_gather(table, index):
    return jnp.take_along_axis(table, index, axis=1, mode="promise_in_bounds")


def dot_nt(a, b):
    return lax.dot_general(a, b, (((1,), (1,)), ((), ())), preferred_element_type=F32)


def low_half(shape):
    return iota(shape, 1) < 64


def aligned(x, step):
    return pl.multiple_of(x * step, step)


def pack_group(j, fields, base, message_ref):
    count = len(fields)
    near_rows = lambda f: pl.ds(aligned(j, 64) + f, 8, stride=8)
    far_rows = lambda f: pl.ds(aligned(j, 64) + 512 + f, 8, stride=8)
    part = lambda f, k: fields[f][pl.ds(base + 8 * k, 8), :]
    for f in range(count):
        message_ref[near_rows(f), :] = part(f, 0)
        message_ref[far_rows(f), :] = part(f, 1)
    for pair in range((count + 1) // 2):
        first = part(2 * pair, 2)
        second = part(2 * pair + 1, 2) if 2 * pair + 1 < count else jnp.zeros_like(first)
        low = low_half(first.shape)
        message_ref[near_rows(count + pair), :] = jnp.where(low, first, pltpu.roll(second, 64, 1))
        message_ref[far_rows(count + pair), :] = jnp.where(low, pltpu.roll(first, 64, 1), second)


def unpack_group(j, message_ref, count):
    near_rows = lambda f: pl.ds(aligned(j, 64) + f, 8, stride=8)
    far_rows = lambda f: pl.ds(aligned(j, 64) + 512 + f, 8, stride=8)
    fields = [[message_ref[near_rows(f), :], message_ref[far_rows(f), :]] for f in range(count)]
    for pair in range((count + 1) // 2):
        near = message_ref[near_rows(count + pair), :]
        far = message_ref[far_rows(count + pair), :]
        low = low_half(near.shape)
        fields[2 * pair].append(jnp.where(low, near, pltpu.roll(far, 64, 1)))
        if 2 * pair + 1 < count:
            fields[2 * pair + 1].append(jnp.where(low, pltpu.roll(near, 64, 1), far))
    return fields


def onehot_rows(ids, count):
    return (iota((count, LANES), 0) == ids).astype(F32).astype(BF16)


def rank_entries(owner_ref, rank_scr, greet):
    upper = (iota((LANES, 2 * LANES), 0) < iota((LANES, 2 * LANES), 1)).astype(F32).astype(BF16)
    owners = iota((PEERS, LANES), 0)
    block = 32

    def body(step, base):
        greet(step)
        hits = [owners == owner_ref[pl.ds(step * block + q, 1), :] for q in range(block)]
        onehots = jnp.concatenate([hit.astype(F32).astype(BF16) for hit in hits], axis=0)
        before = jnp.dot(onehots, upper, preferred_element_type=F32)
        for q, hit in enumerate(hits):
            here = before[PEERS * q : PEERS * q + PEERS]
            rank_scr[pl.ds(step * block + q, 1), :] = jnp.sum(
                jnp.where(hit, here[:, :LANES] + base, 0.0), axis=0, keepdims=True
            )
            base = base + here[:, LANES:]
        return base

    lax.fori_loop(0, owner_ref.shape[0] // block, body, jnp.zeros((PEERS, LANES), F32))


def assign_slots(owner_ref, rank_scr, piece_scr, acc_scr):
    acc_scr[...] = jnp.zeros_like(acc_scr)
    ranks = iota((2 * LANES, LANES), 0).astype(F32)
    block = 48

    def body(step, carry):
        lefts, rights = [], []
        for q in range(block):
            r = step * block + q
            onehot = onehot_rows(owner_ref[pl.ds(r, 1), :], PEERS)
            lefts.append(jnp.concatenate([
                onehot * jnp.broadcast_to(piece_scr[p, pl.ds(r, 1), :], (PEERS, LANES)).astype(BF16)
                for p in range(3)
            ], axis=0))
            rights.append((ranks == rank_scr[pl.ds(r, 1), :]).astype(F32).astype(BF16))
        acc_scr[...] += dot_nt(jnp.concatenate(lefts, axis=1), jnp.concatenate(rights, axis=1))
        return carry

    lax.fori_loop(0, owner_ref.shape[0] // block, body, 0)


def down_sweep(profiles_ref, heat_ref, momentum_ref, mass_ref, factor_ref, reduced_ref, bottom_scr):
    couplings = (heat_ref, momentum_ref)
    zero = jnp.zeros((8, LANES), F32)

    def rows_of(g, i, half):
        return pl.ds(g * 128 + half * 64 + i, 8, stride=8)

    def body(g, carry):
        link, factor, reduced, inverse = carry
        link, factor, reduced, inverse = list(link), list(factor), list(reduced), list(inverse)
        following = jnp.minimum(g + 1, 7)
        keep = (g < 7).astype(F32)
        for i in range(8):
            for half in range(2):
                mass = mass_ref[rows_of(g, i, half), :]
                out_rows = pl.ds(pl.multiple_of(g * 128 + i * 16 + half * 8, 8), 8)
                for pair in range(2):
                    k = 2 * pair + half
                    if i < 7:
                        below = couplings[pair][rows_of(g, i + 1, half), :]
                    else:
                        below = couplings[pair][rows_of(following, 0, half), :] * keep
                    here = link[k]
                    divisor = mass + here + below + here * factor[k]
                    inverse[k] = 1.0 / divisor
                    factor[k] = -below * inverse[k]
                    factor_ref[pair, out_rows, :] = factor[k]
                    for member in range(2):
                        field = 2 * pair + member
                        m = 2 * field + half
                        value = profiles_ref[field, rows_of(g, i, half), :]
                        reduced[m] = (mass * value + here * reduced[m]) * inverse[k]
                        reduced_ref[field, out_rows, :] = reduced[m]
                    link[k] = below
        return tuple(link), tuple(factor), tuple(reduced), tuple(inverse)

    first = tuple(couplings[k // 2][rows_of(0, 0, k % 2), :] for k in range(4))
    _, _, reduced, inverse = lax.fori_loop(
        0, 8, body, (first, (zero,) * 4, (zero,) * 8, (zero,) * 4)
    )
    for half in range(2):
        rows = slice(8 * half, 8 * half + 8)
        for field in range(4):
            bottom_scr[field, rows, :] = reduced[2 * field + half]
        bottom_scr[4, rows, :] = inverse[half]
        bottom_scr[5, rows, :] = inverse[2 + half]


def encode(number, bits):
    value = ((number & 127) + 128).astype(F32) * (2.0**-64 if bits == 7 else 1.0)
    for b in range(bits):
        value = value * jnp.where(((number >> (7 + b)) & 1) == 1, 2.0 ** (2**b), 1.0)
    return value


def decode(value, bits):
    filled = value > 0.0
    row = jnp.zeros(value.shape, I32)
    if bits == 7:
        large = value >= 128.0
        row = jnp.where(large, 64, 0)
        value = jnp.where(large, value, value * 2.0**64)
        bits = 6
    for b in range(bits - 1, -1, -1):
        large = value >= 128.0 * 2.0 ** (2**b)
        row = jnp.where(large, row + 2**b, row)
        value = jnp.where(large, value * 2.0 ** -(2**b), value)
    return row, jnp.where(filled, value - 128.0, 0.0).astype(I32), filled


def prepare_pieces(cell_ref, column_ref, area_ref, piece_scr):
    piece_scr[0] = encode(cell_ref[...], 7)
    piece_scr[1] = encode(column_ref[...], 4)
    piece_scr[2] = area_ref[...].astype(F32)


def prepare_group(
    j, acc_scr, table_ref, bottom_ref, field_scr, column_slot_ref, weight_slot_ref, send_scr
):
    near_table = jnp.broadcast_to(table_ref[0:1, :], (8, LANES))
    far_table = jnp.broadcast_to(table_ref[1:2, :], (8, LANES))
    base = aligned(j, 24)

    def pieces(p):
        near = pl.ds(PEERS * p + aligned(j, 8), 8)
        far = pl.ds(PEERS * p + 64 + aligned(j, 8), 8)
        last_near, last_far = acc_scr[near, LANES : 2 * LANES], acc_scr[far, LANES : 2 * LANES]
        last = jnp.where(low_half(last_near.shape), last_near, pltpu.roll(last_far, 64, 1))
        return acc_scr[near, 0:LANES], acc_scr[far, 0:LANES], last

    highs, lows = [], []
    for k, (cell, column, area) in enumerate(zip(*[pieces(p) for p in range(3)])):
        rows = pl.ds(base + 8 * k, 8)
        row, lane, filled = decode(cell, 7)
        field_scr[0, rows, :] = jnp.where(filled, row * LANES + lane + 256, 0).astype(F32)
        area = area.astype(I32)
        weight = jnp.where(
            area < LANES, lane_gather(near_table, area & 127), lane_gather(far_table, area & 127)
        )
        weight_slot_ref[rows, :] = jnp.where(filled, weight, 0.0)
        row, lane, _ = decode(column, 4)
        column_slot_ref[rows, :] = row * LANES + lane
        highs.append(row)
        lows.append(lane)
    totals = expand(bottom_ref, (0, 1, 4), highs, lows)
    for k in range(3):
        for f in range(3):
            field_scr[f + 1, pl.ds(base + 8 * k, 8), :] = totals[k][f]
    pack_group(j, [field_scr.at[f] for f in range(4)], base, send_scr)


def expand(bottom_ref, fields, highs, lows):
    totals = [[jnp.zeros((8, LANES), F32) for _ in fields] for _ in highs]
    for h in range(16):
        tables = [jnp.broadcast_to(bottom_ref[f, h : h + 1, :], (8, LANES)) for f in fields]
        for k in range(len(highs)):
            hit = highs[k] == h
            for f, table in enumerate(tables):
                totals[k][f] = jnp.where(hit, lane_gather(table, lows[k]), totals[k][f])
    return totals


def expand_wind(bottom_ref, column_slot_ref, wind_slot_ref):
    def body(step, carry):
        blocks = [pl.ds(aligned(step, 48) + 8 * k, 8) for k in range(6)]
        columns = [column_slot_ref[rows, :] for rows in blocks]
        totals = expand(bottom_ref, (5,), [x >> 7 for x in columns], [x & 127 for x in columns])
        for rows, (value,) in zip(blocks, totals):
            wind_slot_ref[rows, :] = value
        return carry

    lax.fori_loop(0, 4, body, 0)


def soil_block(a, b, soil_ref, capacity_ref, conductance_ref, exchange_ref, wetness_ref, type_ref, counts_ref,
               cells_scr, soil_out_ref, table_scr):
    tiles = pl.ds(16 * a + b, 8, stride=2)
    here = (pl.ds(pl.multiple_of(8 * a, 8), 8), slice(LANES * b, LANES * b + LANES))
    bottom_t = cells_scr[0][here]
    bottom_q = cells_scr[1][here]
    heat_scale = cells_scr[2][here]
    kind = type_ref[tiles, :]
    total = jnp.zeros((8, LANES), I32)
    for t in range(4):
        total = jnp.where(kind == t, counts_ref[t], total)
    heat, moist, drag = (exchange_ref[i, tiles, :] for i in range(3))
    gain_t = heat / (1.0 + heat * heat_scale)
    gain_q = moist / (1.0 + moist * heat_scale)
    link_prev = factor = reduced = None
    factors, reduceds = [], []
    for layer in range(8):
        rows = pl.ds((16 * a + b) * 8 + layer, 8, stride=16)
        conductance = conductance_ref[rows, :]
        capacity = capacity_ref[rows, :]
        link = jnp.where(total > layer + 1, conductance, 0.0)
        deep = jnp.where(total == layer + 1, conductance, 0.0)
        diagonal = capacity + link + deep
        rhs = capacity * soil_ref[rows, :]
        if layer == 0:
            divisor = diagonal + gain_t
            rhs = rhs + gain_t * bottom_t
        else:
            divisor = diagonal + link_prev + link_prev * factor
            rhs = rhs + link_prev * reduced
        inverse = 1.0 / divisor
        factor = -link * inverse
        reduced = rhs * inverse
        factors.append(factor)
        reduceds.append(reduced)
        link_prev = link
    value = None
    for layer in range(7, -1, -1):
        rows = pl.ds((16 * a + b) * 8 + layer, 8, stride=16)
        value = reduceds[layer] if layer == 7 else reduceds[layer] - factors[layer] * value
        kept = value if layer == 0 else jnp.where(total > layer, value, soil_ref[rows, :])
        soil_out_ref[rows, :] = kept
    fluxes = (
        gain_t * (value - bottom_t),
        gain_q * (wetness_ref[tiles, :] + 0.5 * value - bottom_q),
        drag,
    )
    for f, flux in enumerate(fluxes):
        table_scr[f, here[0], here[1]] = flux


def clear_cells(acc_scr):
    acc_scr[...] = jnp.zeros_like(acc_scr)


def scatter_group(groups, recv_scr, index_scr, piece_scr, acc_scr):
    lefts, rights = [], []
    for j in groups:
        base = aligned(j, 24)
        ids, *values = unpack_group(j, recv_scr, 4)
        for k in range(3):
            rows = pl.ds(base + 8 * k, 8)
            index_scr[rows, :] = ids[k].astype(I32) - 256
            for f in range(3):
                for p, piece in enumerate(split(values[f][k])):
                    piece_scr[PIECES * f + p, rows, :] = piece
        for q in range(24):
            row = pl.ds(base + q, 1)
            cell = index_scr[row, :]
            onehot = onehot_rows(cell >> 8, 48)
            lefts.append(jnp.concatenate([
                onehot * jnp.broadcast_to(piece_scr[p, row, :], (48, LANES)).astype(BF16)
                for p in range(3 * PIECES)
            ], axis=0))
            rights.append(onehot_rows(cell & 255, 256))
    acc_scr[...] += dot_nt(jnp.concatenate(lefts, axis=1), jnp.concatenate(rights, axis=1))


def cells_of_slots(acc_scr, cells_scr):
    for f in range(3):
        base = 48 * PIECES * f
        cells_scr[f] = sum(acc_scr[base + 48 * p : base + 48 * p + 48] for p in range(PIECES))


def solve_soil(*refs):
    def soil_body(a, carry):
        for b in range(2):
            soil_block(a, b, *refs)
        return carry

    lax.fori_loop(0, 6, soil_body, 0)


def cut_table(table_scr, pieces_scr):
    for f in range(3):
        for p, piece in enumerate(split(table_scr[f])):
            pieces_scr[48 * f : 48 * f + 48, 256 * p : 256 * p + 256] = piece.astype(BF16)


def gather_group(groups, index_scr, pieces_scr, field_scr, reply_scr):
    width = 8 * LANES
    highs, lows = iota((48, width), 0), iota((256, width), 0)
    for j in groups:
        base = aligned(j, 24)
        for k in range(3):
            cell = jnp.concatenate(
                [index_scr[pl.ds(base + 8 * k + q, 1), :] for q in range(8)], axis=1
            )
            onehot = (lows == (cell & 255)).astype(F32).astype(BF16)
            found = sum(
                jnp.dot(pieces_scr[:, 256 * p : 256 * p + 256], onehot, preferred_element_type=F32)
                for p in range(PIECES)
            )
            hit = highs == (cell >> 8)
            for f in range(3):
                value = jnp.sum(
                    jnp.where(hit, found[48 * f : 48 * f + 48], 0.0), axis=0, keepdims=True
                )
                for q in range(8):
                    field_scr[f, pl.ds(base + 8 * k + q, 1), :] = value[:, LANES * q : LANES * q + LANES]
        pack_group(j, [field_scr.at[f] for f in range(3)], base, reply_scr)


def sum_group(groups, return_scr, column_slot_ref, weight_slot_ref, wind_slot_ref, piece_scr, acc_scr):
    lefts, rights = [], []
    for j in groups:
        base = aligned(j, 24)
        heat, moist, drags = unpack_group(j, return_scr, 3)
        for k in range(3):
            rows = pl.ds(base + 8 * k, 8)
            weight = weight_slot_ref[rows, :]
            drag = drags[k]
            values = (
                weight * heat[k],
                weight * moist[k],
                weight * (drag / (1.0 + drag * wind_slot_ref[rows, :])),
                weight,
            )
            for f in range(4):
                for p, piece in enumerate(split(values[f])):
                    piece_scr[PIECES * f + p, rows, :] = piece
        for q in range(24):
            row = pl.ds(base + q, 1)
            column = column_slot_ref[row, :]
            onehot = onehot_rows(column >> 7, 16)
            lefts.append(jnp.concatenate([
                onehot * jnp.broadcast_to(piece_scr[p, row, :], (16, LANES)).astype(BF16)
                for p in range(4 * PIECES)
            ], axis=0))
            rights.append(onehot_rows(column & 127, LANES))
    acc_scr[...] += dot_nt(jnp.concatenate(lefts, axis=1), jnp.concatenate(rights, axis=1))


def column_sums(acc_scr):
    sums = []
    for f in range(4):
        base = 16 * PIECES * f
        sums.append(sum(acc_scr[base + 16 * p : base + 16 * p + 16] for p in range(PIECES)))
    return sums


def lowest_values(sums, bottom_ref, lowest_ref):
    flux = (
        sums[0] / sums[3],
        sums[1] / sums[3],
        -bottom_ref[2] * (sums[2] / sums[3]),
        -bottom_ref[3] * (sums[2] / sums[3]),
    )
    for field in range(4):
        lowest_ref[field] = bottom_ref[field] + bottom_ref[4 + field // 2] * flux[field]


def up_kernel(lowest_ref, factor_ref, reduced_ref, soil_ref, out_ref, soil_out_ref, out_scr, soil_sem, out_sems):
    soil = pltpu.make_async_copy(soil_ref, soil_out_ref, soil_sem)
    soil.start()
    stores = [
        pltpu.make_async_copy(
            out_scr.at[:, pl.ds(128 * g, 128)], out_ref.at[:, pl.ds(128 * g, 128)], out_sems.at[g]
        )
        for g in range(8)
    ]
    values = [lowest_ref[field, 8 * half : 8 * half + 8] for field in range(4) for half in range(2)]
    for g in range(7, -1, -1):
        for i in range(7, -1, -1):
            for half in range(2):
                rows = pl.ds(g * 128 + i * 16 + half * 8, 8)
                for field in range(4):
                    k = 2 * field + half
                    if g < 7 or i < 7:
                        factor = factor_ref[field // 2, rows, :]
                        values[k] = reduced_ref[field, rows, :] - factor * values[k]
                    out_scr[field, pl.ds(g * 128 + half * 64 + i, 8, stride=8), :] = values[k]
        stores[g].start()
    for store in stores:
        store.wait()
    soil.wait()


def device_of(peer):
    return (peer // 32, lax.rem(peer, 32))


def greet(me, first, count):
    barrier = pltpu.get_barrier_semaphore()
    for k in range(count):
        pl.semaphore_signal(
            barrier, inc=1, device_id=device_of(lax.rem(me + first + k, PEERS)),
            device_id_type=pl.DeviceIdType.MESH,
        )


def send_chunk(me, chunk, own, send_ref, recv_ref, rows, send_sem, recv_sem):
    near = CHUNK_PEERS // 2
    mine = lax.rem(me, near) + near * (me // 64)
    here = pl.ds(aligned(me, MSG_ROWS), rows)
    for k in range(1 if own else 0, CHUNK_PEERS):
        place = lax.rem(mine + k, CHUNK_PEERS)
        peer = near * chunk + place % near + 64 * (place // near)
        pltpu.make_async_remote_copy(
            src_ref=send_ref.at[pl.ds(aligned(peer, MSG_ROWS), rows)], dst_ref=recv_ref.at[here],
            send_sem=send_sem, recv_sem=recv_sem, device_id=device_of(peer),
            device_id_type=pl.DeviceIdType.MESH,
        ).start()
    if own:
        pltpu.make_async_copy(send_ref.at[here], recv_ref.at[here], recv_sem).start()


def messages_of(me, count, send_ref, recv_ref, rows, send_sem, recv_sem):
    whole = pl.ds(0, count * rows)
    return pltpu.make_async_remote_copy(
        src_ref=send_ref.at[whole], dst_ref=recv_ref.at[whole], send_sem=send_sem, recv_sem=recv_sem,
        device_id=device_of(me), device_id_type=pl.DeviceIdType.MESH,
    )


def step_kernel(
    owner_any, cell_any, column_any, area_any, table_any, profiles_any, heat_any, momentum_any, mass_any,
    counts_ref, soil_any, capacity_any, conductance_any, exchange_any, wetness_any, type_any,
    lowest_ref, soil_out_ref, factor_scr, reduced_scr,
    owner_ref, cell_ref, column_ref, area_ref, table_ref, exchange_ref, wetness_ref, type_ref,
    profiles_ref, heat_ref, momentum_ref, mass_ref, soil_ref, capacity_ref, conductance_ref, load_sems,
    exchange_scr,
    column_slot_scr, weight_slot_scr, wind_slot_scr, bottom_scr,
    piece_scr, rank_scr, slot_acc_scr, field_scr, slot_piece_scr, cell_acc_scr, cells_scr, table_scr,
    table_piece_scr, index_scr, column_acc_scr, send_scr, recv_scr, reply_scr, return_scr,
    sent_sem, there_sems, back_sems,
):
    me = lax.axis_index("grp") * 32 + lax.axis_index("tile")
    mine = lax.rem(me, 64) // (CHUNK_PEERS // 2)
    loads = [
        pltpu.make_async_copy(source, target, load_sems.at[k])
        for k, (source, target) in enumerate((
            (owner_any, owner_ref), (cell_any, cell_ref), (column_any, column_ref), (area_any, area_ref),
            (table_any, table_ref), (heat_any, heat_ref), (momentum_any, momentum_ref),
            (mass_any, mass_ref), (profiles_any, profiles_ref), (exchange_any, exchange_ref),
            (soil_any, soil_ref), (capacity_any, capacity_ref), (conductance_any, conductance_ref),
            (wetness_any, wetness_ref), (type_any, type_ref),
        ))
    ]
    entry_loads, column_loads, soil_loads = loads[:4], loads[4:10], loads[10:]
    for load in loads:
        load.start()
    greet(me, 1, 1)
    for load in entry_loads:
        load.wait()
    prepare_pieces(cell_ref, column_ref, area_ref, piece_scr)
    rank_entries(owner_ref, rank_scr, lambda step: greet(me, 2 + 42 * step, 42))
    assign_slots(owner_ref, rank_scr, piece_scr, slot_acc_scr)
    for load in column_loads:
        load.wait()
    for row in range(3):
        exchange_scr[row] = exchange_ref[row : row + 1, :].reshape(96, LANES)
    down_sweep(profiles_ref, heat_ref, momentum_ref, mass_ref, factor_scr, reduced_scr, bottom_scr)
    cell_acc_scr[...] = jnp.zeros_like(cell_acc_scr)
    column_acc_scr[...] = jnp.zeros_like(column_acc_scr)

    def groups_of(chunk):
        return [chunk * (8 // CHUNKS) + k for k in range(8 // CHUNKS)]

    def ahead(i):
        return lax.rem(mine + i, CHUNKS)

    def behind(i):
        return lax.rem(mine + CHUNKS - i, CHUNKS)

    def prepare(i):
        for j in groups_of(ahead(i)):
            prepare_group(
                j, slot_acc_scr, table_ref, bottom_scr, field_scr, column_slot_scr, weight_slot_scr,
                send_scr,
            )

    def send(i, own):
        send_chunk(me, ahead(i), own, send_scr, recv_scr, SEND_ROWS, sent_sem.at[0], there_sems.at[mine])

    def scatter(i):
        chunk = behind(i)
        messages_of(
            me, CHUNK_PEERS, send_scr, recv_scr, SEND_ROWS, sent_sem.at[0], there_sems.at[chunk]
        ).wait_recv()
        scatter_group(groups_of(chunk), recv_scr, index_scr, slot_piece_scr, cell_acc_scr)

    prepare(0)
    pl.semaphore_wait(pltpu.get_barrier_semaphore(), PEERS - 1)
    send(0, True)

    def there(i, carry):
        prepare(i)
        send(i, False)
        return carry

    lax.fori_loop(1, CHUNKS, there, 0)

    def arrive(i, carry):
        scatter(i)
        return carry

    lax.fori_loop(0, CHUNKS, arrive, 0)
    for load in soil_loads:
        load.wait()
    cells_of_slots(cell_acc_scr, cells_scr)
    solve_soil(
        soil_ref, capacity_ref, conductance_ref, exchange_scr, wetness_ref, type_ref, counts_ref,
        [cells_scr.at[f] for f in range(3)], soil_out_ref, table_scr,
    )
    cut_table(table_scr, table_piece_scr)

    def gather(i, own):
        chunk = ahead(i)
        gather_group(groups_of(chunk), index_scr, table_piece_scr, field_scr, reply_scr)
        send_chunk(me, chunk, own, reply_scr, return_scr, REPLY_ROWS, sent_sem.at[1], back_sems.at[mine])

    def collect(i):
        chunk = behind(i)
        messages_of(
            me, CHUNK_PEERS, reply_scr, return_scr, REPLY_ROWS, sent_sem.at[1], back_sems.at[chunk]
        ).wait_recv()
        sum_group(
            groups_of(chunk), return_scr, column_slot_scr, weight_slot_scr, wind_slot_scr,
            slot_piece_scr, column_acc_scr,
        )

    gather(0, True)

    def ask(i, carry):
        gather(i, False)
        return carry

    lax.fori_loop(1, LAG, ask, 0)
    expand_wind(bottom_scr, column_slot_scr, wind_slot_scr)

    def back(i, carry):
        gather(i, False)
        collect(i - LAG)
        return carry

    if LAG < CHUNKS:
        lax.fori_loop(LAG, CHUNKS, back, 0)

    def last(i, carry):
        collect(i)
        return carry

    lax.fori_loop(CHUNKS - LAG, CHUNKS, last, 0)
    lowest_values(column_sums(column_acc_scr), bottom_scr, lowest_ref)
    messages_of(
        me, PEERS - 1, send_scr, recv_scr, SEND_ROWS, sent_sem.at[0], there_sems.at[0]
    ).wait_send()
    messages_of(
        me, PEERS - 1, reply_scr, return_scr, REPLY_ROWS, sent_sem.at[1], back_sems.at[0]
    ).wait_send()


def call(kernel, out_shapes, scratch, in_specs, out_specs, **params):
    return pl.pallas_call(
        kernel,
        out_shape=out_shapes,
        in_specs=in_specs,
        out_specs=out_specs,
        scratch_shapes=scratch,
        compiler_params=pltpu.CompilerParams(vmem_limit_bytes=VMEM_LIMIT, **params),
    )


def tiles_of(x):
    *lead, rows, lanes = x.shape
    x = x.reshape(*lead, rows // 8, 8, lanes // LANES, LANES)
    return jnp.swapaxes(x, -3, -2).reshape(*lead, rows * lanes // LANES, LANES)


def untile(x, rows, lanes):
    *lead, _, _ = x.shape
    x = x.reshape(*lead, rows // 8, lanes // LANES, 8, LANES)
    return jnp.swapaxes(x, -3, -2).reshape(*lead, rows, lanes)


def local(
    profiles, heat_coupling, momentum_coupling, layer_mass, soil_temps, heat_capacity, conductance,
    exchange_coeffs, wetness, area_table, entry_column, entry_owner, entry_cell, entry_area,
    surface_type, layer_counts,
):
    shape = jax.ShapeDtypeStruct
    vmem = pl.BlockSpec(memory_space=pltpu.VMEM)
    smem = pl.BlockSpec(memory_space=pltpu.SMEM)
    flat = lambda x: stay(x.reshape(-1, LANES))
    slots = (SLOT_ROWS, LANES)
    messages = pltpu.VMEM((PEERS * MSG_ROWS, LANES), F32)
    hbm = pl.BlockSpec(memory_space=pltpu.HBM)
    entries = pltpu.VMEM((96, LANES), I32)
    stay = lambda x: pltpu.with_memory_space_constraint(x, pltpu.HBM)
    far = lambda x: stay(tiles_of(x))
    columns, cells = pltpu.VMEM((1024, LANES), F32), pltpu.VMEM((768, LANES), F32)
    lowest, soil, factor, reduced = call(
        step_kernel,
        [
            shape((4, 16, LANES), F32), shape((768, LANES), F32),
            shape((2, 1024, LANES), F32), shape((4, 1024, LANES), F32),
        ],
        [
            entries, entries, entries, entries,
            pltpu.VMEM((2, LANES), F32),
            pltpu.VMEM((3, 96 * LANES), F32),
            pltpu.VMEM((96, LANES), F32),
            entries,
            pltpu.VMEM((4, 1024, LANES), F32),
            columns, columns, columns, cells, cells, cells,
            pltpu.SemaphoreType.DMA((15,)),
            pltpu.VMEM((3, 96, LANES), F32),
            pltpu.VMEM(slots, I32),
            pltpu.VMEM(slots, F32),
            pltpu.VMEM(slots, F32),
            pltpu.VMEM((6, 16, LANES), F32),
            pltpu.VMEM((3, 96, LANES), F32),
            pltpu.VMEM((96, LANES), F32),
            pltpu.VMEM((3 * PEERS, 256), F32),
            pltpu.VMEM((4,) + slots, F32),
            pltpu.VMEM((4 * PIECES,) + slots, F32),
            pltpu.VMEM((144 * PIECES, 256), F32),
            pltpu.VMEM((3, 48, 256), F32),
            pltpu.VMEM((3, 48, 256), F32),
            pltpu.VMEM((144, 256 * PIECES), BF16),
            pltpu.VMEM(slots, I32),
            pltpu.VMEM((64 * PIECES, LANES), F32),
            messages, messages, messages, messages,
            pltpu.SemaphoreType.DMA((2,)),
            pltpu.SemaphoreType.DMA((CHUNKS,)),
            pltpu.SemaphoreType.DMA((CHUNKS,)),
        ],
        [hbm] * 9 + [smem] + [hbm] * 6,
        [vmem] * 4,
        collective_id=0, has_side_effects=True,
    )(
        flat(entry_owner), flat(entry_cell), flat(entry_column), flat(entry_area), flat(area_table),
        far(profiles), far(heat_coupling), far(momentum_coupling), far(layer_mass),
        stay(layer_counts), far(soil_temps), far(heat_capacity), far(conductance),
        stay(exchange_coeffs), flat(wetness), flat(surface_type),
    )
    new_profiles, new_soil = call(
        up_kernel,
        [shape((4, 1024, LANES), F32), shape((768, LANES), F32)],
        [
            pltpu.VMEM((4, 1024, LANES), F32),
            pltpu.SemaphoreType.DMA,
            pltpu.SemaphoreType.DMA((8,)),
        ],
        [vmem] * 4,
        [hbm] * 2,
    )(lowest, factor, reduced, soil)
    return untile(new_profiles, 64, 2048), untile(new_soil, 8, 12288)


def solution(mesh):
    split = ("grp", "tile")
    return jax.shard_map(
        local,
        mesh=mesh,
        in_specs=(
            P(None, None, split), P(None, split), P(None, split), P(None, split), P(None, split),
            P(None, split), P(None, split), P(None, split), P(split), P(), P(split), P(split),
            P(split), P(split), P(split), P(),
        ),
        out_specs=(P(None, None, split), P(None, split)),
        check_vma=False,
    )
```

```python
import jax
import jax.numpy as jnp
from jax import lax
from jax.experimental import pallas as pl
from jax.experimental.pallas import tpu as pltpu
from jax.sharding import PartitionSpec as P

PEERS = 128
LANES = 128
SLOT_ROWS = 192
MSG_ROWS = 8
SEND_ROWS = 6
REPLY_ROWS = 5
CHUNKS = 4
CHUNK_PEERS = PEERS // CHUNKS
LAG = 4
PIECES = 2
BF16 = jnp.bfloat16
F32 = jnp.float32
I32 = jnp.int32
VMEM_LIMIT = 28 * 1024 * 1024


def iota(shape, dim):
    return lax.broadcasted_iota(I32, shape, dim)


def split(x):
    pieces = []
    for _ in range(PIECES):
        pieces.append(x.astype(BF16).astype(F32))
        x = x - pieces[-1]
    return pieces


def lane_gather(table, index):
    return jnp.take_along_axis(table, index, axis=1, mode="promise_in_bounds")


def dot_nt(a, b):
    return lax.dot_general(a, b, (((1,), (1,)), ((), ())), preferred_element_type=F32)


def low_half(shape):
    return iota(shape, 1) < 64


def aligned(x, step):
    return pl.multiple_of(x * step, step)


def pack_group(j, fields, base, message_ref):
    count = len(fields)
    near_rows = lambda f: pl.ds(aligned(j, 64) + f, 8, stride=8)
    far_rows = lambda f: pl.ds(aligned(j, 64) + 512 + f, 8, stride=8)
    part = lambda f, k: fields[f][pl.ds(base + 8 * k, 8), :]
    for f in range(count):
        message_ref[near_rows(f), :] = part(f, 0)
        message_ref[far_rows(f), :] = part(f, 1)
    for pair in range((count + 1) // 2):
        first = part(2 * pair, 2)
        second = part(2 * pair + 1, 2) if 2 * pair + 1 < count else jnp.zeros_like(first)
        low = low_half(first.shape)
        message_ref[near_rows(count + pair), :] = jnp.where(low, first, pltpu.roll(second, 64, 1))
        message_ref[far_rows(count + pair), :] = jnp.where(low, pltpu.roll(first, 64, 1), second)


def unpack_group(j, message_ref, count):
    near_rows = lambda f: pl.ds(aligned(j, 64) + f, 8, stride=8)
    far_rows = lambda f: pl.ds(aligned(j, 64) + 512 + f, 8, stride=8)
    fields = [[message_ref[near_rows(f), :], message_ref[far_rows(f), :]] for f in range(count)]
    for pair in range((count + 1) // 2):
        near = message_ref[near_rows(count + pair), :]
        far = message_ref[far_rows(count + pair), :]
        low = low_half(near.shape)
        fields[2 * pair].append(jnp.where(low, near, pltpu.roll(far, 64, 1)))
        if 2 * pair + 1 < count:
            fields[2 * pair + 1].append(jnp.where(low, pltpu.roll(near, 64, 1), far))
    return fields


def onehot_rows(ids, count):
    return (iota((count, LANES), 0) == ids).astype(F32).astype(BF16)


def rank_entries(owner_ref, rank_scr):
    upper = (iota((LANES, 2 * LANES), 0) < iota((LANES, 2 * LANES), 1)).astype(F32).astype(BF16)
    owners = iota((PEERS, LANES), 0)
    block = 32

    def body(step, base):
        hits = [owners == owner_ref[pl.ds(step * block + q, 1), :] for q in range(block)]
        onehots = jnp.concatenate([hit.astype(F32).astype(BF16) for hit in hits], axis=0)
        before = jnp.dot(onehots, upper, preferred_element_type=F32)
        for q, hit in enumerate(hits):
            here = before[PEERS * q : PEERS * q + PEERS]
            rank_scr[pl.ds(step * block + q, 1), :] = jnp.sum(
                jnp.where(hit, here[:, :LANES] + base, 0.0), axis=0, keepdims=True
            )
            base = base + here[:, LANES:]
        return base

    lax.fori_loop(0, owner_ref.shape[0] // block, body, jnp.zeros((PEERS, LANES), F32))


def assign_slots(owner_ref, rank_scr, piece_scr, acc_scr):
    acc_scr[...] = jnp.zeros_like(acc_scr)
    ranks = iota((2 * LANES, LANES), 0).astype(F32)
    block = 48

    def body(step, carry):
        lefts, rights = [], []
        for q in range(block):
            r = step * block + q
            onehot = onehot_rows(owner_ref[pl.ds(r, 1), :], PEERS)
            lefts.append(jnp.concatenate([
                onehot * jnp.broadcast_to(piece_scr[p, pl.ds(r, 1), :], (PEERS, LANES)).astype(BF16)
                for p in range(3)
            ], axis=0))
            rights.append((ranks == rank_scr[pl.ds(r, 1), :]).astype(F32).astype(BF16))
        acc_scr[...] += dot_nt(jnp.concatenate(lefts, axis=1), jnp.concatenate(rights, axis=1))
        return carry

    lax.fori_loop(0, owner_ref.shape[0] // block, body, 0)


def down_sweep(profiles_ref, heat_ref, momentum_ref, mass_ref, factor_ref, reduced_ref, bottom_scr):
    couplings = (heat_ref, momentum_ref)
    zero = jnp.zeros((8, LANES), F32)

    def rows_of(g, i, half):
        return pl.ds(g * 128 + half * 64 + i, 8, stride=8)

    def body(g, carry):
        link, factor, reduced, inverse = carry
        link, factor, reduced, inverse = list(link), list(factor), list(reduced), list(inverse)
        following = jnp.minimum(g + 1, 7)
        keep = (g < 7).astype(F32)
        for i in range(8):
            for half in range(2):
                mass = mass_ref[rows_of(g, i, half), :]
                out_rows = pl.ds(pl.multiple_of(g * 128 + i * 16 + half * 8, 8), 8)
                for pair in range(2):
                    k = 2 * pair + half
                    if i < 7:
                        below = couplings[pair][rows_of(g, i + 1, half), :]
                    else:
                        below = couplings[pair][rows_of(following, 0, half), :] * keep
                    here = link[k]
                    divisor = mass + here + below + here * factor[k]
                    inverse[k] = 1.0 / divisor
                    factor[k] = -below * inverse[k]
                    factor_ref[pair, out_rows, :] = factor[k]
                    for member in range(2):
                        field = 2 * pair + member
                        m = 2 * field + half
                        value = profiles_ref[field, rows_of(g, i, half), :]
                        reduced[m] = (mass * value + here * reduced[m]) * inverse[k]
                        reduced_ref[field, out_rows, :] = reduced[m]
                    link[k] = below
        return tuple(link), tuple(factor), tuple(reduced), tuple(inverse)

    first = tuple(couplings[k // 2][rows_of(0, 0, k % 2), :] for k in range(4))
    _, _, reduced, inverse = lax.fori_loop(
        0, 8, body, (first, (zero,) * 4, (zero,) * 8, (zero,) * 4)
    )
    for half in range(2):
        rows = slice(8 * half, 8 * half + 8)
        for field in range(4):
            bottom_scr[field, rows, :] = reduced[2 * field + half]
        bottom_scr[4, rows, :] = inverse[half]
        bottom_scr[5, rows, :] = inverse[2 + half]


def encode(number, bits):
    value = ((number & 127) + 128).astype(F32) * (2.0**-64 if bits == 7 else 1.0)
    for b in range(bits):
        value = value * jnp.where(((number >> (7 + b)) & 1) == 1, 2.0 ** (2**b), 1.0)
    return value


def decode(value, bits):
    filled = value > 0.0
    row = jnp.zeros(value.shape, I32)
    if bits == 7:
        large = value >= 128.0
        row = jnp.where(large, 64, 0)
        value = jnp.where(large, value, value * 2.0**64)
        bits = 6
    for b in range(bits - 1, -1, -1):
        large = value >= 128.0 * 2.0 ** (2**b)
        row = jnp.where(large, row + 2**b, row)
        value = jnp.where(large, value * 2.0 ** -(2**b), value)
    return row, jnp.where(filled, value - 128.0, 0.0).astype(I32), filled


def prepare_pieces(cell_ref, column_ref, area_ref, piece_scr):
    piece_scr[0] = encode(cell_ref[...], 7)
    piece_scr[1] = encode(column_ref[...], 4)
    piece_scr[2] = area_ref[...].astype(F32)


def prepare_group(
    j, acc_scr, table_ref, bottom_ref, field_scr, column_slot_ref, weight_slot_ref, send_scr
):
    near_table = jnp.broadcast_to(table_ref[0:1, :], (8, LANES))
    far_table = jnp.broadcast_to(table_ref[1:2, :], (8, LANES))
    base = aligned(j, 24)

    def pieces(p):
        near = pl.ds(PEERS * p + aligned(j, 8), 8)
        far = pl.ds(PEERS * p + 64 + aligned(j, 8), 8)
        last_near, last_far = acc_scr[near, LANES : 2 * LANES], acc_scr[far, LANES : 2 * LANES]
        last = jnp.where(low_half(last_near.shape), last_near, pltpu.roll(last_far, 64, 1))
        return acc_scr[near, 0:LANES], acc_scr[far, 0:LANES], last

    highs, lows = [], []
    for k, (cell, column, area) in enumerate(zip(*[pieces(p) for p in range(3)])):
        rows = pl.ds(base + 8 * k, 8)
        row, lane, filled = decode(cell, 7)
        field_scr[0, rows, :] = jnp.where(filled, row * LANES + lane + 256, 0).astype(F32)
        area = area.astype(I32)
        weight = jnp.where(
            area < LANES, lane_gather(near_table, area & 127), lane_gather(far_table, area & 127)
        )
        weight_slot_ref[rows, :] = jnp.where(filled, weight, 0.0)
        row, lane, _ = decode(column, 4)
        column_slot_ref[rows, :] = row * LANES + lane
        highs.append(row)
        lows.append(lane)
    totals = expand(bottom_ref, (0, 1, 4), highs, lows)
    for k in range(3):
        for f in range(3):
            field_scr[f + 1, pl.ds(base + 8 * k, 8), :] = totals[k][f]
    pack_group(j, [field_scr.at[f] for f in range(4)], base, send_scr)


def expand(bottom_ref, fields, highs, lows):
    totals = [[jnp.zeros((8, LANES), F32) for _ in fields] for _ in highs]
    for h in range(16):
        tables = [jnp.broadcast_to(bottom_ref[f, h : h + 1, :], (8, LANES)) for f in fields]
        for k in range(len(highs)):
            hit = highs[k] == h
            for f, table in enumerate(tables):
                totals[k][f] = jnp.where(hit, lane_gather(table, lows[k]), totals[k][f])
    return totals


def expand_wind(bottom_ref, column_slot_ref, wind_slot_ref):
    def body(step, carry):
        blocks = [pl.ds(aligned(step, 48) + 8 * k, 8) for k in range(6)]
        columns = [column_slot_ref[rows, :] for rows in blocks]
        totals = expand(bottom_ref, (5,), [x >> 7 for x in columns], [x & 127 for x in columns])
        for rows, (value,) in zip(blocks, totals):
            wind_slot_ref[rows, :] = value
        return carry

    lax.fori_loop(0, 4, body, 0)


def soil_block(a, b, soil_ref, capacity_ref, conductance_ref, exchange_ref, wetness_ref, type_ref, counts_ref,
               cells_scr, soil_out_ref, table_scr):
    tiles = pl.ds(16 * a + b, 8, stride=2)
    here = (pl.ds(pl.multiple_of(8 * a, 8), 8), slice(LANES * b, LANES * b + LANES))
    bottom_t = cells_scr[0][here]
    bottom_q = cells_scr[1][here]
    heat_scale = cells_scr[2][here]
    kind = type_ref[tiles, :]
    total = jnp.zeros((8, LANES), I32)
    for t in range(4):
        total = jnp.where(kind == t, counts_ref[t], total)
    heat, moist, drag = (exchange_ref[i, tiles, :] for i in range(3))
    gain_t = heat / (1.0 + heat * heat_scale)
    gain_q = moist / (1.0 + moist * heat_scale)
    link_prev = factor = reduced = None
    factors, reduceds = [], []
    for layer in range(8):
        rows = pl.ds((16 * a + b) * 8 + layer, 8, stride=16)
        conductance = conductance_ref[rows, :]
        capacity = capacity_ref[rows, :]
        link = jnp.where(total > layer + 1, conductance, 0.0)
        deep = jnp.where(total == layer + 1, conductance, 0.0)
        diagonal = capacity + link + deep
        rhs = capacity * soil_ref[rows, :]
        if layer == 0:
            divisor = diagonal + gain_t
            rhs = rhs + gain_t * bottom_t
        else:
            divisor = diagonal + link_prev + link_prev * factor
            rhs = rhs + link_prev * reduced
        inverse = 1.0 / divisor
        factor = -link * inverse
        reduced = rhs * inverse
        factors.append(factor)
        reduceds.append(reduced)
        link_prev = link
    value = None
    for layer in range(7, -1, -1):
        rows = pl.ds((16 * a + b) * 8 + layer, 8, stride=16)
        value = reduceds[layer] if layer == 7 else reduceds[layer] - factors[layer] * value
        kept = value if layer == 0 else jnp.where(total > layer, value, soil_ref[rows, :])
        soil_out_ref[rows, :] = kept
    fluxes = (
        gain_t * (value - bottom_t),
        gain_q * (wetness_ref[tiles, :] + 0.5 * value - bottom_q),
        drag,
    )
    for f, flux in enumerate(fluxes):
        table_scr[f, here[0], here[1]] = flux


def clear_cells(acc_scr):
    acc_scr[...] = jnp.zeros_like(acc_scr)


def scatter_group(groups, recv_scr, index_scr, piece_scr, acc_scr):
    lefts, rights = [], []
    for j in groups:
        base = aligned(j, 24)
        ids, *values = unpack_group(j, recv_scr, 4)
        for k in range(3):
            rows = pl.ds(base + 8 * k, 8)
            index_scr[rows, :] = ids[k].astype(I32) - 256
            for f in range(3):
                for p, piece in enumerate(split(values[f][k])):
                    piece_scr[PIECES * f + p, rows, :] = piece
        for q in range(24):
            row = pl.ds(base + q, 1)
            cell = index_scr[row, :]
            onehot = onehot_rows(cell >> 8, 48)
            lefts.append(jnp.concatenate([
                onehot * jnp.broadcast_to(piece_scr[p, row, :], (48, LANES)).astype(BF16)
                for p in range(3 * PIECES)
            ], axis=0))
            rights.append(onehot_rows(cell & 255, 256))
    acc_scr[...] += dot_nt(jnp.concatenate(lefts, axis=1), jnp.concatenate(rights, axis=1))


def cells_of_slots(acc_scr, cells_scr):
    for f in range(3):
        base = 48 * PIECES * f
        cells_scr[f] = sum(acc_scr[base + 48 * p : base + 48 * p + 48] for p in range(PIECES))


def solve_soil(*refs):
    def soil_body(a, carry):
        for b in range(2):
            soil_block(a, b, *refs)
        return carry

    lax.fori_loop(0, 6, soil_body, 0)


def cut_table(table_scr, pieces_scr):
    for f in range(3):
        for p, piece in enumerate(split(table_scr[f])):
            pieces_scr[48 * f : 48 * f + 48, 256 * p : 256 * p + 256] = piece.astype(BF16)


def gather_group(groups, index_scr, pieces_scr, field_scr, reply_scr):
    width = 8 * LANES
    highs, lows = iota((48, width), 0), iota((256, width), 0)
    for j in groups:
        base = aligned(j, 24)
        for k in range(3):
            cell = jnp.concatenate(
                [index_scr[pl.ds(base + 8 * k + q, 1), :] for q in range(8)], axis=1
            )
            onehot = (lows == (cell & 255)).astype(F32).astype(BF16)
            found = sum(
                jnp.dot(pieces_scr[:, 256 * p : 256 * p + 256], onehot, preferred_element_type=F32)
                for p in range(PIECES)
            )
            hit = highs == (cell >> 8)
            for f in range(3):
                value = jnp.sum(
                    jnp.where(hit, found[48 * f : 48 * f + 48], 0.0), axis=0, keepdims=True
                )
                for q in range(8):
                    field_scr[f, pl.ds(base + 8 * k + q, 1), :] = value[:, LANES * q : LANES * q + LANES]
        pack_group(j, [field_scr.at[f] for f in range(3)], base, reply_scr)


def sum_group(groups, return_scr, column_slot_ref, weight_slot_ref, wind_slot_ref, piece_scr, acc_scr):
    lefts, rights = [], []
    for j in groups:
        base = aligned(j, 24)
        heat, moist, drags = unpack_group(j, return_scr, 3)
        for k in range(3):
            rows = pl.ds(base + 8 * k, 8)
            weight = weight_slot_ref[rows, :]
            drag = drags[k]
            values = (
                weight * heat[k],
                weight * moist[k],
                weight * (drag / (1.0 + drag * wind_slot_ref[rows, :])),
                weight,
            )
            for f in range(4):
                for p, piece in enumerate(split(values[f])):
                    piece_scr[PIECES * f + p, rows, :] = piece
        for q in range(24):
            row = pl.ds(base + q, 1)
            column = column_slot_ref[row, :]
            onehot = onehot_rows(column >> 7, 16)
            lefts.append(jnp.concatenate([
                onehot * jnp.broadcast_to(piece_scr[p, row, :], (16, LANES)).astype(BF16)
                for p in range(4 * PIECES)
            ], axis=0))
            rights.append(onehot_rows(column & 127, LANES))
    acc_scr[...] += dot_nt(jnp.concatenate(lefts, axis=1), jnp.concatenate(rights, axis=1))


def column_sums(acc_scr):
    sums = []
    for f in range(4):
        base = 16 * PIECES * f
        sums.append(sum(acc_scr[base + 16 * p : base + 16 * p + 16] for p in range(PIECES)))
    return sums


def lowest_values(sums, bottom_ref, lowest_ref):
    flux = (
        sums[0] / sums[3],
        sums[1] / sums[3],
        -bottom_ref[2] * (sums[2] / sums[3]),
        -bottom_ref[3] * (sums[2] / sums[3]),
    )
    for field in range(4):
        lowest_ref[field] = bottom_ref[field] + bottom_ref[4 + field // 2] * flux[field]


def up_kernel(lowest_ref, factor_ref, reduced_ref, soil_ref, out_ref, soil_out_ref, out_scr, soil_sem, out_sems):
    soil = pltpu.make_async_copy(soil_ref, soil_out_ref, soil_sem)
    soil.start()
    stores = [
        pltpu.make_async_copy(
            out_scr.at[:, pl.ds(128 * g, 128)], out_ref.at[:, pl.ds(128 * g, 128)], out_sems.at[g]
        )
        for g in range(8)
    ]
    values = [lowest_ref[field, 8 * half : 8 * half + 8] for field in range(4) for half in range(2)]
    for g in range(7, -1, -1):
        for i in range(7, -1, -1):
            for half in range(2):
                rows = pl.ds(g * 128 + i * 16 + half * 8, 8)
                for field in range(4):
                    k = 2 * field + half
                    if g < 7 or i < 7:
                        factor = factor_ref[field // 2, rows, :]
                        values[k] = reduced_ref[field, rows, :] - factor * values[k]
                    out_scr[field, pl.ds(g * 128 + half * 64 + i, 8, stride=8), :] = values[k]
        stores[g].start()
    for store in stores:
        store.wait()
    soil.wait()


def device_of(peer):
    return (peer // 32, lax.rem(peer, 32))


def mates():
    group, tile = lax.axis_index("grp"), lax.axis_index("tile")
    row = [(group, lax.rem(tile + k, 32)) for k in range(1, 32)]
    column = [(lax.rem(group + k, 4), tile) for k in range(1, 4)]
    return row, column


def signal(semaphore, devices):
    for device in devices:
        pl.semaphore_signal(
            semaphore, inc=1, device_id=device, device_id_type=pl.DeviceIdType.MESH
        )


def send_chunk(me, chunk, own, send_ref, recv_ref, rows, send_sem, recv_sem):
    near = CHUNK_PEERS // 2
    mine = lax.rem(me, near) + near * (me // 64)
    here = pl.ds(aligned(me, MSG_ROWS), rows)
    for k in range(1 if own else 0, CHUNK_PEERS):
        place = lax.rem(mine + k, CHUNK_PEERS)
        peer = near * chunk + place % near + 64 * (place // near)
        pltpu.make_async_remote_copy(
            src_ref=send_ref.at[pl.ds(aligned(peer, MSG_ROWS), rows)], dst_ref=recv_ref.at[here],
            send_sem=send_sem, recv_sem=recv_sem, device_id=device_of(peer),
            device_id_type=pl.DeviceIdType.MESH,
        ).start()
    if own:
        pltpu.make_async_copy(send_ref.at[here], recv_ref.at[here], recv_sem).start()


def messages_of(me, count, send_ref, recv_ref, rows, send_sem, recv_sem):
    whole = pl.ds(0, count * rows)
    return pltpu.make_async_remote_copy(
        src_ref=send_ref.at[whole], dst_ref=recv_ref.at[whole], send_sem=send_sem, recv_sem=recv_sem,
        device_id=device_of(me), device_id_type=pl.DeviceIdType.MESH,
    )


def step_kernel(
    owner_any, cell_any, column_any, area_any, table_any, profiles_any, heat_any, momentum_any, mass_any,
    counts_ref, soil_any, capacity_any, conductance_any, exchange_any, wetness_any, type_any,
    lowest_ref, soil_out_ref, factor_scr, reduced_scr,
    owner_ref, cell_ref, column_ref, area_ref, table_ref, exchange_ref, wetness_ref, type_ref,
    profiles_ref, heat_ref, momentum_ref, mass_ref, soil_ref, capacity_ref, conductance_ref, load_sems,
    exchange_scr,
    column_slot_scr, weight_slot_scr, wind_slot_scr, bottom_scr,
    piece_scr, rank_scr, slot_acc_scr, field_scr, slot_piece_scr, cell_acc_scr, cells_scr, table_scr,
    table_piece_scr, index_scr, column_acc_scr, send_scr, recv_scr, reply_scr, return_scr,
    sent_sem, there_sems, back_sems, rows_sem,
):
    me = lax.axis_index("grp") * 32 + lax.axis_index("tile")
    mine = lax.rem(me, 64) // (CHUNK_PEERS // 2)
    loads = [
        pltpu.make_async_copy(source, target, load_sems.at[k])
        for k, (source, target) in enumerate((
            (owner_any, owner_ref), (cell_any, cell_ref), (column_any, column_ref), (area_any, area_ref),
            (table_any, table_ref), (heat_any, heat_ref), (momentum_any, momentum_ref),
            (mass_any, mass_ref), (profiles_any, profiles_ref), (exchange_any, exchange_ref),
            (soil_any, soil_ref), (capacity_any, capacity_ref), (conductance_any, conductance_ref),
            (wetness_any, wetness_ref), (type_any, type_ref),
        ))
    ]
    entry_loads, column_loads, soil_loads = loads[:4], loads[4:10], loads[10:]
    for load in loads:
        load.start()
    barrier = pltpu.get_barrier_semaphore()
    row_mates, column_mates = mates()
    signal(barrier, column_mates + row_mates)
    for load in entry_loads:
        load.wait()
    prepare_pieces(cell_ref, column_ref, area_ref, piece_scr)
    rank_entries(owner_ref, rank_scr)
    assign_slots(owner_ref, rank_scr, piece_scr, slot_acc_scr)
    pl.semaphore_wait(barrier, 34)
    signal(rows_sem, column_mates)
    for load in column_loads:
        load.wait()
    for row in range(3):
        exchange_scr[row] = exchange_ref[row : row + 1, :].reshape(96, LANES)
    down_sweep(profiles_ref, heat_ref, momentum_ref, mass_ref, factor_scr, reduced_scr, bottom_scr)
    cell_acc_scr[...] = jnp.zeros_like(cell_acc_scr)
    column_acc_scr[...] = jnp.zeros_like(column_acc_scr)

    def groups_of(chunk):
        return [chunk * (8 // CHUNKS) + k for k in range(8 // CHUNKS)]

    def ahead(i):
        return lax.rem(mine + i, CHUNKS)

    def behind(i):
        return lax.rem(mine + CHUNKS - i, CHUNKS)

    def prepare(i):
        for j in groups_of(ahead(i)):
            prepare_group(
                j, slot_acc_scr, table_ref, bottom_scr, field_scr, column_slot_scr, weight_slot_scr,
                send_scr,
            )

    def send(i, own):
        send_chunk(me, ahead(i), own, send_scr, recv_scr, SEND_ROWS, sent_sem.at[0], there_sems.at[mine])

    def scatter(i):
        chunk = behind(i)
        messages_of(
            me, CHUNK_PEERS, send_scr, recv_scr, SEND_ROWS, sent_sem.at[0], there_sems.at[chunk]
        ).wait_recv()
        scatter_group(groups_of(chunk), recv_scr, index_scr, slot_piece_scr, cell_acc_scr)

    prepare(0)
    pl.semaphore_wait(rows_sem, 3)
    send(0, True)

    def there(i, carry):
        prepare(i)
        send(i, False)
        return carry

    lax.fori_loop(1, CHUNKS, there, 0)

    def arrive(i, carry):
        scatter(i)
        return carry

    lax.fori_loop(0, CHUNKS, arrive, 0)
    for load in soil_loads:
        load.wait()
    cells_of_slots(cell_acc_scr, cells_scr)
    solve_soil(
        soil_ref, capacity_ref, conductance_ref, exchange_scr, wetness_ref, type_ref, counts_ref,
        [cells_scr.at[f] for f in range(3)], soil_out_ref, table_scr,
    )
    cut_table(table_scr, table_piece_scr)

    def gather(i, own):
        chunk = ahead(i)
        gather_group(groups_of(chunk), index_scr, table_piece_scr, field_scr, reply_scr)
        send_chunk(me, chunk, own, reply_scr, return_scr, REPLY_ROWS, sent_sem.at[1], back_sems.at[mine])

    def collect(i):
        chunk = behind(i)
        messages_of(
            me, CHUNK_PEERS, reply_scr, return_scr, REPLY_ROWS, sent_sem.at[1], back_sems.at[chunk]
        ).wait_recv()
        sum_group(
            groups_of(chunk), return_scr, column_slot_scr, weight_slot_scr, wind_slot_scr,
            slot_piece_scr, column_acc_scr,
        )

    gather(0, True)

    def ask(i, carry):
        gather(i, False)
        return carry

    lax.fori_loop(1, LAG, ask, 0)
    expand_wind(bottom_scr, column_slot_scr, wind_slot_scr)

    def back(i, carry):
        gather(i, False)
        collect(i - LAG)
        return carry

    if LAG < CHUNKS:
        lax.fori_loop(LAG, CHUNKS, back, 0)

    def last(i, carry):
        collect(i)
        return carry

    lax.fori_loop(CHUNKS - LAG, CHUNKS, last, 0)
    lowest_values(column_sums(column_acc_scr), bottom_scr, lowest_ref)
    messages_of(
        me, PEERS - 1, send_scr, recv_scr, SEND_ROWS, sent_sem.at[0], there_sems.at[0]
    ).wait_send()
    messages_of(
        me, PEERS - 1, reply_scr, return_scr, REPLY_ROWS, sent_sem.at[1], back_sems.at[0]
    ).wait_send()


def call(kernel, out_shapes, scratch, in_specs, out_specs, **params):
    return pl.pallas_call(
        kernel,
        out_shape=out_shapes,
        in_specs=in_specs,
        out_specs=out_specs,
        scratch_shapes=scratch,
        compiler_params=pltpu.CompilerParams(vmem_limit_bytes=VMEM_LIMIT, **params),
    )


def tiles_of(x):
    *lead, rows, lanes = x.shape
    x = x.reshape(*lead, rows // 8, 8, lanes // LANES, LANES)
    return jnp.swapaxes(x, -3, -2).reshape(*lead, rows * lanes // LANES, LANES)


def untile(x, rows, lanes):
    *lead, _, _ = x.shape
    x = x.reshape(*lead, rows // 8, lanes // LANES, 8, LANES)
    return jnp.swapaxes(x, -3, -2).reshape(*lead, rows, lanes)


def local(
    profiles, heat_coupling, momentum_coupling, layer_mass, soil_temps, heat_capacity, conductance,
    exchange_coeffs, wetness, area_table, entry_column, entry_owner, entry_cell, entry_area,
    surface_type, layer_counts,
):
    shape = jax.ShapeDtypeStruct
    vmem = pl.BlockSpec(memory_space=pltpu.VMEM)
    smem = pl.BlockSpec(memory_space=pltpu.SMEM)
    flat = lambda x: stay(x.reshape(-1, LANES))
    slots = (SLOT_ROWS, LANES)
    messages = pltpu.VMEM((PEERS * MSG_ROWS, LANES), F32)
    hbm = pl.BlockSpec(memory_space=pltpu.HBM)
    entries = pltpu.VMEM((96, LANES), I32)
    stay = lambda x: pltpu.with_memory_space_constraint(x, pltpu.HBM)
    far = lambda x: stay(tiles_of(x))
    columns, cells = pltpu.VMEM((1024, LANES), F32), pltpu.VMEM((768, LANES), F32)
    lowest, soil, factor, reduced = call(
        step_kernel,
        [
            shape((4, 16, LANES), F32), shape((768, LANES), F32),
            shape((2, 1024, LANES), F32), shape((4, 1024, LANES), F32),
        ],
        [
            entries, entries, entries, entries,
            pltpu.VMEM((2, LANES), F32),
            pltpu.VMEM((3, 96 * LANES), F32),
            pltpu.VMEM((96, LANES), F32),
            entries,
            pltpu.VMEM((4, 1024, LANES), F32),
            columns, columns, columns, cells, cells, cells,
            pltpu.SemaphoreType.DMA((15,)),
            pltpu.VMEM((3, 96, LANES), F32),
            pltpu.VMEM(slots, I32),
            pltpu.VMEM(slots, F32),
            pltpu.VMEM(slots, F32),
            pltpu.VMEM((6, 16, LANES), F32),
            pltpu.VMEM((3, 96, LANES), F32),
            pltpu.VMEM((96, LANES), F32),
            pltpu.VMEM((3 * PEERS, 256), F32),
            pltpu.VMEM((4,) + slots, F32),
            pltpu.VMEM((4 * PIECES,) + slots, F32),
            pltpu.VMEM((144 * PIECES, 256), F32),
            pltpu.VMEM((3, 48, 256), F32),
            pltpu.VMEM((3, 48, 256), F32),
            pltpu.VMEM((144, 256 * PIECES), BF16),
            pltpu.VMEM(slots, I32),
            pltpu.VMEM((64 * PIECES, LANES), F32),
            messages, messages, messages, messages,
            pltpu.SemaphoreType.DMA((2,)),
            pltpu.SemaphoreType.DMA((CHUNKS,)),
            pltpu.SemaphoreType.DMA((CHUNKS,)),
            pltpu.SemaphoreType.REGULAR,
        ],
        [hbm] * 9 + [smem] + [hbm] * 6,
        [vmem] * 4,
        collective_id=0, has_side_effects=True,
    )(
        flat(entry_owner), flat(entry_cell), flat(entry_column), flat(entry_area), flat(area_table),
        far(profiles), far(heat_coupling), far(momentum_coupling), far(layer_mass),
        stay(layer_counts), far(soil_temps), far(heat_capacity), far(conductance),
        stay(exchange_coeffs), flat(wetness), flat(surface_type),
    )
    new_profiles, new_soil = call(
        up_kernel,
        [shape((4, 1024, LANES), F32), shape((768, LANES), F32)],
        [
            pltpu.VMEM((4, 1024, LANES), F32),
            pltpu.SemaphoreType.DMA,
            pltpu.SemaphoreType.DMA((8,)),
        ],
        [vmem] * 4,
        [hbm] * 2,
    )(lowest, factor, reduced, soil)
    return untile(new_profiles, 64, 2048), untile(new_soil, 8, 12288)


def solution(mesh):
    split = ("grp", "tile")
    return jax.shard_map(
        local,
        mesh=mesh,
        in_specs=(
            P(None, None, split), P(None, split), P(None, split), P(None, split), P(None, split),
            P(None, split), P(None, split), P(None, split), P(split), P(), P(split), P(split),
            P(split), P(split), P(split), P(),
        ),
        out_specs=(P(None, None, split), P(None, split)),
        check_vma=False,
    )
```
